128 devices in a mesh: wall: 4 (over z), span: 32 (over x, y, core).
Axes of the slice: x: 4, y: 4, z: 4, core: 2. Of those that a mesh axis runs over, the one named last changes fastest.
Arguments:
- velocity: float32 [3, 4, 1024, 4096], P(None, None, 'wall', 'span'), may hold values from -6 to 6
- lower_weight: float32 [4, 1024, 4096], P(None, 'wall', 'span'), may hold values from 1000 to 100000
- upper_weight: float32 [4, 1024, 4096], P(None, 'wall', 'span'), may hold values from 1000 to 100000
- forces: float32 [3, 4, 32, 32, 4, 768], P(None, 'wall', 'span'), may hold values from -6 to 6
- cells: int32 [4, 32, 32, 4, 768], P('wall', 'span'), may hold values from 0 to 32767
- counts: int32 [4, 32, 32, 4], P('wall', 'span'), may hold values from 1 to 768, as said below
Outputs:
- velocity_next: float32 [3, 4, 1024, 4096], P(None, None, 'wall', 'span')
- deposit: bfloat16 [3, 4, 1024, 4096], P(None, None, 'wall', 'span')
The draws below stay inside these ranges and needn't reach their ends.
Inputs may be any that keep to these rules, and one draw needn't show every extreme that they name: `counts`: in every wall row one destination receives 768 live slots from every sender in one plane.
All inputs are finite; a program needn't handle non-finite values.
Results may differ from the reference program's by a relative error of at most 0.0024.
Values sent between devices are 32-bit elements; how exact they have to be, the bound alone decides.
A program may use at most 64 MiB of HBM per device.

```python
import math
import jax
import jax.numpy as jnp
from jax import lax

NY = 1024
CZ = 128
X = 4
CAPX = 768
CY = 256
NZ = 4096
N_WALL = 4
N_SPAN = 32


def draw_counts(key, part):
    key_dense, key_count, key_dest, key_plane = jax.random.split(key, 4)
    shape = (N_WALL, N_SPAN, N_SPAN, X)
    dense = jax.random.randint(key_dense, (N_WALL, N_SPAN, 1, 1), 0, 4) == 0
    ceiling = jnp.where(dense, CAPX + 1, CAPX // 3 + 1)
    drawn = jax.random.randint(key_count, shape, 1, jnp.broadcast_to(ceiling, shape))
    chosen_dest = jax.random.randint(key_dest, (N_WALL, 1, 1, 1), 0, N_SPAN)
    chosen_plane = jax.random.randint(key_plane, (N_WALL, 1, 1, 1), 0, X)
    dest_index = lax.broadcasted_iota(jnp.int32, shape, 1)
    plane_index = lax.broadcasted_iota(jnp.int32, shape, 3)
    filled = (dest_index == chosen_dest) & (plane_index == chosen_plane)
    return jnp.where(filled, CAPX, drawn).astype(jnp.int32)


def set_ends(result, own_key, low, largest):
    longest = result.shape.index(max(result.shape))
    spots = []
    for shift in (0, 1):
        where = [jax.random.randint(jax.random.fold_in(own_key, axis), (), 0, length) for axis, length in enumerate(result.shape)]
        where[longest] = (where[longest] + shift) % result.shape[longest]
        spots.append(tuple(where))
    return result.at[spots[0]].set(low).at[spots[1]].set(largest)


def levels(rng, dims, cuts, low, high):
    def one(dim, shards_of):
        steps = jax.random.uniform(jax.random.fold_in(jax.random.fold_in(rng, 6), dim), (shards_of,), jnp.float32, low / len(cuts), high / len(cuts))
        return jnp.repeat(jnp.exp(steps), dims[dim] // shards_of).reshape((-1,) + (1,) * (len(dims) - dim - 1))

    factor_of = one(*cuts[0])
    for cut in cuts[1:]:
        factor_of = factor_of * one(*cut)
    return factor_of


def gaussian(stream_key, shape, width, most, shards=(), kind=jnp.bfloat16):
    array = width * jax.random.normal(stream_key, shape, jnp.float32)
    if shards:
        array = array * levels(stream_key, shape, shards, -0.22, 0.18)
    return jnp.clip(array, -most, most).astype(kind)


def setup_inputs(seed: int = 0) -> dict:
    keys = jax.random.split(jax.random.key(seed), 7)
    velocity = gaussian(keys[0], (3, X, NY, NZ), 1.0, 6.0, ((2, 4), (3, 32)), jnp.float32)
    lower_weight = jnp.clip(jnp.exp(math.log(100000.0) - 4.6051702 * jax.random.uniform(keys[1], (X, NY, NZ), jnp.float32) ** levels(keys[1], (X, NY, NZ), ((1, 4), (2, 32)), -0.2, 0.2)), 1000.0, 100000.0)
    upper_weight = jnp.clip(jnp.exp(math.log(100000.0) - 4.6051702 * jax.random.uniform(keys[2], (X, NY, NZ), jnp.float32) ** levels(keys[2], (X, NY, NZ), ((1, 4), (2, 32)), -0.2, 0.2)), 1000.0, 100000.0)
    forces = gaussian(keys[3], (3, N_WALL, N_SPAN, N_SPAN, X, CAPX), 1.0, 6.0, ((1, 4), (2, 32)), jnp.float32)
    cells = set_ends(jax.random.randint(keys[4], (N_WALL, N_SPAN, N_SPAN, X, CAPX), 0, CY * CZ), jax.random.fold_in(keys[4], 1), 0, (CY * CZ) - 1).astype(jnp.int32)
    counts = draw_counts(jax.random.fold_in(keys[6], 71), 0)
    return {"velocity": velocity, "lower_weight": lower_weight, "upper_weight": upper_weight, "forces": forces, "cells": cells, "counts": counts}


diffusion_number = 0.2


def deposit_forces(forces, cells, counts):
    moved = jnp.transpose(forces, (0, 1, 3, 2, 4, 5))
    slot = jnp.arange(CAPX, dtype=jnp.int32)
    live = slot[None, None, None, None, :] < counts[..., None]
    plane = jnp.arange(X, dtype=jnp.int32)[None, None, None, :, None]
    wall_row = jnp.arange(N_WALL, dtype=jnp.int32)[:, None, None, None, None]
    span_col = jnp.arange(N_SPAN, dtype=jnp.int32)[None, :, None, None, None]
    height = wall_row * CY + cells // CZ
    across = span_col * CZ + cells % CZ
    target = (plane * NY + height) * NZ + across
    target = jnp.broadcast_to(target, live.shape).reshape(-1).astype(jnp.int32)
    total = X * NY * NZ

    def one_component(component):
        masked = jnp.where(live, component, jnp.zeros_like(component))
        return jax.ops.segment_sum(masked.reshape(-1), target, num_segments=total)

    return jnp.stack([one_component(moved[index]) for index in range(3)]).reshape(3, X, NY, NZ)


def solve_columns(lower_weight, upper_weight, rhs):
    heights = jnp.arange(NY, dtype=jnp.int32)[None, :, None]
    sub = jnp.where(heights == 0, jnp.zeros_like(lower_weight), -lower_weight)
    sup = jnp.where(heights == NY - 1, jnp.zeros_like(upper_weight), -upper_weight)
    diag = 1.0 + lower_weight + upper_weight
    sub_rows = jnp.moveaxis(sub, 1, 0)
    diag_rows = jnp.moveaxis(diag, 1, 0)
    sup_rows = jnp.moveaxis(sup, 1, 0)
    rhs_rows = jnp.moveaxis(rhs, 2, 0)

    def forward(carry, row):
        ratio_prev, value_prev = carry
        sub_row, diag_row, sup_row, rhs_row = row
        pivot = diag_row - sub_row * ratio_prev
        ratio = sup_row / pivot
        value = (rhs_row - sub_row[None] * value_prev) / pivot[None]
        return (ratio, value), (ratio, value)

    start = (jnp.zeros((X, NZ), jnp.float32), jnp.zeros((3, X, NZ), jnp.float32))
    _, (ratios, values) = lax.scan(forward, start, (sub_rows, diag_rows, sup_rows, rhs_rows))

    def backward(after, row):
        ratio, value = row
        current = value - ratio[None] * after
        return current, current

    _, solved = lax.scan(backward, jnp.zeros((3, X, NZ), jnp.float32), (ratios, values), reverse=True)
    return jnp.moveaxis(solved, 0, 2)


def reference(velocity, lower_weight, upper_weight, forces, cells, counts):
    force_field = deposit_forces(forces, cells, counts)
    stream = jnp.roll(velocity, 1, axis=1) + jnp.roll(velocity, -1, axis=1)
    spanwise = jnp.roll(velocity, -1, axis=3) + jnp.roll(velocity, 1, axis=3)
    rhs = velocity + diffusion_number * (stream - 2.0 * velocity) + diffusion_number * (spanwise - 2.0 * velocity) + force_field
    velocity_next = solve_columns(lower_weight, upper_weight, rhs)
    return velocity_next, force_field.astype(jnp.bfloat16)
```

```python
import functools

import jax
import jax.numpy as jnp
from jax import lax
from jax.experimental import pallas as pl
from jax.experimental.pallas import tpu as pltpu
from jax.sharding import PartitionSpec as P

MESH = pl.DeviceIdType.MESH
diffusion_number = 0.2
SPAN = 32
WALL = 4
PLANES = 4
COMPS = 3
ROWS = 256
LANES = 128
SLOTS = 768
CHUNKS = 8
STEPS = ROWS // CHUNKS
SEND_ORDER = (
    list(range(1, 8)) + list(range(16, 24)) + list(range(8, 16)) + list(range(24, 32))
)


def kernel(
    vel_hbm,
    low_hbm,
    upp_hbm,
    forces_hbm,
    cells_hbm,
    counts,
    next_hbm,
    dep_hbm,
    recv,
    cells,
    vel,
    low,
    upp,
    rhs,
    field,
    dep,
    ybuf,
    w_ref,
    lw_ref,
    c_ref,
    a_ref,
    b_ref,
    g_ref,
    hc_ref,
    pack,
    hsend,
    hrecv,
    cf,
    bd,
    xlu,
    send_sem,
    recv_sem,
    halo_send,
    halo_recv,
    cf_send,
    cf_recv,
    bd_send,
    bd_recv,
    load_sem,
    out_sem,
):
    wall = lax.axis_index("wall")
    me = lax.axis_index("span")
    px, py, pc = me // 8, (me // 2) % 4, me % 2

    def peer(k, sign):
        dx, dy, dc = k // 8, (k // 2) % 4, k % 2
        x = (px + 4 + sign * dx) % 4
        y = (py + 4 + sign * dy) % 4
        c = (pc + dc) % 2
        return x * 8 + y * 2 + c

    loads = [
        pltpu.make_async_copy(vel_hbm, vel, load_sem.at[0]),
        pltpu.make_async_copy(low_hbm, low, load_sem.at[1]),
        pltpu.make_async_copy(upp_hbm, upp, load_sem.at[2]),
        pltpu.make_async_copy(cells_hbm.at[0, 0], cells, load_sem.at[3]),
        pltpu.make_async_copy(forces_hbm.at[:, 0, 0, me], recv.at[:, 0], load_sem.at[4]),
    ]
    for copy in loads:
        copy.start()

    barrier = pltpu.get_barrier_semaphore()
    for k in range(1, SPAN):
        pl.semaphore_signal(barrier, inc=1, device_id={"span": peer(k, 1)}, device_id_type=MESH)
    for j in range(1, WALL):
        pl.semaphore_signal(
            barrier, inc=1, device_id={"wall": (wall + j) % WALL}, device_id_type=MESH
        )
    pl.semaphore_wait(barrier, SPAN - 1 + WALL - 1)

    def block_copy(k, target):
        return pltpu.make_async_remote_copy(
            src_ref=forces_hbm.at[:, 0, 0, target],
            dst_ref=recv.at[:, k],
            send_sem=send_sem.at[k],
            recv_sem=recv_sem.at[k],
            device_id={"span": target},
            device_id_type=MESH,
        )

    sends = [block_copy(k, peer(k, 1)) for k in SEND_ORDER]
    for copy in sends:
        copy.start()

    loads[0].wait()
    lane = lax.broadcasted_iota(jnp.int32, (ROWS, LANES), 1)
    edges = []
    for side, column in ((0, 0), (1, LANES - 1)):
        packed = jnp.zeros((ROWS, LANES), jnp.float32)
        for i in range(COMPS * PLANES):
            block = vel[i // PLANES, i % PLANES]
            packed = jnp.where(lane == i, pltpu.roll(block, (i - column) % LANES, 1), packed)
        hsend[side] = jnp.transpose(packed)[0:16]
        target = (me + SPAN - 1) % SPAN if side == 0 else (me + 1) % SPAN
        copy = pltpu.make_async_remote_copy(
            src_ref=hsend.at[side],
            dst_ref=hrecv.at[side],
            send_sem=halo_send.at[side],
            recv_sem=halo_recv.at[side],
            device_id={"span": target},
            device_id_type=MESH,
        )
        copy.start()
        edges.append(copy)

    field[...] = jnp.zeros_like(field)
    for copy in loads[1:]:
        copy.wait()

    io_m = lax.broadcasted_iota(jnp.int32, (LANES, 256), 0).astype(jnp.bfloat16)
    io_n = lax.broadcasted_iota(jnp.int32, (256, 256), 0).astype(jnp.bfloat16)
    slot = lax.broadcasted_iota(jnp.int32, (1, SLOTS), 1)

    def deposit(k, through):
        @pl.when(k > 0)
        def _():
            block_copy(k, me).wait_recv()

        source = peer(k, -1)
        for p in range(PLANES):
            cell = cells[source, p : p + 1, :]
            live = slot < counts[0, 0, source, p]
            m = jnp.where(live, (cell >> 7) & 127, 255).astype(jnp.float32).astype(jnp.bfloat16)
            n = (((cell >> 14) << 7) + (cell & 127)).astype(jnp.float32).astype(jnp.bfloat16)
            values = [recv[c, k, p : p + 1, :] for c in range(COMPS)]
            high = [v.astype(jnp.bfloat16) for v in values]
            rest = [(v - h.astype(jnp.float32)).astype(jnp.bfloat16) for v, h in zip(values, high)]
            total = None
            for start in range(0, SLOTS, 256):
                part = slice(start, start + 256)
                hot_m = m[:, part] == io_m
                hot_n = jnp.where(n[:, part] == io_n, jnp.bfloat16(1), jnp.bfloat16(0))
                weighted = jnp.concatenate(
                    [jnp.where(hot_m, v[:, part], jnp.bfloat16(0)) for v in high + rest], axis=0
                )
                term = lax.dot_general(
                    weighted, hot_n, (((1,), (1,)), ((), ())), preferred_element_type=jnp.float32
                )
                total = term if total is None else total + term
            total = total.reshape(2, COMPS, LANES, 256)
            total = total[0] + total[1]
            for c in range(COMPS):
                field[c, p, 0:128, :] += total[c, :, 0:128]
                field[c, p, 128:256, :] += total[c, :, 128:256]
        for row in range(ROWS // SPAN):
            index = pl.ds(k * (ROWS // SPAN) + row, PLANES, stride=ROWS)
            lower = low[index, :]
            upper = upp[index, :]
            gain = 1.0 + lower * through
            inverse = 1.0 / (gain + upper)
            w_ref[index, :] = inverse
            lw_ref[index, :] = lower * inverse
            c_ref[index, :] = upper * inverse
            through = gain * inverse
        return through

    lax.fori_loop(0, SPAN, deposit, jnp.ones((PLANES, LANES), jnp.float32))

    sub = lax.broadcasted_iota(jnp.int32, (CHUNKS, LANES), 0)

    def down(x, d):
        return jnp.where(sub >= d, pltpu.roll(x, d, 0), 0.0)

    def up(x, d):
        return jnp.where(sub < CHUNKS - d, pltpu.roll(x, CHUNKS - d, 0), 0.0)

    def levels(x, shift):
        out = [x]
        for d in (1, 2):
            out.append(out[-1] * shift(out[-1], d))
        return out

    def scan(x, factors, shift):
        for d, factor in zip((1, 2, 4), factors):
            x = x + factor * shift(x, d)
        return x

    def chunk(p, r):
        return pl.ds(p * ROWS + r, CHUNKS, stride=STEPS)

    def prefix(r, carry):
        out = []
        for p in range(PLANES):
            value = carry[p] * lw_ref[chunk(p, r), :]
            a_ref[p, r] = value
            out.append(value)
        return tuple(out)

    one = jnp.ones((CHUNKS, LANES), jnp.float32)
    alpha = lax.fori_loop(0, STEPS, prefix, (one,) * PLANES, unroll=4)
    alphas = [levels(x, down) for x in alpha]
    through_low = []
    for p in range(PLANES):
        ends = scan(jnp.where(sub == 0, alpha[p], 0.0), alphas[p], down)
        through_low.append(jnp.where(sub == 0, 1.0, pltpu.roll(ends, 1, 0)))

    def suffix(i, carry):
        r = STEPS - 1 - i
        out = []
        for p in range(PLANES):
            ratio = c_ref[chunk(p, r), :]
            b = carry[p] * ratio
            g = a_ref[p, r] * through_low[p] + ratio * carry[PLANES + p]
            b_ref[p, r] = b
            g_ref[p, r] = g
            out.append((b, g))
        return tuple(x[0] for x in out) + tuple(x[1] for x in out)

    zero = jnp.zeros((CHUNKS, LANES), jnp.float32)
    done = lax.fori_loop(0, STEPS, suffix, (one,) * PLANES + (zero,) * PLANES, unroll=4)
    beta, g_first = done[:PLANES], done[PLANES:]
    betas = [levels(x, up) for x in beta]
    g_carry = []
    for p in range(PLANES):
        g_all = scan(g_first[p], betas[p], up)
        g_carry.append(up(g_all, 1))
        h_all = scan(jnp.where(sub == CHUNKS - 1, beta[p], 0.0), betas[p], up)
        h_carry = jnp.where(sub == CHUNKS - 1, 1.0, pltpu.roll(h_all, CHUNKS - 1, 0))
        hc_ref[p] = h_carry
        cf[wall, 0, p : p + 1, :] = g_all[0:1]
        cf[wall, 1, p : p + 1, :] = h_all[0:1]
        last_g = g_ref[p, STEPS - 1] + b_ref[p, STEPS - 1] * g_carry[p]
        cf[wall, 2, p : p + 1, :] = last_g[CHUNKS - 1 :]
        last_h = b_ref[p, STEPS - 1] * h_carry
        cf[wall, 3, p : p + 1, :] = last_h[CHUNKS - 1 :]

    def to_walls(ref, sems):
        copies = []
        for j in range(1, WALL):
            copy = pltpu.make_async_remote_copy(
                src_ref=ref.at[wall],
                dst_ref=ref.at[wall],
                send_sem=sems[0].at[j],
                recv_sem=sems[1].at[j],
                device_id={"wall": (wall + j) % WALL},
                device_id_type=MESH,
            )
            copy.start()
            copies.append(copy)
        return copies

    def from_walls(ref, sems):
        for j in range(1, WALL):
            pltpu.make_async_remote_copy(
                src_ref=ref.at[wall],
                dst_ref=ref.at[(wall + WALL - j) % WALL],
                send_sem=sems[0].at[j],
                recv_sem=sems[1].at[j],
                device_id={"wall": (wall + j) % WALL},
                device_id_type=MESH,
            ).wait_recv()

    coefficients = to_walls(cf, (cf_send, cf_recv))

    def full_g(r, carry):
        for p in range(PLANES):
            g_ref[p, r] = g_ref[p, r] + b_ref[p, r] * g_carry[p]
        return carry

    lax.fori_loop(0, STEPS, full_g, 0, unroll=4)

    for copy in edges:
        copy.wait_recv()
    for side in range(2):
        pack[...] = jnp.zeros_like(pack)
        pack[0:16] = hrecv[side]
        rhs[0, side] = jnp.transpose(pack[...])
    last = lane == LANES - 1
    first = lane == 0
    above_columns = rhs[0, 0]
    below_columns = rhs[0, 1]
    for c in range(COMPS):
        for p in range(PLANES):
            i = c * PLANES + p
            here = vel[c, p]
            above = jnp.where(
                last, pltpu.roll(above_columns, LANES - 1 - i, 1), pltpu.roll(here, LANES - 1, 1)
            )
            below = jnp.where(
                first, pltpu.roll(below_columns, (LANES - i) % LANES, 1), pltpu.roll(here, 1, 1)
            )
            stream = vel[c, (p + 1) % PLANES] + vel[c, (p + PLANES - 1) % PLANES]
            rhs[c, p] = (
                here
                + diffusion_number * (stream - 2.0 * here)
                + diffusion_number * (above + below - 2.0 * here)
            )

    for c in range(COMPS):
        for p in range(PLANES):
            dep[c, p] = field[c, p].astype(jnp.bfloat16)
    dep_out = pltpu.make_async_copy(dep, dep_hbm, out_sem.at[0])
    dep_out.start()

    pairs = [(c, p) for c in range(COMPS) for p in range(PLANES)]

    def forward(r, carry):
        out = []
        for p in range(PLANES):
            inverse = w_ref[chunk(p, r), :]
            factor = lw_ref[chunk(p, r), :]
            for c in range(COMPS):
                index = pl.ds(r, CHUNKS, stride=STEPS)
                right = rhs[c, p, index, :] + field[c, p, index, :]
                value = right * inverse + factor * carry[p * COMPS + c]
                ybuf[c, p, r] = value
                out.append(value)
        return tuple(out)

    ends = lax.fori_loop(0, STEPS, forward, (zero,) * (PLANES * COMPS), unroll=2)
    carries = []
    for p in range(PLANES):
        for c in range(COMPS):
            carries.append(down(scan(ends[p * COMPS + c], alphas[p], down), 1))

    def backward(i, carry):
        r = STEPS - 1 - i
        out = []
        for p in range(PLANES):
            ratio = c_ref[chunk(p, r), :]
            prefix_product = a_ref[p, r]
            for c in range(COMPS):
                j = p * COMPS + c
                value = ybuf[c, p, r] + prefix_product * carries[j] + ratio * carry[j]
                ybuf[c, p, r] = value
                out.append(value)
        return tuple(out)

    starts = lax.fori_loop(0, STEPS, backward, (zero,) * (PLANES * COMPS), unroll=2)
    tails = []
    for p in range(PLANES):
        for c in range(COMPS):
            j = p * COMPS + c
            whole = scan(starts[j], betas[p], up)
            tails.append(up(whole, 1))
            bd[wall, 0, c, p : p + 1, :] = whole[0:1]
            bd[wall, 1, c, p : p + 1, :] = ybuf[c, p, STEPS - 1][CHUNKS - 1 :]
    boundaries = to_walls(bd, (bd_send, bd_recv))
    from_walls(cf, (cf_send, cf_recv))
    betas_in = [jnp.zeros((PLANES, LANES), jnp.float32)]
    divisors, slopes = [], []
    for d in range(WALL):
        g0, h0, g1, h1 = (cf[d, q] for q in range(4))
        divisor = 1.0 / (1.0 - g0 * betas_in[d])
        slope = h0 * divisor
        divisors.append(divisor)
        slopes.append(slope)
        betas_in.append(g1 * betas_in[d] * slope + h1)
    from_walls(bd, (bd_send, bd_recv))
    for c in range(COMPS):
        alpha_in = [jnp.zeros((PLANES, LANES), jnp.float32)]
        heads = []
        for d in range(WALL):
            head = (bd[d, 0, c] + cf[d, 0] * alpha_in[d]) * divisors[d]
            heads.append(head)
            alpha_in.append(bd[d, 1, c] + cf[d, 2] * (alpha_in[d] + betas_in[d] * head))
        upper_value = jnp.zeros((PLANES, LANES), jnp.float32)
        x_low = upper_value
        x_high = upper_value
        for d in reversed(range(WALL)):
            x_high = jnp.where(wall == d, upper_value, x_high)
            upper_value = heads[d] + slopes[d] * upper_value
            x_low = jnp.where(wall == d, alpha_in[d] + betas_in[d] * upper_value, x_low)
        xlu[0, c] = x_low
        xlu[1, c] = x_high

    lows = []
    highs = []
    for p in range(PLANES):
        for c in range(COMPS):
            lows.append(jnp.broadcast_to(xlu[0, c, p : p + 1, :], (CHUNKS, LANES)))
            highs.append(tails[p * COMPS + c] + hc_ref[p] * xlu[1, c, p : p + 1, :])

    def correct(r, carry):
        for p in range(PLANES):
            b = b_ref[p, r]
            g = g_ref[p, r]
            for c in range(COMPS):
                j = p * COMPS + c
                value = ybuf[c, p, r] + b * highs[j] + g * lows[j]
                rhs[c, p, pl.ds(r, CHUNKS, stride=STEPS), :] = value
        return carry

    lax.fori_loop(0, STEPS, correct, 0, unroll=2)
    next_out = pltpu.make_async_copy(rhs, next_hbm, out_sem.at[1])
    next_out.start()
    for copy in sends:
        copy.wait_send()
    for copy in edges + coefficients + boundaries:
        copy.wait_send()
    dep_out.wait()
    next_out.wait()


def local(velocity, lower_weight, upper_weight, forces, cells, counts):
    f32 = jnp.float32
    grid = (COMPS, PLANES, ROWS, LANES)
    flat = (PLANES * ROWS, LANES)
    steps = (PLANES, STEPS, CHUNKS, LANES)
    dma = pltpu.SemaphoreType.DMA
    any_space = pl.BlockSpec(memory_space=pl.ANY)
    return pl.pallas_call(
        kernel,
        name="substep",
        out_shape=(jax.ShapeDtypeStruct(grid, f32), jax.ShapeDtypeStruct(grid, jnp.bfloat16)),
        in_specs=[any_space] * 5 + [pl.BlockSpec(memory_space=pltpu.SMEM)],
        out_specs=(any_space, any_space),
        scratch_shapes=[
            pltpu.VMEM((COMPS, SPAN, PLANES, SLOTS), f32),
            pltpu.VMEM((SPAN, PLANES, SLOTS), jnp.int32),
            pltpu.VMEM(grid, f32),
            pltpu.VMEM(flat, f32),
            pltpu.VMEM(flat, f32),
            pltpu.VMEM(grid, f32),
            pltpu.VMEM(grid, f32),
            pltpu.VMEM(grid, jnp.bfloat16),
            pltpu.VMEM((COMPS,) + steps, f32),
            pltpu.VMEM(flat, f32),
            pltpu.VMEM(flat, f32),
            pltpu.VMEM(flat, f32),
            pltpu.VMEM(steps, f32),
            pltpu.VMEM(steps, f32),
            pltpu.VMEM(steps, f32),
            pltpu.VMEM((PLANES, CHUNKS, LANES), f32),
            pltpu.VMEM((LANES, ROWS), f32),
            pltpu.VMEM((2, 16, ROWS), f32),
            pltpu.VMEM((2, 16, ROWS), f32),
            pltpu.VMEM((WALL, 4, PLANES, LANES), f32),
            pltpu.VMEM((WALL, 2, COMPS, PLANES, LANES), f32),
            pltpu.VMEM((2, COMPS, PLANES, LANES), f32),
            dma((SPAN,)),
            dma((SPAN,)),
            dma((2,)),
            dma((2,)),
            dma((WALL,)),
            dma((WALL,)),
            dma((WALL,)),
            dma((WALL,)),
            dma((5,)),
            dma((2,)),
        ],
        compiler_params=pltpu.CompilerParams(collective_id=0, has_side_effects=True),
    )(
        velocity,
        lower_weight.reshape(flat),
        upper_weight.reshape(flat),
        forces,
        cells,
        counts,
    )


def solution(mesh):
    placed = (
        P(None, None, "wall", "span"),
        P(None, "wall", "span"),
        P(None, "wall", "span"),
        P(None, "wall", "span", None, None, None),
        P("wall", "span", None, None, None),
        P("wall", "span", None, None),
    )
    return jax.shard_map(
        local,
        mesh=mesh,
        in_specs=placed,
        out_specs=(P(None, None, "wall", "span"), P(None, None, "wall", "span")),
        check_vma=False,
    )
```

```python
import functools

import jax
import jax.numpy as jnp
from jax import lax
from jax.experimental import pallas as pl
from jax.experimental.pallas import tpu as pltpu
from jax.sharding import PartitionSpec as P

MESH = pl.DeviceIdType.MESH
diffusion_number = 0.2
SPAN = 32
WALL = 4
PLANES = 4
COMPS = 3
ROWS = 256
LANES = 128
SLOTS = 768
CHUNKS = 8
STEPS = ROWS // CHUNKS
SEND_ORDER = (
    list(range(1, 8)) + list(range(16, 24)) + list(range(8, 16)) + list(range(24, 32))
)


def kernel(
    vel_hbm,
    low_hbm,
    upp_hbm,
    forces_hbm,
    cells_hbm,
    counts_hbm,
    next_hbm,
    dep_hbm,
    recv,
    cells,
    counts,
    vel,
    low,
    upp,
    rhs,
    field,
    dep,
    ybuf,
    w_ref,
    lw_ref,
    c_ref,
    a_ref,
    b_ref,
    g_ref,
    hc_ref,
    quant,
    pack,
    cols,
    hsend,
    hrecv,
    cf,
    bd,
    xlu,
    send_sem,
    recv_sem,
    halo_send,
    halo_recv,
    cf_send,
    cf_recv,
    bd_send,
    bd_recv,
    load_sem,
    out_sem,
):
    wall = lax.axis_index("wall")
    me = lax.axis_index("span")
    px, py, pc = me // 8, (me // 2) % 4, me % 2

    def peer(k, sign):
        dx, dy, dc = k // 8, (k // 2) % 4, k % 2
        x = (px + 4 + sign * dx) % 4
        y = (py + 4 + sign * dy) % 4
        c = (pc + dc) % 2
        return x * 8 + y * 2 + c

    low_flat = low.reshape(PLANES * ROWS, LANES)
    upp_flat = upp.reshape(PLANES * ROWS, LANES)
    w_flat = w_ref.reshape(PLANES * ROWS, LANES)
    lw_flat = lw_ref.reshape(PLANES * ROWS, LANES)
    c_flat = c_ref.reshape(PLANES * ROWS, LANES)
    loads = [
        pltpu.make_async_copy(counts_hbm.at[0, 0], counts, load_sem.at[0]),
        pltpu.make_async_copy(cells_hbm.at[0, 0], cells, load_sem.at[1]),
        pltpu.make_async_copy(forces_hbm.at[:, 0, 0, me], recv.at[:, 0], load_sem.at[2]),
    ]
    vel_loads = []
    for j in range(CHUNKS):
        rows = pl.ds(j * STEPS, STEPS)
        vel_loads.append(
            pltpu.make_async_copy(
                vel_hbm.at[:, :, rows, :], vel.at[:, :, :, j, :], load_sem.at[8 + j]
            )
        )
        for q, (source, target) in enumerate(((low_hbm, low), (upp_hbm, upp))):
            loads.append(
                pltpu.make_async_copy(
                    source.at[:, rows, :], target.at[:, :, j, :], load_sem.at[16 + 8 * q + j]
                )
            )
    for copy in vel_loads:
        copy.start()
    for copy in loads:
        copy.start()

    barrier = pltpu.get_barrier_semaphore()
    for k in range(1, SPAN):
        pl.semaphore_signal(barrier, inc=1, device_id={"span": peer(k, 1)}, device_id_type=MESH)
    for j in range(1, WALL):
        pl.semaphore_signal(
            barrier, inc=1, device_id={"wall": (wall + j) % WALL}, device_id_type=MESH
        )
    pl.semaphore_wait(barrier, SPAN - 1 + WALL - 1)

    def block_copy(k, target):
        return pltpu.make_async_remote_copy(
            src_ref=forces_hbm.at[:, 0, 0, target],
            dst_ref=recv.at[:, k],
            send_sem=send_sem.at[k],
            recv_sem=recv_sem.at[k],
            device_id={"span": target},
            device_id_type=MESH,
        )

    sends = [block_copy(k, peer(k, 1)) for k in SEND_ORDER]
    for copy in sends:
        copy.start()

    for copy in vel_loads:
        copy.wait()
    lane = lax.broadcasted_iota(jnp.int32, (ROWS, LANES), 1)
    edges = []
    for side, column in ((0, 0), (1, LANES - 1)):
        packed = jnp.zeros((ROWS, LANES), jnp.float32)
        for i in range(COMPS * PLANES):
            block = vel[i // PLANES, i % PLANES].reshape(ROWS, LANES)
            packed = jnp.where(lane == i, pltpu.roll(block, (i - column) % LANES, 1), packed)
        hsend[side] = jnp.transpose(packed)[0:16]
        target = (me + SPAN - 1) % SPAN if side == 0 else (me + 1) % SPAN
        copy = pltpu.make_async_remote_copy(
            src_ref=hsend.at[side],
            dst_ref=hrecv.at[side],
            send_sem=halo_send.at[side],
            recv_sem=halo_recv.at[side],
            device_id={"span": target},
            device_id_type=MESH,
        )
        copy.start()
        edges.append(copy)

    field[...] = jnp.zeros_like(field)
    for copy in loads:
        copy.wait()
    for copy in edges:
        copy.wait_recv()
    for side in range(2):
        pack[...] = jnp.zeros_like(pack)
        pack[0:16] = hrecv[side]
        cols[side] = jnp.transpose(pack[...])

    float8 = jnp.float8_e4m3fn
    one8, zero8 = jnp.ones((), float8), jnp.zeros((), float8)
    io_m = lax.broadcasted_iota(jnp.int32, (LANES, 256), 0).astype(jnp.int8)
    io_n = (lax.broadcasted_iota(jnp.int32, (256, 256), 0) - 128).astype(jnp.int8)
    slot = lax.broadcasted_iota(jnp.int32, (1, SLOTS), 1)
    last = lax.broadcasted_iota(jnp.int32, (CHUNKS, LANES), 1) == LANES - 1
    first = lax.broadcasted_iota(jnp.int32, (CHUNKS, LANES), 1) == 0

    def arrive(i):
        for j in range(2):
            @pl.when(2 * i + j > 0)
            def _():
                block_copy(2 * i + j, me).wait_recv()

    def quantize(i, buffer):
        blocks = [[recv[c, 2 * i + j] for c in range(COMPS)] for j in range(2)]
        top = None
        for block in blocks[0] + blocks[1]:
            top = jnp.abs(block) if top is None else jnp.maximum(top, jnp.abs(block))
        top = jnp.maximum(jnp.max(top, axis=(0, 1), keepdims=True), 1e-30)
        scale = 384.0 / top
        for j in range(2):
            for c in range(COMPS):
                rest = blocks[j][c] * scale
                for t in range(3):
                    term = rest.astype(float8).astype(jnp.float32)
                    quant[buffer, j, t, c] = term
                    rest = rest - term
        return top * (1.0 / 384.0)

    def deposit(i, carry):
        through, unit = carry

        @pl.when(i < SPAN // 2 - 1)
        def _():
            arrive(i + 1)

        buffer = i % 2
        sources = [peer(2 * i + j, -1) for j in range(2)]
        for p in range(PLANES):
            total = None
            for j in range(2):
                cell = cells[sources[j], p : p + 1, :]
                live = slot < counts[sources[j], p]
                row = ((cell >> 7) & 31) * CHUNKS + (cell >> 12)
                m = jnp.where(live, row & 127, -1).astype(jnp.int8)
                n = (((row >> 7) << 7) + (cell & 127) - 128).astype(jnp.int8)
                values = [
                    [quant[buffer, j, t, c, p : p + 1, :].astype(float8) for c in range(COMPS)]
                    for t in range(3)
                ]
                for start in range(0, SLOTS, 256):
                    part = slice(start, start + 256)
                    hot_m = m[:, part] == io_m
                    hot_n = jnp.where(n[:, part] == io_n, one8, zero8)
                    for t in range(3):
                        weighted = jnp.concatenate(
                            [jnp.where(hot_m, values[t][c][:, part], zero8) for c in range(COMPS)],
                            axis=0,
                        )
                        term = lax.dot_general(
                            weighted,
                            hot_n,
                            (((1,), (1,)), ((), ())),
                            preferred_element_type=jnp.float32,
                        )
                        total = term if total is None else total + term
            total = total.reshape(COMPS, LANES, 256) * unit
            for c in range(COMPS):
                field[c, p, 0:128, :] += total[c, :, 0:128]
                field[c, p, 128:256, :] += total[c, :, 128:256]
        for row in range(16):
            index = pl.ds(((i % 2) * 16 + row) * CHUNKS + i // 2, PLANES, stride=ROWS)
            lower = low_flat[index, :]
            upper = upp_flat[index, :]
            gain = 1.0 + lower * through
            inverse = 1.0 / (gain + upper)
            w_flat[index, :] = inverse
            lw_flat[index, :] = lower * inverse
            c_flat[index, :] = upper * inverse
            through = gain * inverse
        for half in range(2):
            r = 2 * i + half
            edge = pl.ds(pl.multiple_of(r * CHUNKS, CHUNKS), CHUNKS)
            columns = [cols[side, edge, :] for side in range(2)]
            for c in range(COMPS):
                planes = [vel[c, p, r] for p in range(PLANES)]
                for p in range(PLANES):
                    q = c * PLANES + p
                    here = planes[p]
                    above = jnp.where(
                        last,
                        pltpu.roll(columns[0], LANES - 1 - q, 1),
                        pltpu.roll(here, LANES - 1, 1),
                    )
                    below = jnp.where(
                        first, pltpu.roll(columns[1], (LANES - q) % LANES, 1), pltpu.roll(here, 1, 1)
                    )
                    stream = planes[(p + 1) % PLANES] + planes[(p + PLANES - 1) % PLANES]
                    rhs[c, p, r] = (
                        here
                        + diffusion_number * (stream - 2.0 * here)
                        + diffusion_number * (above + below - 2.0 * here)
                    )
        unit = quantize(jnp.minimum(i + 1, SPAN // 2 - 1), 1 - buffer)
        return through, unit

    arrive(0)
    unit = quantize(0, 0)
    lax.fori_loop(0, SPAN // 2, deposit, (jnp.ones((PLANES, LANES), jnp.float32), unit))

    plain = vel.reshape(COMPS, PLANES, ROWS, LANES)
    field_steps = field.reshape(COMPS, PLANES, STEPS, CHUNKS, LANES)
    moves = []
    for j in range(CHUNKS):
        copy = pltpu.make_async_copy(
            field_steps.at[:, :, :, j, :],
            plain.at[:, :, pl.ds(j * STEPS, STEPS), :],
            load_sem.at[8 + j],
        )
        copy.start()
        moves.append(copy)

    sub = lax.broadcasted_iota(jnp.int32, (CHUNKS, LANES), 0)

    def down(x, d):
        return jnp.where(sub >= d, pltpu.roll(x, d, 0), 0.0)

    def up(x, d):
        return jnp.where(sub < CHUNKS - d, pltpu.roll(x, CHUNKS - d, 0), 0.0)

    def levels(x, shift):
        out = [x]
        for d in (1, 2):
            out.append(out[-1] * shift(out[-1], d))
        return out

    def scan(x, factors, shift):
        for d, factor in zip((1, 2, 4), factors):
            x = x + factor * shift(x, d)
        return x

    def prefix(r, carry):
        out = []
        for p in range(PLANES):
            value = carry[p] * lw_ref[p, r]
            a_ref[p, r] = value
            out.append(value)
        return tuple(out)

    one = jnp.ones((CHUNKS, LANES), jnp.float32)
    alpha = lax.fori_loop(0, STEPS, prefix, (one,) * PLANES, unroll=4)
    alphas = [levels(x, down) for x in alpha]
    through_low = []
    for p in range(PLANES):
        ends = scan(jnp.where(sub == 0, alpha[p], 0.0), alphas[p], down)
        through_low.append(jnp.where(sub == 0, 1.0, pltpu.roll(ends, 1, 0)))

    def suffix(i, carry):
        r = STEPS - 1 - i
        out = []
        for p in range(PLANES):
            ratio = c_ref[p, r]
            b = carry[p] * ratio
            g = a_ref[p, r] * through_low[p] + ratio * carry[PLANES + p]
            b_ref[p, r] = b
            g_ref[p, r] = g
            out.append((b, g))
        return tuple(x[0] for x in out) + tuple(x[1] for x in out)

    zero = jnp.zeros((CHUNKS, LANES), jnp.float32)
    done = lax.fori_loop(0, STEPS, suffix, (one,) * PLANES + (zero,) * PLANES, unroll=4)
    beta, g_first = done[:PLANES], done[PLANES:]
    betas = [levels(x, up) for x in beta]
    g_carry = []
    for p in range(PLANES):
        g_all = scan(g_first[p], betas[p], up)
        g_carry.append(up(g_all, 1))
        h_all = scan(jnp.where(sub == CHUNKS - 1, beta[p], 0.0), betas[p], up)
        h_carry = jnp.where(sub == CHUNKS - 1, 1.0, pltpu.roll(h_all, CHUNKS - 1, 0))
        hc_ref[p] = h_carry
        cf[wall, 0, p : p + 1, :] = g_all[0:1]
        cf[wall, 1, p : p + 1, :] = h_all[0:1]
        last_g = g_ref[p, STEPS - 1] + b_ref[p, STEPS - 1] * g_carry[p]
        cf[wall, 2, p : p + 1, :] = last_g[CHUNKS - 1 :]
        last_h = b_ref[p, STEPS - 1] * h_carry
        cf[wall, 3, p : p + 1, :] = last_h[CHUNKS - 1 :]

    def to_walls(ref, sems):
        copies = []
        for j in range(1, WALL):
            copy = pltpu.make_async_remote_copy(
                src_ref=ref.at[wall],
                dst_ref=ref.at[wall],
                send_sem=sems[0].at[j],
                recv_sem=sems[1].at[j],
                device_id={"wall": (wall + j) % WALL},
                device_id_type=MESH,
            )
            copy.start()
            copies.append(copy)
        return copies

    def from_walls(ref, sems):
        for j in range(1, WALL):
            pltpu.make_async_remote_copy(
                src_ref=ref.at[wall],
                dst_ref=ref.at[(wall + WALL - j) % WALL],
                send_sem=sems[0].at[j],
                recv_sem=sems[1].at[j],
                device_id={"wall": (wall + j) % WALL},
                device_id_type=MESH,
            ).wait_recv()

    coefficients = to_walls(cf, (cf_send, cf_recv))

    def full_g(r, carry):
        for p in range(PLANES):
            g_ref[p, r] = g_ref[p, r] + b_ref[p, r] * g_carry[p]
        return carry

    lax.fori_loop(0, STEPS, full_g, 0, unroll=4)

    def forward(r, carry):
        out = []
        for p in range(PLANES):
            inverse = w_ref[p, r]
            factor = lw_ref[p, r]
            for c in range(COMPS):
                right = rhs[c, p, r] + field_steps[c, p, r]
                value = right * inverse + factor * carry[p * COMPS + c]
                ybuf[c, p, r] = value
                out.append(value)
        return tuple(out)

    ends = lax.fori_loop(0, STEPS, forward, (zero,) * (PLANES * COMPS), unroll=2)
    carries = []
    for p in range(PLANES):
        for c in range(COMPS):
            carries.append(down(scan(ends[p * COMPS + c], alphas[p], down), 1))

    def backward(i, carry):
        r = STEPS - 1 - i
        out = []
        for p in range(PLANES):
            ratio = c_ref[p, r]
            prefix_product = a_ref[p, r]
            for c in range(COMPS):
                j = p * COMPS + c
                value = ybuf[c, p, r] + prefix_product * carries[j] + ratio * carry[j]
                ybuf[c, p, r] = value
                out.append(value)
        return tuple(out)

    starts = lax.fori_loop(0, STEPS, backward, (zero,) * (PLANES * COMPS), unroll=2)
    tails = []
    for p in range(PLANES):
        for c in range(COMPS):
            j = p * COMPS + c
            whole = scan(starts[j], betas[p], up)
            tails.append(up(whole, 1))
            bd[wall, 0, c, p : p + 1, :] = whole[0:1]
            bd[wall, 1, c, p : p + 1, :] = ybuf[c, p, STEPS - 1][CHUNKS - 1 :]
    boundaries = to_walls(bd, (bd_send, bd_recv))
    from_walls(cf, (cf_send, cf_recv))
    betas_in = [jnp.zeros((PLANES, LANES), jnp.float32)]
    divisors, slopes = [], []
    for d in range(WALL):
        g0, h0, g1, h1 = (cf[d, q] for q in range(4))
        divisor = 1.0 / (1.0 - g0 * betas_in[d])
        slope = h0 * divisor
        divisors.append(divisor)
        slopes.append(slope)
        betas_in.append(g1 * betas_in[d] * slope + h1)
    for copy in moves:
        copy.wait()

    def narrow(q, carry):
        for c in range(COMPS):
            dep[c, q] = plain[c, q].astype(jnp.bfloat16)
        return carry

    lax.fori_loop(0, PLANES, narrow, 0)
    dep_out = pltpu.make_async_copy(dep, dep_hbm, load_sem.at[0])
    dep_out.start()
    from_walls(bd, (bd_send, bd_recv))
    for c in range(COMPS):
        alpha_in = [jnp.zeros((PLANES, LANES), jnp.float32)]
        heads = []
        for d in range(WALL):
            head = (bd[d, 0, c] + cf[d, 0] * alpha_in[d]) * divisors[d]
            heads.append(head)
            alpha_in.append(bd[d, 1, c] + cf[d, 2] * (alpha_in[d] + betas_in[d] * head))
        upper_value = jnp.zeros((PLANES, LANES), jnp.float32)
        x_low = upper_value
        x_high = upper_value
        for d in reversed(range(WALL)):
            x_high = jnp.where(wall == d, upper_value, x_high)
            upper_value = heads[d] + slopes[d] * upper_value
            x_low = jnp.where(wall == d, alpha_in[d] + betas_in[d] * upper_value, x_low)
        xlu[0, c] = x_low
        xlu[1, c] = x_high

    lows = []
    highs = []
    for p in range(PLANES):
        for c in range(COMPS):
            lows.append(jnp.broadcast_to(xlu[0, c, p : p + 1, :], (CHUNKS, LANES)))
            highs.append(tails[p * COMPS + c] + hc_ref[p] * xlu[1, c, p : p + 1, :])

    outs = []
    for p in range(PLANES):

        def correct(r, carry, p=p):
            b = b_ref[p, r]
            g = g_ref[p, r]
            for c in range(COMPS):
                j = p * COMPS + c
                rhs[c, p, r] = ybuf[c, p, r] + b * highs[j] + g * lows[j]
            return carry

        lax.fori_loop(0, STEPS, correct, 0, unroll=8)
        for j in range(CHUNKS):
            copy = pltpu.make_async_copy(
                rhs.at[:, p, :, j, :],
                next_hbm.at[:, p, pl.ds(j * STEPS, STEPS), :],
                out_sem.at[p * CHUNKS + j],
            )
            copy.start()
            outs.append(copy)
    for copy in sends:
        copy.wait_send()
    for copy in edges + coefficients + boundaries:
        copy.wait_send()
    dep_out.wait()
    for copy in outs:
        copy.wait()


def local(velocity, lower_weight, upper_weight, forces, cells, counts):
    f32 = jnp.float32
    grid = (COMPS, PLANES, ROWS, LANES)
    steps = (PLANES, STEPS, CHUNKS, LANES)
    dma = pltpu.SemaphoreType.DMA
    any_space = pl.BlockSpec(memory_space=pl.ANY)
    return pl.pallas_call(
        kernel,
        name="substep",
        out_shape=(jax.ShapeDtypeStruct(grid, f32), jax.ShapeDtypeStruct(grid, jnp.bfloat16)),
        in_specs=[any_space] * 6,
        out_specs=(any_space, any_space),
        scratch_shapes=[
            pltpu.VMEM((COMPS, SPAN, PLANES, SLOTS), f32),
            pltpu.VMEM((SPAN, PLANES, SLOTS), jnp.int32),
            pltpu.SMEM((SPAN, PLANES), jnp.int32),
            pltpu.VMEM((COMPS,) + steps, f32),
            pltpu.VMEM(steps, f32),
            pltpu.VMEM(steps, f32),
            pltpu.VMEM((COMPS,) + steps, f32),
            pltpu.VMEM(grid, f32),
            pltpu.VMEM(grid, jnp.bfloat16),
            pltpu.VMEM((COMPS,) + steps, f32),
            pltpu.VMEM(steps, f32),
            pltpu.VMEM(steps, f32),
            pltpu.VMEM(steps, f32),
            pltpu.VMEM(steps, f32),
            pltpu.VMEM(steps, f32),
            pltpu.VMEM(steps, f32),
            pltpu.VMEM((PLANES, CHUNKS, LANES), f32),
            pltpu.VMEM((2, 2, 3, COMPS, PLANES, SLOTS), f32),
            pltpu.VMEM((LANES, ROWS), f32),
            pltpu.VMEM((2, ROWS, LANES), f32),
            pltpu.VMEM((2, 16, ROWS), f32),
            pltpu.VMEM((2, 16, ROWS), f32),
            pltpu.VMEM((WALL, 4, PLANES, LANES), f32),
            pltpu.VMEM((WALL, 2, COMPS, PLANES, LANES), f32),
            pltpu.VMEM((2, COMPS, PLANES, LANES), f32),
            dma((SPAN,)),
            dma((SPAN,)),
            dma((2,)),
            dma((2,)),
            dma((WALL,)),
            dma((WALL,)),
            dma((WALL,)),
            dma((WALL,)),
            dma((32,)),
            dma((PLANES * CHUNKS,)),
        ],
        compiler_params=pltpu.CompilerParams(collective_id=0, has_side_effects=True),
    )(
        velocity,
        lower_weight,
        upper_weight,
        forces,
        cells,
        counts,
    )


def solution(mesh):
    placed = (
        P(None, None, "wall", "span"),
        P(None, "wall", "span"),
        P(None, "wall", "span"),
        P(None, "wall", "span", None, None, None),
        P("wall", "span", None, None, None),
        P("wall", "span", None, None),
    )
    return jax.shard_map(
        local,
        mesh=mesh,
        in_specs=placed,
        out_specs=(P(None, None, "wall", "span"), P(None, None, "wall", "span")),
        check_vma=False,
    )
```

```python
import functools

import jax
import jax.numpy as jnp
from jax import lax
from jax.experimental import pallas as pl
from jax.experimental.pallas import tpu as pltpu
from jax.sharding import PartitionSpec as P

MESH = pl.DeviceIdType.MESH
diffusion_number = 0.2
SPAN = 32
WALL = 4
PLANES = 4
COMPS = 3
ROWS = 256
LANES = 128
SLOTS = 768
CHUNKS = 8
STEPS = ROWS // CHUNKS
SEND_ORDER = (
    list(range(1, 8)) + list(range(16, 24)) + list(range(8, 16)) + list(range(24, 32))
)


def kernel(
    vel_hbm,
    low_hbm,
    upp_hbm,
    forces_hbm,
    cells_hbm,
    counts_hbm,
    part_hbm,
    b_hbm,
    g_hbm,
    ends_hbm,
    field_hbm,
    recv,
    cells,
    counts,
    vel,
    low,
    upp,
    rhs,
    field,
    ybuf,
    w_ref,
    lw_ref,
    c_ref,
    a_ref,
    b_ref,
    g_ref,
    hc_ref,
    ends_ref,
    quant,
    pack,
    cols,
    hsend,
    hrecv,
    cf,
    bd,
    xlu,
    send_sem,
    recv_sem,
    halo_send,
    halo_recv,
    cf_send,
    cf_recv,
    bd_send,
    bd_recv,
    load_sem,
    out_sem,
):
    wall = lax.axis_index("wall")
    me = lax.axis_index("span")
    px, py, pc = me // 8, (me // 2) % 4, me % 2

    def peer(k, sign):
        dx, dy, dc = k // 8, (k // 2) % 4, k % 2
        x = (px + 4 + sign * dx) % 4
        y = (py + 4 + sign * dy) % 4
        c = (pc + dc) % 2
        return x * 8 + y * 2 + c

    low_flat = low.reshape(PLANES * ROWS, LANES)
    upp_flat = upp.reshape(PLANES * ROWS, LANES)
    w_flat = w_ref.reshape(PLANES * ROWS, LANES)
    lw_flat = lw_ref.reshape(PLANES * ROWS, LANES)
    c_flat = c_ref.reshape(PLANES * ROWS, LANES)
    loads = [
        pltpu.make_async_copy(counts_hbm.at[0, 0], counts, load_sem.at[0]),
        pltpu.make_async_copy(cells_hbm.at[0, 0], cells, load_sem.at[1]),
        pltpu.make_async_copy(forces_hbm.at[:, 0, 0, me], recv.at[:, 0], load_sem.at[2]),
    ]
    vel_loads = []
    for j in range(CHUNKS):
        rows = pl.ds(j * STEPS, STEPS)
        vel_loads.append(
            pltpu.make_async_copy(
                vel_hbm.at[:, rows, :], vel.at[:, :, j, :], load_sem.at[8 + j]
            )
        )
        for q, (source, target) in enumerate(((low_hbm, low), (upp_hbm, upp))):
            loads.append(
                pltpu.make_async_copy(
                    source.at[:, rows, :], target.at[:, :, j, :], load_sem.at[16 + 8 * q + j]
                )
            )
    for copy in vel_loads:
        copy.start()
    for copy in loads:
        copy.start()

    barrier = pltpu.get_barrier_semaphore()
    for k in range(1, SPAN):
        pl.semaphore_signal(barrier, inc=1, device_id={"span": peer(k, 1)}, device_id_type=MESH)
    for j in range(1, WALL):
        pl.semaphore_signal(
            barrier, inc=1, device_id={"wall": (wall + j) % WALL}, device_id_type=MESH
        )
    pl.semaphore_wait(barrier, SPAN - 1 + WALL - 1)

    def block_copy(k, target):
        return pltpu.make_async_remote_copy(
            src_ref=forces_hbm.at[:, 0, 0, target],
            dst_ref=recv.at[:, k],
            send_sem=send_sem.at[k],
            recv_sem=recv_sem.at[k],
            device_id={"span": target},
            device_id_type=MESH,
        )

    sends = [block_copy(k, peer(k, 1)) for k in SEND_ORDER]
    sends[0].start()

    for copy in vel_loads:
        copy.wait()
    lane = lax.broadcasted_iota(jnp.int32, (ROWS, LANES), 1)
    edges = []
    for side, column in ((0, 0), (1, LANES - 1)):
        packed = jnp.zeros((ROWS, LANES), jnp.float32)
        for i in range(COMPS * PLANES):
            block = vel[i].reshape(ROWS, LANES)
            packed = jnp.where(lane == i, pltpu.roll(block, (i - column) % LANES, 1), packed)
        hsend[side] = jnp.transpose(packed)[0:16]
        target = (me + SPAN - 1) % SPAN if side == 0 else (me + 1) % SPAN
        copy = pltpu.make_async_remote_copy(
            src_ref=hsend.at[side],
            dst_ref=hrecv.at[side],
            send_sem=halo_send.at[side],
            recv_sem=halo_recv.at[side],
            device_id={"span": target},
            device_id_type=MESH,
        )
        copy.start()
        edges.append(copy)

    for copy in sends[1:]:
        copy.start()
    field[...] = jnp.zeros_like(field)
    cols[...] = jnp.zeros_like(cols)
    pack[...] = jnp.zeros_like(pack)
    for copy in loads:
        copy.wait()

    float8 = jnp.float8_e4m3fn
    one8, zero8 = jnp.ones((), float8), jnp.zeros((), float8)
    io_m = lax.broadcasted_iota(jnp.int32, (LANES, 256), 0).astype(jnp.int8)
    io_n = (lax.broadcasted_iota(jnp.int32, (256, 256), 0) - 128).astype(jnp.int8)
    slot = lax.broadcasted_iota(jnp.int32, (1, SLOTS), 1)
    last = lax.broadcasted_iota(jnp.int32, (CHUNKS, LANES), 1) == LANES - 1
    first = lax.broadcasted_iota(jnp.int32, (CHUNKS, LANES), 1) == 0

    def arrive(i):
        for j in range(2):
            @pl.when(2 * i + j > 0)
            def _():
                block_copy(2 * i + j, me).wait_recv()

    def quantize(i, buffer):
        blocks = [[recv[c, 2 * i + j] for c in range(COMPS)] for j in range(2)]
        top = None
        for block in blocks[0] + blocks[1]:
            top = jnp.abs(block) if top is None else jnp.maximum(top, jnp.abs(block))
        top = jnp.maximum(jnp.max(top, axis=(0, 1), keepdims=True), 1e-30)
        scale = 384.0 / top
        for j in range(2):
            for c in range(COMPS):
                rest = blocks[j][c] * scale
                for t in range(3):
                    term = rest.astype(float8).astype(jnp.float32)
                    quant[buffer, j, t, c] = term
                    rest = rest - term
        return top * (1.0 / 384.0)

    def deposit(i, carry):
        through, unit = carry

        @pl.when(i < SPAN // 2 - 1)
        def _():
            arrive(i + 1)

        @pl.when(i == 2)
        def _():
            for side in range(2):
                edges[side].wait_recv()
                pack[0:16] = hrecv[side]
                cols[side] = jnp.transpose(pack[...])

        buffer = i % 2
        sources = [peer(2 * i + j, -1) for j in range(2)]
        for p in range(PLANES):
            total = None
            for j in range(2):
                cell = cells[sources[j], p : p + 1, :]
                live = slot < counts[p, sources[j]]
                row = ((cell >> 7) & 31) * CHUNKS + (cell >> 12)
                m = jnp.where(live, row & 127, -1).astype(jnp.int8)
                n = (((row >> 7) << 7) + (cell & 127) - 128).astype(jnp.int8)
                values = [
                    [quant[buffer, j, t, c, p : p + 1, :].astype(float8) for c in range(COMPS)]
                    for t in range(3)
                ]
                for start in range(0, SLOTS, 256):
                    part = slice(start, start + 256)
                    hot_m = m[:, part] == io_m
                    hot_n = jnp.where(n[:, part] == io_n, one8, zero8)
                    for t in range(3):
                        weighted = jnp.concatenate(
                            [jnp.where(hot_m, values[t][c][:, part], zero8) for c in range(COMPS)],
                            axis=0,
                        )
                        term = lax.dot_general(
                            weighted,
                            hot_n,
                            (((1,), (1,)), ((), ())),
                            preferred_element_type=jnp.float32,
                        )
                        total = term if total is None else total + term
            total = total.reshape(COMPS, LANES, 256) * unit
            for c in range(COMPS):
                field[c * PLANES + p, 0:128, :] += total[c, :, 0:128]
                field[c * PLANES + p, 128:256, :] += total[c, :, 128:256]
        for row in range(16):
            index = pl.ds(((i % 2) * 16 + row) * CHUNKS + i // 2, PLANES, stride=ROWS)
            lower = low_flat[index, :]
            upper = upp_flat[index, :]
            gain = 1.0 + lower * through
            inverse = 1.0 / (gain + upper)
            w_flat[index, :] = inverse
            lw_flat[index, :] = lower * inverse
            c_flat[index, :] = upper * inverse
            through = gain * inverse
        for step in range(3):
            r = jnp.clip(3 * (i - 2) + step, 0, STEPS - 1)
            edge = pl.ds(pl.multiple_of(r * CHUNKS, CHUNKS), CHUNKS)
            columns = [cols[side, edge, :] for side in range(2)]
            for c in range(COMPS):
                planes = [vel[c * PLANES + p, r] for p in range(PLANES)]
                for p in range(PLANES):
                    q = c * PLANES + p
                    here = planes[p]
                    above = jnp.where(
                        last,
                        pltpu.roll(columns[0], LANES - 1 - q, 1),
                        pltpu.roll(here, LANES - 1, 1),
                    )
                    below = jnp.where(
                        first, pltpu.roll(columns[1], (LANES - q) % LANES, 1), pltpu.roll(here, 1, 1)
                    )
                    stream = planes[(p + 1) % PLANES] + planes[(p + PLANES - 1) % PLANES]
                    rhs[q, r] = (
                        here
                        + diffusion_number * (stream - 2.0 * here)
                        + diffusion_number * (above + below - 2.0 * here)
                    )
        unit = quantize(jnp.minimum(i + 1, SPAN // 2 - 1), 1 - buffer)
        return through, unit

    arrive(0)
    unit = quantize(0, 0)
    lax.fori_loop(0, SPAN // 2, deposit, (jnp.ones((PLANES, LANES), jnp.float32), unit))

    field_steps = field.reshape(COMPS * PLANES, STEPS, CHUNKS, LANES)
    outs = [pltpu.make_async_copy(field, field_hbm, out_sem.at[0])]
    outs[0].start()

    sub = lax.broadcasted_iota(jnp.int32, (CHUNKS, LANES), 0)

    def down(x, d):
        return jnp.where(sub >= d, pltpu.roll(x, d, 0), 0.0)

    def up(x, d):
        return jnp.where(sub < CHUNKS - d, pltpu.roll(x, CHUNKS - d, 0), 0.0)

    def levels(x, shift):
        out = [x]
        for d in (1, 2):
            out.append(out[-1] * shift(out[-1], d))
        return out

    def scan(x, factors, shift):
        for d, factor in zip((1, 2, 4), factors):
            x = x + factor * shift(x, d)
        return x

    def prefix(r, carry):
        out = []
        for p in range(PLANES):
            value = carry[p] * lw_ref[p, r]
            a_ref[p, r] = value
            out.append(value)
        return tuple(out)

    one = jnp.ones((CHUNKS, LANES), jnp.float32)
    alpha = lax.fori_loop(0, STEPS, prefix, (one,) * PLANES, unroll=4)
    alphas = [levels(x, down) for x in alpha]
    through_low = []
    for p in range(PLANES):
        ends = scan(jnp.where(sub == 0, alpha[p], 0.0), alphas[p], down)
        through_low.append(jnp.where(sub == 0, 1.0, pltpu.roll(ends, 1, 0)))

    def suffix(i, carry):
        r = STEPS - 1 - i
        out = []
        for p in range(PLANES):
            ratio = c_ref[p, r]
            b = carry[p] * ratio
            g = a_ref[p, r] * through_low[p] + ratio * carry[PLANES + p]
            b_ref[p, r] = b
            g_ref[p, r] = g
            out.append((b, g))
        return tuple(x[0] for x in out) + tuple(x[1] for x in out)

    zero = jnp.zeros((CHUNKS, LANES), jnp.float32)
    done = lax.fori_loop(0, STEPS, suffix, (one,) * PLANES + (zero,) * PLANES, unroll=4)
    beta, g_first = done[:PLANES], done[PLANES:]
    betas = [levels(x, up) for x in beta]
    g_carry = []
    for p in range(PLANES):
        g_all = scan(g_first[p], betas[p], up)
        g_carry.append(up(g_all, 1))
        h_all = scan(jnp.where(sub == CHUNKS - 1, beta[p], 0.0), betas[p], up)
        h_carry = jnp.where(sub == CHUNKS - 1, 1.0, pltpu.roll(h_all, CHUNKS - 1, 0))
        hc_ref[p] = h_carry
        cf[wall, 0, p : p + 1, :] = g_all[0:1]
        cf[wall, 1, p : p + 1, :] = h_all[0:1]
        last_g = g_ref[p, STEPS - 1] + b_ref[p, STEPS - 1] * g_carry[p]
        cf[wall, 2, p : p + 1, :] = last_g[CHUNKS - 1 :]
        last_h = b_ref[p, STEPS - 1] * h_carry
        cf[wall, 3, p : p + 1, :] = last_h[CHUNKS - 1 :]

    def to_walls(ref, sems):
        copies = []
        for j in range(1, WALL):
            copy = pltpu.make_async_remote_copy(
                src_ref=ref.at[wall],
                dst_ref=ref.at[wall],
                send_sem=sems[0].at[j],
                recv_sem=sems[1].at[j],
                device_id={"wall": (wall + j) % WALL},
                device_id_type=MESH,
            )
            copy.start()
            copies.append(copy)
        return copies

    def from_walls(ref, sems):
        for j in range(1, WALL):
            pltpu.make_async_remote_copy(
                src_ref=ref.at[wall],
                dst_ref=ref.at[(wall + WALL - j) % WALL],
                send_sem=sems[0].at[j],
                recv_sem=sems[1].at[j],
                device_id={"wall": (wall + j) % WALL},
                device_id_type=MESH,
            ).wait_recv()

    coefficients = to_walls(cf, (cf_send, cf_recv))

    def full_g(r, carry):
        for p in range(PLANES):
            g_ref[p, r] = g_ref[p, r] + b_ref[p, r] * g_carry[p]
        return carry

    lax.fori_loop(0, STEPS, full_g, 0, unroll=4)
    for q, (source, target) in enumerate(((b_ref, b_hbm), (g_ref, g_hbm))):
        outs.append(pltpu.make_async_copy(source, target, out_sem.at[1 + q]))
        outs[-1].start()

    def forward(r, carry):
        out = []
        for p in range(PLANES):
            inverse = w_ref[p, r]
            factor = lw_ref[p, r]
            for c in range(COMPS):
                right = rhs[c * PLANES + p, r] + field_steps[c * PLANES + p, r]
                value = right * inverse + factor * carry[p * COMPS + c]
                ybuf[c * PLANES + p, r] = value
                out.append(value)
        return tuple(out)

    ends = lax.fori_loop(0, STEPS, forward, (zero,) * (PLANES * COMPS), unroll=2)
    carries = []
    for p in range(PLANES):
        for c in range(COMPS):
            carries.append(down(scan(ends[p * COMPS + c], alphas[p], down), 1))

    def backward(i, carry):
        r = STEPS - 1 - i
        out = []
        for p in range(PLANES):
            ratio = c_ref[p, r]
            prefix_product = a_ref[p, r]
            for c in range(COMPS):
                j = p * COMPS + c
                value = ybuf[c * PLANES + p, r] + prefix_product * carries[j] + ratio * carry[j]
                ybuf[c * PLANES + p, r] = value
                out.append(value)
        return tuple(out)

    starts = lax.fori_loop(0, STEPS, backward, (zero,) * (PLANES * COMPS), unroll=2)
    tails = []
    for p in range(PLANES):
        for c in range(COMPS):
            j = p * COMPS + c
            whole = scan(starts[j], betas[p], up)
            tails.append(up(whole, 1))
            bd[wall, 0, c, p : p + 1, :] = whole[0:1]
            bd[wall, 1, c, p : p + 1, :] = ybuf[c * PLANES + p, STEPS - 1][CHUNKS - 1 :]
    boundaries = to_walls(bd, (bd_send, bd_recv))
    outs.append(pltpu.make_async_copy(ybuf, part_hbm, out_sem.at[3]))
    outs[-1].start()
    from_walls(cf, (cf_send, cf_recv))
    betas_in = [jnp.zeros((PLANES, LANES), jnp.float32)]
    divisors, slopes = [], []
    for d in range(WALL):
        g0, h0, g1, h1 = (cf[d, q] for q in range(4))
        divisor = 1.0 / (1.0 - g0 * betas_in[d])
        slope = h0 * divisor
        divisors.append(divisor)
        slopes.append(slope)
        betas_in.append(g1 * betas_in[d] * slope + h1)
    from_walls(bd, (bd_send, bd_recv))
    for c in range(COMPS):
        alpha_in = [jnp.zeros((PLANES, LANES), jnp.float32)]
        heads = []
        for d in range(WALL):
            head = (bd[d, 0, c] + cf[d, 0] * alpha_in[d]) * divisors[d]
            heads.append(head)
            alpha_in.append(bd[d, 1, c] + cf[d, 2] * (alpha_in[d] + betas_in[d] * head))
        upper_value = jnp.zeros((PLANES, LANES), jnp.float32)
        x_low = upper_value
        x_high = upper_value
        for d in reversed(range(WALL)):
            x_high = jnp.where(wall == d, upper_value, x_high)
            upper_value = heads[d] + slopes[d] * upper_value
            x_low = jnp.where(wall == d, alpha_in[d] + betas_in[d] * upper_value, x_low)
        xlu[0, c] = x_low
        xlu[1, c] = x_high

    for p in range(PLANES):
        for c in range(COMPS):
            q = c * PLANES + p
            ends_ref[0, q] = tails[p * COMPS + c] + hc_ref[p] * xlu[1, c, p : p + 1, :]
            ends_ref[1, q] = jnp.broadcast_to(xlu[0, c, p : p + 1, :], (CHUNKS, LANES))
    outs.append(pltpu.make_async_copy(ends_ref, ends_hbm, out_sem.at[4]))
    outs[-1].start()
    for copy in sends:
        copy.wait_send()
    for copy in edges + coefficients + boundaries:
        copy.wait_send()
    for copy in outs:
        copy.wait()


def finish(
    part_hbm,
    b_hbm,
    g_hbm,
    ends_hbm,
    field_hbm,
    next_hbm,
    dep_hbm,
    part,
    b_ref,
    g_ref,
    ends,
    field,
    dep,
    sems,
    part_sem,
    field_sem,
    out_sem,
    dep_sem,
):
    small = [
        pltpu.make_async_copy(source, target, sems.at[q])
        for q, (source, target) in enumerate(((b_hbm, b_ref), (g_hbm, g_ref), (ends_hbm, ends)))
    ]
    groups = [pl.ds(c * PLANES, PLANES) for c in range(COMPS)]
    parts = [
        pltpu.make_async_copy(part_hbm.at[groups[c]], part.at[groups[c]], part_sem.at[c])
        for c in range(COMPS)
    ]
    fields = []
    for j in range(CHUNKS):
        fields.append(
            pltpu.make_async_copy(
                field_hbm.at[:, :, j, :],
                field.at[:, pl.ds(j * STEPS, STEPS), :],
                field_sem.at[j],
            )
        )
    for copy in small[:2] + parts[:1] + small[2:] + parts[1:] + fields:
        copy.start()
    for copy in small:
        copy.wait()
    outs = []
    for c in range(COMPS):
        parts[c].wait()
        highs = [ends[0, c * PLANES + p] for p in range(PLANES)]
        lows = [ends[1, c * PLANES + p] for p in range(PLANES)]

        def correct(r, carry, c=c, highs=highs, lows=lows):
            for p in range(PLANES):
                q = c * PLANES + p
                part[q, r] = part[q, r] + b_ref[p, r] * highs[p] + g_ref[p, r] * lows[p]
            return carry

        lax.fori_loop(0, STEPS, correct, 0, unroll=8)
        for j in range(CHUNKS):
            copy = pltpu.make_async_copy(
                part.at[groups[c], :, j, :],
                next_hbm.at[groups[c], pl.ds(j * STEPS, STEPS), :],
                out_sem.at[c * CHUNKS + j],
            )
            copy.start()
            outs.append(copy)
    for copy in fields:
        copy.wait()
    for c in range(COMPS):

        def narrow(p, carry, c=c):
            dep[c * PLANES + p] = field[c * PLANES + p].astype(jnp.bfloat16)
            return carry

        lax.fori_loop(0, PLANES, narrow, 0)
        copy = pltpu.make_async_copy(dep.at[groups[c]], dep_hbm.at[groups[c]], dep_sem.at[c])
        copy.start()
        outs.append(copy)
    for copy in outs:
        copy.wait()


def local(velocity, lower_weight, upper_weight, forces, cells, counts):
    f32 = jnp.float32
    flat = (COMPS * PLANES, ROWS, LANES)
    steps = (PLANES, STEPS, CHUNKS, LANES)
    all_steps = (COMPS * PLANES, STEPS, CHUNKS, LANES)
    dma = pltpu.SemaphoreType.DMA
    any_space = pl.BlockSpec(memory_space=pl.ANY)
    ends = (2, COMPS * PLANES, CHUNKS, LANES)
    solved = pl.pallas_call(
        kernel,
        name="substep",
        out_shape=(
            jax.ShapeDtypeStruct(all_steps, f32),
            jax.ShapeDtypeStruct(steps, f32),
            jax.ShapeDtypeStruct(steps, f32),
            jax.ShapeDtypeStruct(ends, f32),
            jax.ShapeDtypeStruct(flat, f32),
        ),
        in_specs=[any_space] * 6,
        out_specs=(any_space,) * 5,
        scratch_shapes=[
            pltpu.VMEM((COMPS, SPAN, PLANES, SLOTS), f32),
            pltpu.VMEM((SPAN, PLANES, SLOTS), jnp.int32),
            pltpu.SMEM((PLANES, SPAN), jnp.int32),
            pltpu.VMEM(all_steps, f32),
            pltpu.VMEM(steps, f32),
            pltpu.VMEM(steps, f32),
            pltpu.VMEM(all_steps, f32),
            pltpu.VMEM(flat, f32),
            pltpu.VMEM(all_steps, f32),
            pltpu.VMEM(steps, f32),
            pltpu.VMEM(steps, f32),
            pltpu.VMEM(steps, f32),
            pltpu.VMEM(steps, f32),
            pltpu.VMEM(steps, f32),
            pltpu.VMEM(steps, f32),
            pltpu.VMEM((PLANES, CHUNKS, LANES), f32),
            pltpu.VMEM(ends, f32),
            pltpu.VMEM((2, 2, 3, COMPS, PLANES, SLOTS), f32),
            pltpu.VMEM((LANES, ROWS), f32),
            pltpu.VMEM((2, ROWS, LANES), f32),
            pltpu.VMEM((2, 16, ROWS), f32),
            pltpu.VMEM((2, 16, ROWS), f32),
            pltpu.VMEM((WALL, 4, PLANES, LANES), f32),
            pltpu.VMEM((WALL, 2, COMPS, PLANES, LANES), f32),
            pltpu.VMEM((2, COMPS, PLANES, LANES), f32),
            dma((SPAN,)),
            dma((SPAN,)),
            dma((2,)),
            dma((2,)),
            dma((WALL,)),
            dma((WALL,)),
            dma((WALL,)),
            dma((WALL,)),
            dma((32,)),
            dma((5,)),
        ],
        compiler_params=pltpu.CompilerParams(collective_id=0, has_side_effects=True),
    )(
        velocity.reshape(flat),
        lower_weight,
        upper_weight,
        forces,
        cells,
        jnp.swapaxes(counts, 2, 3),
    )
    velocity_next, deposit = pl.pallas_call(
        finish,
        name="finish",
        out_shape=(jax.ShapeDtypeStruct(flat, f32), jax.ShapeDtypeStruct(flat, jnp.bfloat16)),
        in_specs=[any_space] * 5,
        out_specs=(any_space,) * 2,
        scratch_shapes=[
            pltpu.VMEM(all_steps, f32),
            pltpu.VMEM(steps, f32),
            pltpu.VMEM(steps, f32),
            pltpu.VMEM(ends, f32),
            pltpu.VMEM(flat, f32),
            pltpu.VMEM(flat, jnp.bfloat16),
            dma((3,)),
            dma((COMPS,)),
            dma((CHUNKS,)),
            dma((COMPS * CHUNKS,)),
            dma((COMPS,)),
        ],
    )(*solved[:4], solved[4].reshape(all_steps))
    return velocity_next.reshape(velocity.shape), deposit.reshape(velocity.shape)


def solution(mesh):
    placed = (
        P(None, None, "wall", "span"),
        P(None, "wall", "span"),
        P(None, "wall", "span"),
        P(None, "wall", "span", None, None, None),
        P("wall", "span", None, None, None),
        P("wall", "span", None, None),
    )
    return jax.shard_map(
        local,
        mesh=mesh,
        in_specs=placed,
        out_specs=(P(None, None, "wall", "span"), P(None, None, "wall", "span")),
        check_vma=False,
    )
```

```python
import functools

import jax
import jax.numpy as jnp
from jax import lax
from jax.experimental import pallas as pl
from jax.experimental.pallas import tpu as pltpu
from jax.sharding import PartitionSpec as P

MESH = pl.DeviceIdType.MESH
diffusion_number = 0.2
SPAN = 32
WALL = 4
PLANES = 4
COMPS = 3
ROWS = 256
LANES = 128
SLOTS = 768
CHUNKS = 8
STEPS = ROWS // CHUNKS
GROUP = 4
TURNS = SPAN // GROUP


def kernel(
    vel_hbm,
    low_hbm,
    upp_hbm,
    forces_hbm,
    cells_hbm,
    counts_hbm,
    part_hbm,
    b_hbm,
    g_hbm,
    ends_hbm,
    field_hbm,
    recv,
    cells,
    counts,
    vel,
    low,
    upp,
    rhs,
    field,
    ybuf,
    w_ref,
    lw_ref,
    c_ref,
    a_ref,
    b_ref,
    g_ref,
    hc_ref,
    ends_ref,
    spots,
    quant,
    pack,
    cols,
    hsend,
    hrecv,
    cf,
    bd,
    xlu,
    send_sem,
    recv_sem,
    halo_send,
    halo_recv,
    cf_send,
    cf_recv,
    bd_send,
    bd_recv,
    load_sem,
    out_sem,
):
    wall = lax.axis_index("wall")
    me = lax.axis_index("span")
    px, py, pc = me // 8, (me // 2) % 4, me % 2

    def peer(k, sign):
        low_y, low_x, high_y, high_x, dc = (k // 2) % 2, (k // 4) % 2, (k // 8) % 2, k // 16, k % 2
        dy = low_y + 2 * high_y
        dx = ((low_x + 2 * high_x) * (1 + 2 * low_y)) % 4
        x = (px + 4 + sign * dx) % 4
        y = (py + 4 + sign * dy) % 4
        c = (pc + dc) % 2
        return x * 8 + y * 2 + c

    low_flat = low.reshape(PLANES * ROWS, LANES)
    upp_flat = upp.reshape(PLANES * ROWS, LANES)
    w_flat = w_ref.reshape(PLANES * ROWS, LANES)
    lw_flat = lw_ref.reshape(PLANES * ROWS, LANES)
    c_flat = c_ref.reshape(PLANES * ROWS, LANES)
    loads = [
        pltpu.make_async_copy(counts_hbm.at[0, 0], counts, load_sem.at[0]),
        pltpu.make_async_copy(cells_hbm.at[0, 0], cells, load_sem.at[1]),
        pltpu.make_async_copy(forces_hbm.at[:, 0, 0, me], recv.at[:, 0], load_sem.at[2]),
    ]
    vel_loads = []
    for j in range(CHUNKS):
        rows = pl.ds(j * STEPS, STEPS)
        vel_loads.append(
            pltpu.make_async_copy(
                vel_hbm.at[:, rows, :], vel.at[:, :, j, :], load_sem.at[8 + j]
            )
        )
        for q, (source, target) in enumerate(((low_hbm, low), (upp_hbm, upp))):
            loads.append(
                pltpu.make_async_copy(
                    source.at[:, rows, :], target.at[:, :, j, :], load_sem.at[16 + 8 * q + j]
                )
            )
    for copy in vel_loads:
        copy.start()
    for copy in loads:
        copy.start()

    barrier = pltpu.get_barrier_semaphore()
    for k in range(1, SPAN):
        pl.semaphore_signal(barrier, inc=1, device_id={"span": peer(k, 1)}, device_id_type=MESH)
    for j in range(1, WALL):
        pl.semaphore_signal(
            barrier, inc=1, device_id={"wall": (wall + j) % WALL}, device_id_type=MESH
        )
    pl.semaphore_wait(barrier, SPAN - 1 + WALL - 1)

    def block_copy(k, target):
        return pltpu.make_async_remote_copy(
            src_ref=forces_hbm.at[:, 0, 0, target],
            dst_ref=recv.at[:, k],
            send_sem=send_sem.at[k],
            recv_sem=recv_sem.at[k],
            device_id={"span": target},
            device_id_type=MESH,
        )

    sends = [block_copy(k, peer(k, 1)) for k in range(1, SPAN)]
    for copy in sends[:7]:
        copy.start()

    for copy in vel_loads:
        copy.wait()
    lane = lax.broadcasted_iota(jnp.int32, (ROWS, LANES), 1)
    edges = []
    for side, column in ((0, 0), (1, LANES - 1)):
        packed = jnp.zeros((ROWS, LANES), jnp.float32)
        for i in range(COMPS * PLANES):
            block = vel[i].reshape(ROWS, LANES)
            packed = jnp.where(lane == i, pltpu.roll(block, (i - column) % LANES, 1), packed)
        hsend[side] = jnp.transpose(packed)[0:16]
        target = (me + SPAN - 1) % SPAN if side == 0 else (me + 1) % SPAN
        copy = pltpu.make_async_remote_copy(
            src_ref=hsend.at[side],
            dst_ref=hrecv.at[side],
            send_sem=halo_send.at[side],
            recv_sem=halo_recv.at[side],
            device_id={"span": target},
            device_id_type=MESH,
        )
        copy.start()
        edges.append(copy)

    for copy in sends[7:]:
        copy.start()
    field[...] = jnp.zeros_like(field)
    cols[...] = jnp.zeros_like(cols)
    pack[...] = jnp.zeros_like(pack)
    for copy in loads:
        copy.wait()

    slot = lax.broadcasted_iota(jnp.int32, (PLANES, SLOTS), 1)
    plane = lax.broadcasted_iota(jnp.int32, (PLANES, SLOTS), 0)

    def locate(s, carry):
        cell = cells[s]
        limit = jnp.where(plane < 1, counts[0, s], counts[1, s])
        limit = jnp.where(plane < 2, limit, jnp.where(plane < 3, counts[2, s], counts[3, s]))
        row = ((cell >> 7) & 31) * CHUNKS + (cell >> 12)
        spots[0, s] = jnp.where(slot < limit, row & 127, -1)
        spots[1, s] = (((row >> 7) << 7) + (cell & 127) - 128)
        return carry

    lax.fori_loop(0, SPAN, locate, 0, unroll=2)

    float8 = jnp.float8_e4m3fn
    one8, zero8 = jnp.ones((), float8), jnp.zeros((), float8)
    io_m = lax.broadcasted_iota(jnp.int32, (LANES, 256), 0).astype(jnp.int8)
    io_n = (lax.broadcasted_iota(jnp.int32, (256, 256), 0) - 128).astype(jnp.int8)
    last = lax.broadcasted_iota(jnp.int32, (CHUNKS, LANES), 1) == LANES - 1
    first = lax.broadcasted_iota(jnp.int32, (CHUNKS, LANES), 1) == 0

    def arrive(i):
        for j in range(GROUP):
            block_copy(GROUP * i + j, me).wait_recv()

    def quantize(i, buffer):
        blocks = [[recv[c, GROUP * i + j] for c in range(COMPS)] for j in range(GROUP)]
        top = None
        for block in sum(blocks, []):
            top = jnp.abs(block) if top is None else jnp.maximum(top, jnp.abs(block))
        top = jnp.maximum(jnp.max(top, axis=(0, 1), keepdims=True), 1e-30)
        scale = 384.0 / top
        for j in range(GROUP):
            for c in range(COMPS):
                rest = blocks[j][c] * scale
                for t in range(3):
                    term = rest.astype(float8).astype(jnp.float32)
                    quant[buffer, j, t, c] = term
                    rest = rest - term
        return top * (1.0 / 384.0)

    def deposit(i, carry):
        through, unit = carry

        @pl.when(i < TURNS - 1)
        def _():
            arrive(i + 1)

        @pl.when(i == 1)
        def _():
            for side in range(2):
                edges[side].wait_recv()
                pack[0:16] = hrecv[side]
                cols[side] = jnp.transpose(pack[...])

        buffer = i % 2
        sources = [peer(GROUP * i + j, -1) for j in range(GROUP)]
        for p in range(PLANES):
            total = None
            for j in range(GROUP):
                m = spots[0, sources[j], p : p + 1, :].astype(jnp.int8)
                n = spots[1, sources[j], p : p + 1, :].astype(jnp.int8)
                values = [
                    [quant[buffer, j, t, c, p : p + 1, :].astype(float8) for c in range(COMPS)]
                    for t in range(3)
                ]
                for start in range(0, SLOTS, 256):
                    part = slice(start, start + 256)
                    hot_m = m[:, part] == io_m
                    hot_n = jnp.where(n[:, part] == io_n, one8, zero8)
                    for t in range(3):
                        weighted = jnp.concatenate(
                            [jnp.where(hot_m, values[t][c][:, part], zero8) for c in range(COMPS)],
                            axis=0,
                        )
                        term = lax.dot_general(
                            weighted,
                            hot_n,
                            (((1,), (1,)), ((), ())),
                            preferred_element_type=jnp.float32,
                        )
                        total = term if total is None else total + term
            total = total.reshape(COMPS, LANES, 256) * unit
            for c in range(COMPS):
                field[c * PLANES + p, 0:128, :] += total[c, :, 0:128]
                field[c * PLANES + p, 128:256, :] += total[c, :, 128:256]
        for row in range(ROWS // TURNS):
            index = pl.ds(row * CHUNKS + i, PLANES, stride=ROWS)
            lower = low_flat[index, :]
            upper = upp_flat[index, :]
            gain = 1.0 + lower * through
            inverse = 1.0 / (gain + upper)
            w_flat[index, :] = inverse
            lw_flat[index, :] = lower * inverse
            c_flat[index, :] = upper * inverse
            through = gain * inverse
        for step in range(5):
            r = jnp.clip(5 * (i - 1) + step, 0, STEPS - 1)
            edge = pl.ds(pl.multiple_of(r * CHUNKS, CHUNKS), CHUNKS)
            columns = [cols[side, edge, :] for side in range(2)]
            for c in range(COMPS):
                planes = [vel[c * PLANES + p, r] for p in range(PLANES)]
                for p in range(PLANES):
                    q = c * PLANES + p
                    here = planes[p]
                    above = jnp.where(
                        last,
                        pltpu.roll(columns[0], LANES - 1 - q, 1),
                        pltpu.roll(here, LANES - 1, 1),
                    )
                    below = jnp.where(
                        first, pltpu.roll(columns[1], (LANES - q) % LANES, 1), pltpu.roll(here, 1, 1)
                    )
                    stream = planes[(p + 1) % PLANES] + planes[(p + PLANES - 1) % PLANES]
                    rhs[q, r] = (
                        here
                        + diffusion_number * (stream - 2.0 * here)
                        + diffusion_number * (above + below - 2.0 * here)
                    )
        unit = quantize(jnp.minimum(i + 1, TURNS - 1), 1 - buffer)
        return through, unit

    for k in range(1, GROUP):
        block_copy(k, me).wait_recv()
    unit = quantize(0, 0)
    lax.fori_loop(0, TURNS, deposit, (jnp.ones((PLANES, LANES), jnp.float32), unit))

    field_steps = field.reshape(COMPS * PLANES, STEPS, CHUNKS, LANES)
    outs = [pltpu.make_async_copy(field, field_hbm, out_sem.at[0])]
    outs[0].start()

    sub = lax.broadcasted_iota(jnp.int32, (CHUNKS, LANES), 0)

    def down(x, d):
        return jnp.where(sub >= d, pltpu.roll(x, d, 0), 0.0)

    def up(x, d):
        return jnp.where(sub < CHUNKS - d, pltpu.roll(x, CHUNKS - d, 0), 0.0)

    def levels(x, shift):
        out = [x]
        for d in (1, 2):
            out.append(out[-1] * shift(out[-1], d))
        return out

    def scan(x, factors, shift):
        for d, factor in zip((1, 2, 4), factors):
            x = x + factor * shift(x, d)
        return x

    def prefix(r, carry):
        out = []
        for p in range(PLANES):
            value = carry[p] * lw_ref[p, r]
            a_ref[p, r] = value
            out.append(value)
        return tuple(out)

    one = jnp.ones((CHUNKS, LANES), jnp.float32)
    alpha = lax.fori_loop(0, STEPS, prefix, (one,) * PLANES, unroll=4)
    alphas = [levels(x, down) for x in alpha]
    through_low = []
    for p in range(PLANES):
        ends = scan(jnp.where(sub == 0, alpha[p], 0.0), alphas[p], down)
        through_low.append(jnp.where(sub == 0, 1.0, pltpu.roll(ends, 1, 0)))

    def suffix(i, carry):
        r = STEPS - 1 - i
        out = []
        for p in range(PLANES):
            ratio = c_ref[p, r]
            b = carry[p] * ratio
            g = a_ref[p, r] * through_low[p] + ratio * carry[PLANES + p]
            b_ref[p, r] = b
            g_ref[p, r] = g
            out.append((b, g))
        return tuple(x[0] for x in out) + tuple(x[1] for x in out)

    zero = jnp.zeros((CHUNKS, LANES), jnp.float32)
    done = lax.fori_loop(0, STEPS, suffix, (one,) * PLANES + (zero,) * PLANES, unroll=4)
    beta, g_first = done[:PLANES], done[PLANES:]
    betas = [levels(x, up) for x in beta]
    g_carry = []
    for p in range(PLANES):
        g_all = scan(g_first[p], betas[p], up)
        g_carry.append(up(g_all, 1))
        h_all = scan(jnp.where(sub == CHUNKS - 1, beta[p], 0.0), betas[p], up)
        h_carry = jnp.where(sub == CHUNKS - 1, 1.0, pltpu.roll(h_all, CHUNKS - 1, 0))
        hc_ref[p] = h_carry
        cf[wall, 0, p : p + 1, :] = g_all[0:1]
        cf[wall, 1, p : p + 1, :] = h_all[0:1]
        last_g = g_ref[p, STEPS - 1] + b_ref[p, STEPS - 1] * g_carry[p]
        cf[wall, 2, p : p + 1, :] = last_g[CHUNKS - 1 :]
        last_h = b_ref[p, STEPS - 1] * h_carry
        cf[wall, 3, p : p + 1, :] = last_h[CHUNKS - 1 :]

    def to_walls(ref, sems):
        copies = []
        for j in range(1, WALL):
            copy = pltpu.make_async_remote_copy(
                src_ref=ref.at[wall],
                dst_ref=ref.at[wall],
                send_sem=sems[0].at[j],
                recv_sem=sems[1].at[j],
                device_id={"wall": (wall + j) % WALL},
                device_id_type=MESH,
            )
            copy.start()
            copies.append(copy)
        return copies

    def from_walls(ref, sems):
        for j in range(1, WALL):
            pltpu.make_async_remote_copy(
                src_ref=ref.at[wall],
                dst_ref=ref.at[(wall + WALL - j) % WALL],
                send_sem=sems[0].at[j],
                recv_sem=sems[1].at[j],
                device_id={"wall": (wall + j) % WALL},
                device_id_type=MESH,
            ).wait_recv()

    coefficients = to_walls(cf, (cf_send, cf_recv))

    def full_g(r, carry):
        for p in range(PLANES):
            g_ref[p, r] = g_ref[p, r] + b_ref[p, r] * g_carry[p]
        return carry

    lax.fori_loop(0, STEPS, full_g, 0, unroll=4)
    for q, (source, target) in enumerate(((b_ref, b_hbm), (g_ref, g_hbm))):
        outs.append(pltpu.make_async_copy(source, target, out_sem.at[1 + q]))
        outs[-1].start()

    def forward(r, carry):
        out = []
        for p in range(PLANES):
            inverse = w_ref[p, r]
            factor = lw_ref[p, r]
            for c in range(COMPS):
                right = rhs[c * PLANES + p, r] + field_steps[c * PLANES + p, r]
                value = right * inverse + factor * carry[p * COMPS + c]
                ybuf[c * PLANES + p, r] = value
                out.append(value)
        return tuple(out)

    ends = lax.fori_loop(0, STEPS, forward, (zero,) * (PLANES * COMPS), unroll=8)
    carries = []
    for p in range(PLANES):
        for c in range(COMPS):
            carries.append(down(scan(ends[p * COMPS + c], alphas[p], down), 1))

    def backward(i, carry):
        r = STEPS - 1 - i
        out = []
        for p in range(PLANES):
            ratio = c_ref[p, r]
            prefix_product = a_ref[p, r]
            for c in range(COMPS):
                j = p * COMPS + c
                value = ybuf[c * PLANES + p, r] + prefix_product * carries[j] + ratio * carry[j]
                ybuf[c * PLANES + p, r] = value
                out.append(value)
        return tuple(out)

    starts = lax.fori_loop(0, STEPS, backward, (zero,) * (PLANES * COMPS), unroll=8)
    tails = []
    for p in range(PLANES):
        for c in range(COMPS):
            j = p * COMPS + c
            whole = scan(starts[j], betas[p], up)
            tails.append(up(whole, 1))
            bd[wall, 0, c, p : p + 1, :] = whole[0:1]
            bd[wall, 1, c, p : p + 1, :] = ybuf[c * PLANES + p, STEPS - 1][CHUNKS - 1 :]
    boundaries = to_walls(bd, (bd_send, bd_recv))
    outs.append(pltpu.make_async_copy(ybuf, part_hbm, out_sem.at[3]))
    outs[-1].start()
    from_walls(cf, (cf_send, cf_recv))
    betas_in = [jnp.zeros((PLANES, LANES), jnp.float32)]
    divisors, slopes = [], []
    for d in range(WALL):
        g0, h0, g1, h1 = (cf[d, q] for q in range(4))
        divisor = 1.0 / (1.0 - g0 * betas_in[d])
        slope = h0 * divisor
        divisors.append(divisor)
        slopes.append(slope)
        betas_in.append(g1 * betas_in[d] * slope + h1)
    from_walls(bd, (bd_send, bd_recv))
    for c in range(COMPS):
        alpha_in = [jnp.zeros((PLANES, LANES), jnp.float32)]
        heads = []
        for d in range(WALL):
            head = (bd[d, 0, c] + cf[d, 0] * alpha_in[d]) * divisors[d]
            heads.append(head)
            alpha_in.append(bd[d, 1, c] + cf[d, 2] * (alpha_in[d] + betas_in[d] * head))
        upper_value = jnp.zeros((PLANES, LANES), jnp.float32)
        x_low = upper_value
        x_high = upper_value
        for d in reversed(range(WALL)):
            x_high = jnp.where(wall == d, upper_value, x_high)
            upper_value = heads[d] + slopes[d] * upper_value
            x_low = jnp.where(wall == d, alpha_in[d] + betas_in[d] * upper_value, x_low)
        xlu[0, c] = x_low
        xlu[1, c] = x_high

    for p in range(PLANES):
        for c in range(COMPS):
            q = c * PLANES + p
            ends_ref[0, q] = tails[p * COMPS + c] + hc_ref[p] * xlu[1, c, p : p + 1, :]
            ends_ref[1, q] = jnp.broadcast_to(xlu[0, c, p : p + 1, :], (CHUNKS, LANES))
    outs.append(pltpu.make_async_copy(ends_ref, ends_hbm, out_sem.at[4]))
    outs[-1].start()
    for copy in sends:
        copy.wait_send()
    for copy in edges + coefficients + boundaries:
        copy.wait_send()
    for copy in outs:
        copy.wait()


def finish(
    part_hbm,
    b_hbm,
    g_hbm,
    ends_hbm,
    field_hbm,
    next_hbm,
    dep_hbm,
    part,
    b_ref,
    g_ref,
    ends,
    field,
    dep,
    sems,
    part_sem,
    field_sem,
    out_sem,
    dep_sem,
):
    small = [
        pltpu.make_async_copy(source, target, sems.at[q])
        for q, (source, target) in enumerate(((b_hbm, b_ref), (g_hbm, g_ref), (ends_hbm, ends)))
    ]
    groups = [pl.ds(c * PLANES, PLANES) for c in range(COMPS)]
    parts = [
        pltpu.make_async_copy(part_hbm.at[groups[c]], part.at[groups[c]], part_sem.at[c])
        for c in range(COMPS)
    ]
    fields = []
    for j in range(CHUNKS):
        fields.append(
            pltpu.make_async_copy(
                field_hbm.at[:, :, j, :],
                field.at[:, pl.ds(j * STEPS, STEPS), :],
                field_sem.at[j],
            )
        )
    for copy in small[:2] + parts[:1] + small[2:] + parts[1:] + fields:
        copy.start()
    for copy in small:
        copy.wait()
    outs = []
    for c in range(COMPS):
        parts[c].wait()
        highs = [ends[0, c * PLANES + p] for p in range(PLANES)]
        lows = [ends[1, c * PLANES + p] for p in range(PLANES)]

        def correct(r, carry, c=c, highs=highs, lows=lows):
            for p in range(PLANES):
                q = c * PLANES + p
                part[q, r] = part[q, r] + b_ref[p, r] * highs[p] + g_ref[p, r] * lows[p]
            return carry

        lax.fori_loop(0, STEPS, correct, 0, unroll=8)
        for j in range(CHUNKS):
            copy = pltpu.make_async_copy(
                part.at[groups[c], :, j, :],
                next_hbm.at[groups[c], pl.ds(j * STEPS, STEPS), :],
                out_sem.at[c * CHUNKS + j],
            )
            copy.start()
            outs.append(copy)
    for copy in fields:
        copy.wait()
    for c in range(COMPS):

        def narrow(p, carry, c=c):
            dep[c * PLANES + p] = field[c * PLANES + p].astype(jnp.bfloat16)
            return carry

        lax.fori_loop(0, PLANES, narrow, 0)
        copy = pltpu.make_async_copy(dep.at[groups[c]], dep_hbm.at[groups[c]], dep_sem.at[c])
        copy.start()
        outs.append(copy)
    for copy in outs:
        copy.wait()


def local(velocity, lower_weight, upper_weight, forces, cells, counts):
    f32 = jnp.float32
    flat = (COMPS * PLANES, ROWS, LANES)
    steps = (PLANES, STEPS, CHUNKS, LANES)
    all_steps = (COMPS * PLANES, STEPS, CHUNKS, LANES)
    dma = pltpu.SemaphoreType.DMA
    any_space = pl.BlockSpec(memory_space=pl.ANY)
    ends = (2, COMPS * PLANES, CHUNKS, LANES)
    solved = pl.pallas_call(
        kernel,
        name="substep",
        out_shape=(
            jax.ShapeDtypeStruct(all_steps, f32),
            jax.ShapeDtypeStruct(steps, f32),
            jax.ShapeDtypeStruct(steps, f32),
            jax.ShapeDtypeStruct(ends, f32),
            jax.ShapeDtypeStruct(flat, f32),
        ),
        in_specs=[any_space] * 6,
        out_specs=(any_space,) * 5,
        scratch_shapes=[
            pltpu.VMEM((COMPS, SPAN, PLANES, SLOTS), f32),
            pltpu.VMEM((SPAN, PLANES, SLOTS), jnp.int32),
            pltpu.SMEM((PLANES, SPAN), jnp.int32),
            pltpu.VMEM(all_steps, f32),
            pltpu.VMEM(steps, f32),
            pltpu.VMEM(steps, f32),
            pltpu.VMEM(all_steps, f32),
            pltpu.VMEM(flat, f32),
            pltpu.VMEM(all_steps, f32),
            pltpu.VMEM(steps, f32),
            pltpu.VMEM(steps, f32),
            pltpu.VMEM(steps, f32),
            pltpu.VMEM(steps, f32),
            pltpu.VMEM(steps, f32),
            pltpu.VMEM(steps, f32),
            pltpu.VMEM((PLANES, CHUNKS, LANES), f32),
            pltpu.VMEM(ends, f32),
            pltpu.VMEM((2, SPAN, PLANES, SLOTS), jnp.int32),
            pltpu.VMEM((2, GROUP, 3, COMPS, PLANES, SLOTS), f32),
            pltpu.VMEM((LANES, ROWS), f32),
            pltpu.VMEM((2, ROWS, LANES), f32),
            pltpu.VMEM((2, 16, ROWS), f32),
            pltpu.VMEM((2, 16, ROWS), f32),
            pltpu.VMEM((WALL, 4, PLANES, LANES), f32),
            pltpu.VMEM((WALL, 2, COMPS, PLANES, LANES), f32),
            pltpu.VMEM((2, COMPS, PLANES, LANES), f32),
            dma((SPAN,)),
            dma((SPAN,)),
            dma((2,)),
            dma((2,)),
            dma((WALL,)),
            dma((WALL,)),
            dma((WALL,)),
            dma((WALL,)),
            dma((32,)),
            dma((5,)),
        ],
        compiler_params=pltpu.CompilerParams(collective_id=0, has_side_effects=True),
    )(
        velocity.reshape(flat),
        lower_weight,
        upper_weight,
        forces,
        cells,
        jnp.swapaxes(counts, 2, 3),
    )
    velocity_next, deposit = pl.pallas_call(
        finish,
        name="finish",
        out_shape=(jax.ShapeDtypeStruct(flat, f32), jax.ShapeDtypeStruct(flat, jnp.bfloat16)),
        in_specs=[any_space] * 5,
        out_specs=(any_space,) * 2,
        scratch_shapes=[
            pltpu.VMEM(all_steps, f32),
            pltpu.VMEM(steps, f32),
            pltpu.VMEM(steps, f32),
            pltpu.VMEM(ends, f32),
            pltpu.VMEM(flat, f32),
            pltpu.VMEM(flat, jnp.bfloat16),
            dma((3,)),
            dma((COMPS,)),
            dma((CHUNKS,)),
            dma((COMPS * CHUNKS,)),
            dma((COMPS,)),
        ],
    )(*solved[:4], solved[4].reshape(all_steps))
    return velocity_next.reshape(velocity.shape), deposit.reshape(velocity.shape)


def solution(mesh):
    placed = (
        P(None, None, "wall", "span"),
        P(None, "wall", "span"),
        P(None, "wall", "span"),
        P(None, "wall", "span", None, None, None),
        P("wall", "span", None, None, None),
        P("wall", "span", None, None),
    )
    return jax.shard_map(
        local,
        mesh=mesh,
        in_specs=placed,
        out_specs=(P(None, None, "wall", "span"), P(None, None, "wall", "span")),
        check_vma=False,
    )
```

```python
import functools

import jax
import jax.numpy as jnp
from jax import lax
from jax.experimental import pallas as pl
from jax.experimental.pallas import tpu as pltpu
from jax.sharding import PartitionSpec as P

MESH = pl.DeviceIdType.MESH
diffusion_number = 0.2
SPAN = 32
WALL = 4
PLANES = 4
COMPS = 3
ROWS = 256
LANES = 128
SLOTS = 768
CHUNKS = 8
STEPS = ROWS // CHUNKS
GROUP = 4
TURNS = SPAN // GROUP


def kernel(
    vel_hbm,
    low_hbm,
    upp_hbm,
    forces_hbm,
    cells_hbm,
    counts_hbm,
    part_hbm,
    b_hbm,
    g_hbm,
    ends_hbm,
    field_hbm,
    recv,
    cells,
    counts,
    vel,
    low,
    upp,
    rhs,
    field,
    ybuf,
    w_ref,
    lw_ref,
    c_ref,
    a_ref,
    b_ref,
    g_ref,
    hc_ref,
    ends_ref,
    spots,
    quant,
    pack,
    cols,
    hsend,
    hrecv,
    cf,
    bd,
    xlu,
    send_sem,
    recv_sem,
    halo_send,
    halo_recv,
    cf_send,
    cf_recv,
    bd_send,
    bd_recv,
    load_sem,
    out_sem,
):
    wall = lax.axis_index("wall")
    me = lax.axis_index("span")
    px, py, pc = lax.div(me, 8), lax.rem(lax.div(me, 2), 4), lax.rem(me, 2)

    def peers(i, sign):
        if isinstance(i, int):
            half, high = i % 2 + 2 * (i // 4), i // 2 % 2
            turned = 3 * half % 4
        else:
            half, high = lax.rem(i, 2) + 2 * lax.div(i, 4), lax.rem(lax.div(i, 2), 2)
            turned = lax.rem(3 * half, 4)
        out = []
        for low in range(2):
            x = lax.rem(px + 4 + sign * (turned if low else half), 4)
            y = lax.rem(py + 4 + sign * (low + 2 * high), 4)
            for core in range(2):
                out.append(x * 8 + y * 2 + lax.rem(pc + core, 2))
        return out

    everyone = sum((peers(i, 1) for i in range(TURNS)), [])

    low_flat = low.reshape(PLANES * ROWS, LANES)
    upp_flat = upp.reshape(PLANES * ROWS, LANES)
    w_flat = w_ref.reshape(PLANES * ROWS, LANES)
    lw_flat = lw_ref.reshape(PLANES * ROWS, LANES)
    c_flat = c_ref.reshape(PLANES * ROWS, LANES)
    loads = [
        pltpu.make_async_copy(counts_hbm.at[0, 0], counts, load_sem.at[0]),
        pltpu.make_async_copy(cells_hbm.at[0, 0], cells, load_sem.at[1]),
        pltpu.make_async_copy(forces_hbm.at[:, 0, 0, me], recv.at[:, 0], load_sem.at[2]),
    ]
    vel_loads = []
    for j in range(CHUNKS):
        rows = pl.ds(j * STEPS, STEPS)
        vel_loads.append(
            pltpu.make_async_copy(
                vel_hbm.at[:, rows, :], vel.at[:, :, j, :], load_sem.at[8 + j]
            )
        )
        for q, (source, target) in enumerate(((low_hbm, low), (upp_hbm, upp))):
            loads.append(
                pltpu.make_async_copy(
                    source.at[:, rows, :], target.at[:, :, j, :], load_sem.at[16 + 8 * q + j]
                )
            )
    for copy in vel_loads:
        copy.start()
    for copy in loads:
        copy.start()

    barrier = pltpu.get_barrier_semaphore()
    for k in range(1, SPAN):
        pl.semaphore_signal(barrier, inc=1, device_id={"span": everyone[k]}, device_id_type=MESH)
    for j in range(1, WALL):
        pl.semaphore_signal(
            barrier, inc=1, device_id={"wall": (wall + j) % WALL}, device_id_type=MESH
        )
    pl.semaphore_wait(barrier, SPAN - 1 + WALL - 1)

    def block_copy(k, target):
        return pltpu.make_async_remote_copy(
            src_ref=forces_hbm.at[:, 0, 0, target],
            dst_ref=recv.at[:, k],
            send_sem=send_sem.at[k],
            recv_sem=recv_sem.at[k],
            device_id={"span": target},
            device_id_type=MESH,
        )

    for k in range(1, 2 * GROUP):
        block_copy(k, everyone[k]).start()

    for copy in vel_loads:
        copy.wait()
    lane = lax.broadcasted_iota(jnp.int32, (ROWS, LANES), 1)
    edges = []
    for side, column in ((0, 0), (1, LANES - 1)):
        packed = jnp.zeros((ROWS, LANES), jnp.float32)
        for i in range(COMPS * PLANES):
            block = vel[i].reshape(ROWS, LANES)
            packed = jnp.where(lane == i, pltpu.roll(block, (i - column) % LANES, 1), packed)
        hsend[side] = jnp.transpose(packed)[0:16]
        target = (me + SPAN - 1) % SPAN if side == 0 else (me + 1) % SPAN
        copy = pltpu.make_async_remote_copy(
            src_ref=hsend.at[side],
            dst_ref=hrecv.at[side],
            send_sem=halo_send.at[side],
            recv_sem=halo_recv.at[side],
            device_id={"span": target},
            device_id_type=MESH,
        )
        copy.start()
        edges.append(copy)

    field[...] = jnp.zeros_like(field)
    cols[...] = jnp.zeros_like(cols)
    pack[...] = jnp.zeros_like(pack)
    for copy in loads:
        copy.wait()

    slot = lax.broadcasted_iota(jnp.int32, (PLANES, SLOTS), 1)
    plane = lax.broadcasted_iota(jnp.int32, (PLANES, SLOTS), 0)

    def locate(s, carry):
        cell = cells[s]
        limit = jnp.where(plane < 1, counts[0, s], counts[1, s])
        limit = jnp.where(plane < 2, limit, jnp.where(plane < 3, counts[2, s], counts[3, s]))
        row = ((cell >> 7) & 31) * CHUNKS + (cell >> 12)
        spots[0, s] = jnp.where(slot < limit, row & 127, -1)
        spots[1, s] = (((row >> 7) << 7) + (cell & 127) - 128)
        return carry

    lax.fori_loop(0, SPAN, locate, 0, unroll=2)

    float8 = jnp.float8_e4m3fn
    one8, zero8 = jnp.ones((), float8), jnp.zeros((), float8)
    io_m = lax.broadcasted_iota(jnp.int32, (LANES, 256), 0).astype(jnp.int8)
    io_n = (lax.broadcasted_iota(jnp.int32, (256, 256), 0) - 128).astype(jnp.int8)
    last = lax.broadcasted_iota(jnp.int32, (CHUNKS, LANES), 1) == LANES - 1
    first = lax.broadcasted_iota(jnp.int32, (CHUNKS, LANES), 1) == 0

    def arrive(i):
        for j in range(GROUP):
            block_copy(GROUP * i + j, me).wait_recv()

    def quantize(i, buffer):
        blocks = [[recv[c, GROUP * i + j] for c in range(COMPS)] for j in range(GROUP)]
        top = None
        for block in sum(blocks, []):
            top = jnp.abs(block) if top is None else jnp.maximum(top, jnp.abs(block))
        top = jnp.maximum(jnp.max(top, axis=(0, 1), keepdims=True), 1e-30)
        scale = 384.0 / top
        for j in range(GROUP):
            for c in range(COMPS):
                rest = blocks[j][c] * scale
                for t in range(3):
                    term = rest.astype(float8).astype(jnp.float32)
                    quant[buffer, j, t, c] = term
                    rest = rest - term
        return top * (1.0 / 384.0)

    def deposit(i, carry):
        through, unit = carry

        @pl.when(i < TURNS - 2)
        def _():
            for j, target in enumerate(peers(i + 2, 1)):
                block_copy(GROUP * (i + 2) + j, target).start()

        @pl.when(i < TURNS - 1)
        def _():
            arrive(i + 1)

        @pl.when(i == 1)
        def _():
            for side in range(2):
                edges[side].wait_recv()
                pack[0:16] = hrecv[side]
                cols[side] = jnp.transpose(pack[...])

        buffer = lax.rem(i, 2)
        sources = peers(i, -1)
        for p in range(PLANES):
            total = None
            for j in range(GROUP):
                m = spots[0, sources[j], p : p + 1, :].astype(jnp.int8)
                n = spots[1, sources[j], p : p + 1, :].astype(jnp.int8)
                values = [
                    [quant[buffer, j, t, c, p : p + 1, :].astype(float8) for c in range(COMPS)]
                    for t in range(3)
                ]
                for start in range(0, SLOTS, 256):
                    part = slice(start, start + 256)
                    hot_m = m[:, part] == io_m
                    hot_n = jnp.where(n[:, part] == io_n, one8, zero8)
                    for t in range(3):
                        weighted = jnp.concatenate(
                            [jnp.where(hot_m, values[t][c][:, part], zero8) for c in range(COMPS)],
                            axis=0,
                        )
                        term = lax.dot_general(
                            weighted,
                            hot_n,
                            (((1,), (1,)), ((), ())),
                            preferred_element_type=jnp.float32,
                        )
                        total = term if total is None else total + term
            total = total.reshape(COMPS, LANES, 256) * unit
            for c in range(COMPS):
                field[c * PLANES + p, 0:128, :] += total[c, :, 0:128]
                field[c * PLANES + p, 128:256, :] += total[c, :, 128:256]
        for row in range(ROWS // TURNS):
            index = pl.ds(row * CHUNKS + i, PLANES, stride=ROWS)
            lower = low_flat[index, :]
            upper = upp_flat[index, :]
            gain = 1.0 + lower * through
            inverse = 1.0 / (gain + upper)
            w_flat[index, :] = inverse
            lw_flat[index, :] = lower * inverse
            c_flat[index, :] = upper * inverse
            through = gain * inverse
        for step in range(5):
            r = jnp.clip(5 * (i - 1) + step, 0, STEPS - 1)
            edge = pl.ds(pl.multiple_of(r * CHUNKS, CHUNKS), CHUNKS)
            columns = [cols[side, edge, :] for side in range(2)]
            for c in range(COMPS):
                planes = [vel[c * PLANES + p, r] for p in range(PLANES)]
                for p in range(PLANES):
                    q = c * PLANES + p
                    here = planes[p]
                    above = jnp.where(
                        last,
                        pltpu.roll(columns[0], LANES - 1 - q, 1),
                        pltpu.roll(here, LANES - 1, 1),
                    )
                    below = jnp.where(
                        first, pltpu.roll(columns[1], (LANES - q) % LANES, 1), pltpu.roll(here, 1, 1)
                    )
                    stream = planes[(p + 1) % PLANES] + planes[(p + PLANES - 1) % PLANES]
                    rhs[q, r] = (
                        here
                        + diffusion_number * (stream - 2.0 * here)
                        + diffusion_number * (above + below - 2.0 * here)
                    )
        unit = quantize(jnp.minimum(i + 1, TURNS - 1), 1 - buffer)
        return through, unit

    for k in range(1, GROUP):
        block_copy(k, me).wait_recv()
    unit = quantize(0, 0)
    lax.fori_loop(0, TURNS, deposit, (jnp.ones((PLANES, LANES), jnp.float32), unit))

    field_steps = field.reshape(COMPS * PLANES, STEPS, CHUNKS, LANES)
    outs = [pltpu.make_async_copy(field, field_hbm, out_sem.at[0])]
    outs[0].start()

    sub = lax.broadcasted_iota(jnp.int32, (CHUNKS, LANES), 0)

    def down(x, d):
        return jnp.where(sub >= d, pltpu.roll(x, d, 0), 0.0)

    def up(x, d):
        return jnp.where(sub < CHUNKS - d, pltpu.roll(x, CHUNKS - d, 0), 0.0)

    def levels(x, shift):
        out = [x]
        for d in (1, 2):
            out.append(out[-1] * shift(out[-1], d))
        return out

    def scan(x, factors, shift):
        for d, factor in zip((1, 2, 4), factors):
            x = x + factor * shift(x, d)
        return x

    def prefix(r, carry):
        out = []
        for p in range(PLANES):
            value = carry[p] * lw_ref[p, r]
            a_ref[p, r] = value
            out.append(value)
        return tuple(out)

    one = jnp.ones((CHUNKS, LANES), jnp.float32)
    alpha = lax.fori_loop(0, STEPS, prefix, (one,) * PLANES, unroll=4)
    alphas = [levels(x, down) for x in alpha]
    through_low = []
    for p in range(PLANES):
        ends = scan(jnp.where(sub == 0, alpha[p], 0.0), alphas[p], down)
        through_low.append(jnp.where(sub == 0, 1.0, pltpu.roll(ends, 1, 0)))

    def suffix(i, carry):
        r = STEPS - 1 - i
        out = []
        for p in range(PLANES):
            ratio = c_ref[p, r]
            b = carry[p] * ratio
            g = a_ref[p, r] * through_low[p] + ratio * carry[PLANES + p]
            b_ref[p, r] = b
            g_ref[p, r] = g
            out.append((b, g))
        return tuple(x[0] for x in out) + tuple(x[1] for x in out)

    zero = jnp.zeros((CHUNKS, LANES), jnp.float32)
    done = lax.fori_loop(0, STEPS, suffix, (one,) * PLANES + (zero,) * PLANES, unroll=4)
    beta, g_first = done[:PLANES], done[PLANES:]
    betas = [levels(x, up) for x in beta]
    g_carry = []
    for p in range(PLANES):
        g_all = scan(g_first[p], betas[p], up)
        g_carry.append(up(g_all, 1))
        h_all = scan(jnp.where(sub == CHUNKS - 1, beta[p], 0.0), betas[p], up)
        h_carry = jnp.where(sub == CHUNKS - 1, 1.0, pltpu.roll(h_all, CHUNKS - 1, 0))
        hc_ref[p] = h_carry
        cf[wall, 0, p : p + 1, :] = g_all[0:1]
        cf[wall, 1, p : p + 1, :] = h_all[0:1]
        last_g = g_ref[p, STEPS - 1] + b_ref[p, STEPS - 1] * g_carry[p]
        cf[wall, 2, p : p + 1, :] = last_g[CHUNKS - 1 :]
        last_h = b_ref[p, STEPS - 1] * h_carry
        cf[wall, 3, p : p + 1, :] = last_h[CHUNKS - 1 :]

    def to_walls(ref, sems):
        copies = []
        for j in range(1, WALL):
            copy = pltpu.make_async_remote_copy(
                src_ref=ref.at[wall],
                dst_ref=ref.at[wall],
                send_sem=sems[0].at[j],
                recv_sem=sems[1].at[j],
                device_id={"wall": (wall + j) % WALL},
                device_id_type=MESH,
            )
            copy.start()
            copies.append(copy)
        return copies

    def from_walls(ref, sems):
        for j in range(1, WALL):
            pltpu.make_async_remote_copy(
                src_ref=ref.at[wall],
                dst_ref=ref.at[(wall + WALL - j) % WALL],
                send_sem=sems[0].at[j],
                recv_sem=sems[1].at[j],
                device_id={"wall": (wall + j) % WALL},
                device_id_type=MESH,
            ).wait_recv()

    coefficients = to_walls(cf, (cf_send, cf_recv))

    def full_g(r, carry):
        for p in range(PLANES):
            g_ref[p, r] = g_ref[p, r] + b_ref[p, r] * g_carry[p]
        return carry

    lax.fori_loop(0, STEPS, full_g, 0, unroll=4)
    for q, (source, target) in enumerate(((b_ref, b_hbm), (g_ref, g_hbm))):
        outs.append(pltpu.make_async_copy(source, target, out_sem.at[1 + q]))
        outs[-1].start()

    def forward(r, carry):
        out = []
        for p in range(PLANES):
            inverse = w_ref[p, r]
            factor = lw_ref[p, r]
            for c in range(COMPS):
                right = rhs[c * PLANES + p, r] + field_steps[c * PLANES + p, r]
                value = right * inverse + factor * carry[p * COMPS + c]
                ybuf[c * PLANES + p, r] = value
                out.append(value)
        return tuple(out)

    ends = lax.fori_loop(0, STEPS, forward, (zero,) * (PLANES * COMPS), unroll=8)
    carries = []
    for p in range(PLANES):
        for c in range(COMPS):
            carries.append(down(scan(ends[p * COMPS + c], alphas[p], down), 1))

    def backward(i, carry):
        r = STEPS - 1 - i
        out = []
        for p in range(PLANES):
            ratio = c_ref[p, r]
            prefix_product = a_ref[p, r]
            for c in range(COMPS):
                j = p * COMPS + c
                value = ybuf[c * PLANES + p, r] + prefix_product * carries[j] + ratio * carry[j]
                ybuf[c * PLANES + p, r] = value
                out.append(value)
        return tuple(out)

    starts = lax.fori_loop(0, STEPS, backward, (zero,) * (PLANES * COMPS), unroll=8)
    tails = []
    for p in range(PLANES):
        for c in range(COMPS):
            j = p * COMPS + c
            whole = scan(starts[j], betas[p], up)
            tails.append(up(whole, 1))
            bd[wall, 0, c, p : p + 1, :] = whole[0:1]
            bd[wall, 1, c, p : p + 1, :] = ybuf[c * PLANES + p, STEPS - 1][CHUNKS - 1 :]
    boundaries = to_walls(bd, (bd_send, bd_recv))
    outs.append(pltpu.make_async_copy(ybuf, part_hbm, out_sem.at[3]))
    outs[-1].start()
    from_walls(cf, (cf_send, cf_recv))
    betas_in = [jnp.zeros((PLANES, LANES), jnp.float32)]
    divisors, slopes = [], []
    for d in range(WALL):
        g0, h0, g1, h1 = (cf[d, q] for q in range(4))
        divisor = 1.0 / (1.0 - g0 * betas_in[d])
        slope = h0 * divisor
        divisors.append(divisor)
        slopes.append(slope)
        betas_in.append(g1 * betas_in[d] * slope + h1)
    from_walls(bd, (bd_send, bd_recv))
    for c in range(COMPS):
        alpha_in = [jnp.zeros((PLANES, LANES), jnp.float32)]
        heads = []
        for d in range(WALL):
            head = (bd[d, 0, c] + cf[d, 0] * alpha_in[d]) * divisors[d]
            heads.append(head)
            alpha_in.append(bd[d, 1, c] + cf[d, 2] * (alpha_in[d] + betas_in[d] * head))
        upper_value = jnp.zeros((PLANES, LANES), jnp.float32)
        x_low = upper_value
        x_high = upper_value
        for d in reversed(range(WALL)):
            x_high = jnp.where(wall == d, upper_value, x_high)
            upper_value = heads[d] + slopes[d] * upper_value
            x_low = jnp.where(wall == d, alpha_in[d] + betas_in[d] * upper_value, x_low)
        xlu[0, c] = x_low
        xlu[1, c] = x_high

    for p in range(PLANES):
        for c in range(COMPS):
            q = c * PLANES + p
            ends_ref[0, q] = tails[p * COMPS + c] + hc_ref[p] * xlu[1, c, p : p + 1, :]
            ends_ref[1, q] = jnp.broadcast_to(xlu[0, c, p : p + 1, :], (CHUNKS, LANES))
    outs.append(pltpu.make_async_copy(ends_ref, ends_hbm, out_sem.at[4]))
    outs[-1].start()
    for k in range(1, SPAN):
        block_copy(k, everyone[k]).wait_send()
    for copy in edges + coefficients + boundaries:
        copy.wait_send()
    for copy in outs:
        copy.wait()


def finish(
    part_hbm,
    b_hbm,
    g_hbm,
    ends_hbm,
    field_hbm,
    next_hbm,
    dep_hbm,
    part,
    b_ref,
    g_ref,
    ends,
    field,
    dep,
    sems,
    part_sem,
    field_sem,
    out_sem,
    dep_sem,
):
    small = [
        pltpu.make_async_copy(source, target, sems.at[q])
        for q, (source, target) in enumerate(((b_hbm, b_ref), (g_hbm, g_ref), (ends_hbm, ends)))
    ]
    groups = [pl.ds(c * PLANES, PLANES) for c in range(COMPS)]
    parts = [
        pltpu.make_async_copy(part_hbm.at[groups[c]], part.at[groups[c]], part_sem.at[c])
        for c in range(COMPS)
    ]
    fields = []
    for j in range(CHUNKS):
        fields.append(
            pltpu.make_async_copy(
                field_hbm.at[:, :, j, :],
                field.at[:, pl.ds(j * STEPS, STEPS), :],
                field_sem.at[j],
            )
        )
    for copy in small[:2] + parts[:1] + small[2:] + parts[1:] + fields:
        copy.start()
    for copy in small:
        copy.wait()
    outs = []
    for c in range(COMPS):
        parts[c].wait()
        highs = [ends[0, c * PLANES + p] for p in range(PLANES)]
        lows = [ends[1, c * PLANES + p] for p in range(PLANES)]

        def correct(r, carry, c=c, highs=highs, lows=lows):
            for p in range(PLANES):
                q = c * PLANES + p
                part[q, r] = part[q, r] + b_ref[p, r] * highs[p] + g_ref[p, r] * lows[p]
            return carry

        lax.fori_loop(0, STEPS, correct, 0, unroll=8)
        for j in range(CHUNKS):
            copy = pltpu.make_async_copy(
                part.at[groups[c], :, j, :],
                next_hbm.at[groups[c], pl.ds(j * STEPS, STEPS), :],
                out_sem.at[c * CHUNKS + j],
            )
            copy.start()
            outs.append(copy)
    for copy in fields:
        copy.wait()
    for c in range(COMPS):

        def narrow(p, carry, c=c):
            dep[c * PLANES + p] = field[c * PLANES + p].astype(jnp.bfloat16)
            return carry

        lax.fori_loop(0, PLANES, narrow, 0)
        copy = pltpu.make_async_copy(dep.at[groups[c]], dep_hbm.at[groups[c]], dep_sem.at[c])
        copy.start()
        outs.append(copy)
    for copy in outs:
        copy.wait()


def local(velocity, lower_weight, upper_weight, forces, cells, counts):
    f32 = jnp.float32
    flat = (COMPS * PLANES, ROWS, LANES)
    steps = (PLANES, STEPS, CHUNKS, LANES)
    all_steps = (COMPS * PLANES, STEPS, CHUNKS, LANES)
    dma = pltpu.SemaphoreType.DMA
    any_space = pl.BlockSpec(memory_space=pl.ANY)
    ends = (2, COMPS * PLANES, CHUNKS, LANES)
    solved = pl.pallas_call(
        kernel,
        name="substep",
        out_shape=(
            jax.ShapeDtypeStruct(all_steps, f32),
            jax.ShapeDtypeStruct(steps, f32),
            jax.ShapeDtypeStruct(steps, f32),
            jax.ShapeDtypeStruct(ends, f32),
            jax.ShapeDtypeStruct(flat, f32),
        ),
        in_specs=[any_space] * 6,
        out_specs=(any_space,) * 5,
        scratch_shapes=[
            pltpu.VMEM((COMPS, SPAN, PLANES, SLOTS), f32),
            pltpu.VMEM((SPAN, PLANES, SLOTS), jnp.int32),
            pltpu.SMEM((PLANES, SPAN), jnp.int32),
            pltpu.VMEM(all_steps, f32),
            pltpu.VMEM(steps, f32),
            pltpu.VMEM(steps, f32),
            pltpu.VMEM(all_steps, f32),
            pltpu.VMEM(flat, f32),
            pltpu.VMEM(all_steps, f32),
            pltpu.VMEM(steps, f32),
            pltpu.VMEM(steps, f32),
            pltpu.VMEM(steps, f32),
            pltpu.VMEM(steps, f32),
            pltpu.VMEM(steps, f32),
            pltpu.VMEM(steps, f32),
            pltpu.VMEM((PLANES, CHUNKS, LANES), f32),
            pltpu.VMEM(ends, f32),
            pltpu.VMEM((2, SPAN, PLANES, SLOTS), jnp.int32),
            pltpu.VMEM((2, GROUP, 3, COMPS, PLANES, SLOTS), f32),
            pltpu.VMEM((LANES, ROWS), f32),
            pltpu.VMEM((2, ROWS, LANES), f32),
            pltpu.VMEM((2, 16, ROWS), f32),
            pltpu.VMEM((2, 16, ROWS), f32),
            pltpu.VMEM((WALL, 4, PLANES, LANES), f32),
            pltpu.VMEM((WALL, 2, COMPS, PLANES, LANES), f32),
            pltpu.VMEM((2, COMPS, PLANES, LANES), f32),
            dma((SPAN,)),
            dma((SPAN,)),
            dma((2,)),
            dma((2,)),
            dma((WALL,)),
            dma((WALL,)),
            dma((WALL,)),
            dma((WALL,)),
            dma((32,)),
            dma((5,)),
        ],
        compiler_params=pltpu.CompilerParams(
            collective_id=0,
            has_side_effects=True,
        ),
    )(
        velocity.reshape(flat),
        lower_weight,
        upper_weight,
        forces,
        cells,
        jnp.swapaxes(counts, 2, 3),
    )
    velocity_next, deposit = pl.pallas_call(
        finish,
        name="finish",
        out_shape=(jax.ShapeDtypeStruct(flat, f32), jax.ShapeDtypeStruct(flat, jnp.bfloat16)),
        in_specs=[any_space] * 5,
        out_specs=(any_space,) * 2,
        scratch_shapes=[
            pltpu.VMEM(all_steps, f32),
            pltpu.VMEM(steps, f32),
            pltpu.VMEM(steps, f32),
            pltpu.VMEM(ends, f32),
            pltpu.VMEM(flat, f32),
            pltpu.VMEM(flat, jnp.bfloat16),
            dma((3,)),
            dma((COMPS,)),
            dma((CHUNKS,)),
            dma((COMPS * CHUNKS,)),
            dma((COMPS,)),
        ],
    )(*solved[:4], solved[4].reshape(all_steps))
    return velocity_next.reshape(velocity.shape), deposit.reshape(velocity.shape)


def solution(mesh):
    placed = (
        P(None, None, "wall", "span"),
        P(None, "wall", "span"),
        P(None, "wall", "span"),
        P(None, "wall", "span", None, None, None),
        P("wall", "span", None, None, None),
        P("wall", "span", None, None),
    )
    return jax.shard_map(
        local,
        mesh=mesh,
        in_specs=placed,
        out_specs=(P(None, None, "wall", "span"), P(None, None, "wall", "span")),
        check_vma=False,
    )
```

```python
import functools

import jax
import jax.numpy as jnp
from jax import lax
from jax.experimental import pallas as pl
from jax.experimental.pallas import tpu as pltpu
from jax.sharding import PartitionSpec as P

MESH = pl.DeviceIdType.MESH
diffusion_number = 0.2
SPAN = 32
WALL = 4
PLANES = 4
COMPS = 3
ROWS = 256
LANES = 128
SLOTS = 768
CHUNKS = 8
STEPS = ROWS // CHUNKS
GROUP = 4
TURNS = SPAN // GROUP
AHEAD = 4


def kernel(
    vel_hbm,
    low_hbm,
    upp_hbm,
    forces_hbm,
    cells_hbm,
    counts_hbm,
    part_hbm,
    b_hbm,
    g_hbm,
    ends_hbm,
    field_hbm,
    recv,
    cells,
    counts,
    vel,
    low,
    upp,
    rhs,
    field,
    ybuf,
    w_ref,
    lw_ref,
    c_ref,
    a_ref,
    b_ref,
    g_ref,
    hc_ref,
    ends_ref,
    spots,
    quant,
    pack,
    cols,
    hsend,
    hrecv,
    cf,
    bd,
    xlu,
    send_sem,
    recv_sem,
    halo_send,
    halo_recv,
    cf_send,
    cf_recv,
    bd_send,
    bd_recv,
    load_sem,
    out_sem,
):
    wall = lax.axis_index("wall")
    me = lax.axis_index("span")
    px, py, pc = lax.div(me, 8), lax.rem(lax.div(me, 2), 4), lax.rem(me, 2)

    def peers(i, sign):
        if isinstance(i, int):
            half, high = i % 2 + 2 * (i // 4), i // 2 % 2
            turned = 3 * half % 4
        else:
            half, high = lax.rem(i, 2) + 2 * lax.div(i, 4), lax.rem(lax.div(i, 2), 2)
            turned = lax.rem(3 * half, 4)
        out = []
        for low in range(2):
            x = lax.rem(px + 4 + sign * (turned if low else half), 4)
            y = lax.rem(py + 4 + sign * (low + 2 * high), 4)
            for core in range(2):
                out.append(x * 8 + y * 2 + lax.rem(pc + core, 2))
        return out

    everyone = sum((peers(i, 1) for i in range(TURNS)), [])

    low_flat = low.reshape(PLANES * ROWS, LANES)
    upp_flat = upp.reshape(PLANES * ROWS, LANES)
    w_flat = w_ref.reshape(PLANES * ROWS, LANES)
    lw_flat = lw_ref.reshape(PLANES * ROWS, LANES)
    c_flat = c_ref.reshape(PLANES * ROWS, LANES)
    loads = [
        pltpu.make_async_copy(counts_hbm.at[0, 0], counts, load_sem.at[0]),
        pltpu.make_async_copy(cells_hbm.at[0, 0], cells, load_sem.at[1]),
        pltpu.make_async_copy(forces_hbm.at[:, 0, 0, me], recv.at[:, 0], load_sem.at[2]),
    ]
    vel_loads = []
    for j in range(CHUNKS):
        rows = pl.ds(j * STEPS, STEPS)
        vel_loads.append(
            pltpu.make_async_copy(
                vel_hbm.at[:, rows, :], vel.at[:, :, j, :], load_sem.at[8 + j]
            )
        )
        for q, (source, target) in enumerate(((low_hbm, low), (upp_hbm, upp))):
            loads.append(
                pltpu.make_async_copy(
                    source.at[:, rows, :], target.at[:, :, j, :], load_sem.at[16 + 8 * q + j]
                )
            )
    for copy in vel_loads:
        copy.start()
    for copy in loads:
        copy.start()

    barrier = pltpu.get_barrier_semaphore()
    for k in range(1, SPAN):
        pl.semaphore_signal(barrier, inc=1, device_id={"span": everyone[k]}, device_id_type=MESH)
    for j in range(1, WALL):
        pl.semaphore_signal(
            barrier, inc=1, device_id={"wall": (wall + j) % WALL}, device_id_type=MESH
        )
    pl.semaphore_wait(barrier, SPAN - 1 + WALL - 1)

    def block_copy(k, target):
        return pltpu.make_async_remote_copy(
            src_ref=forces_hbm.at[:, 0, 0, target],
            dst_ref=recv.at[:, k],
            send_sem=send_sem.at[k],
            recv_sem=recv_sem.at[k],
            device_id={"span": target},
            device_id_type=MESH,
        )

    for k in range(1, AHEAD * GROUP):
        block_copy(k, everyone[k]).start()

    for copy in vel_loads:
        copy.wait()
    lane = lax.broadcasted_iota(jnp.int32, (ROWS, LANES), 1)
    edges = []
    for side, column in ((0, 0), (1, LANES - 1)):
        packed = jnp.zeros((ROWS, LANES), jnp.float32)
        for i in range(COMPS * PLANES):
            block = vel[i].reshape(ROWS, LANES)
            packed = jnp.where(lane == i, pltpu.roll(block, (i - column) % LANES, 1), packed)
        hsend[side] = jnp.transpose(packed)[0:16]
        target = (me + SPAN - 1) % SPAN if side == 0 else (me + 1) % SPAN
        copy = pltpu.make_async_remote_copy(
            src_ref=hsend.at[side],
            dst_ref=hrecv.at[side],
            send_sem=halo_send.at[side],
            recv_sem=halo_recv.at[side],
            device_id={"span": target},
            device_id_type=MESH,
        )
        copy.start()
        edges.append(copy)

    field[...] = jnp.zeros_like(field)
    cols[...] = jnp.zeros_like(cols)
    pack[...] = jnp.zeros_like(pack)
    for copy in loads:
        copy.wait()

    slot = lax.broadcasted_iota(jnp.int32, (PLANES, SLOTS), 1)
    plane = lax.broadcasted_iota(jnp.int32, (PLANES, SLOTS), 0)

    def locate(s, carry):
        cell = cells[s]
        limit = jnp.where(plane < 1, counts[0, s], counts[1, s])
        limit = jnp.where(plane < 2, limit, jnp.where(plane < 3, counts[2, s], counts[3, s]))
        row = ((cell >> 7) & 31) * CHUNKS + (cell >> 12)
        spots[0, s] = jnp.where(slot < limit, row & 127, -1)
        spots[1, s] = (((row >> 7) << 7) + (cell & 127) - 128)
        return carry

    lax.fori_loop(0, SPAN, locate, 0, unroll=2)

    float8 = jnp.float8_e4m3fn
    one8, zero8 = jnp.ones((), float8), jnp.zeros((), float8)
    io_m = lax.broadcasted_iota(jnp.int32, (LANES, 256), 0).astype(jnp.int8)
    io_n = (lax.broadcasted_iota(jnp.int32, (256, 256), 0) - 128).astype(jnp.int8)
    last = lax.broadcasted_iota(jnp.int32, (CHUNKS, LANES), 1) == LANES - 1
    first = lax.broadcasted_iota(jnp.int32, (CHUNKS, LANES), 1) == 0

    def arrive(i):
        for j in range(GROUP):
            block_copy(GROUP * i + j, me).wait_recv()

    def quantize(i, buffer):
        blocks = [[recv[c, GROUP * i + j] for c in range(COMPS)] for j in range(GROUP)]
        top = None
        for block in sum(blocks, []):
            top = jnp.abs(block) if top is None else jnp.maximum(top, jnp.abs(block))
        top = jnp.maximum(jnp.max(top, axis=(0, 1), keepdims=True), 1e-30)
        scale = 384.0 / top
        for j in range(GROUP):
            for c in range(COMPS):
                rest = blocks[j][c] * scale
                for t in range(3):
                    term = rest.astype(float8).astype(jnp.float32)
                    quant[buffer, j, t, c] = term
                    rest = rest - term
        return top * (1.0 / 384.0)

    def deposit(i, carry):
        through, unit = carry

        @pl.when(i < TURNS - AHEAD)
        def _():
            for j, target in enumerate(peers(i + AHEAD, 1)):
                block_copy(GROUP * (i + AHEAD) + j, target).start()

        @pl.when(i < TURNS - 1)
        def _():
            arrive(i + 1)

        @pl.when(i == 1)
        def _():
            for side in range(2):
                edges[side].wait_recv()
                pack[0:16] = hrecv[side]
                cols[side] = jnp.transpose(pack[...])

        buffer = lax.rem(i, 2)
        sources = peers(i, -1)
        for p in range(PLANES):
            total = None
            for j in range(GROUP):
                m = spots[0, sources[j], p : p + 1, :].astype(jnp.int8)
                n = spots[1, sources[j], p : p + 1, :].astype(jnp.int8)
                values = [
                    [quant[buffer, j, t, c, p : p + 1, :].astype(float8) for c in range(COMPS)]
                    for t in range(3)
                ]
                for start in range(0, SLOTS, 256):
                    part = slice(start, start + 256)
                    hot_m = m[:, part] == io_m
                    hot_n = jnp.where(n[:, part] == io_n, one8, zero8)
                    for t in range(3):
                        weighted = jnp.concatenate(
                            [jnp.where(hot_m, values[t][c][:, part], zero8) for c in range(COMPS)],
                            axis=0,
                        )
                        term = lax.dot_general(
                            weighted,
                            hot_n,
                            (((1,), (1,)), ((), ())),
                            preferred_element_type=jnp.float32,
                        )
                        total = term if total is None else total + term
            total = total.reshape(COMPS, LANES, 256) * unit
            for c in range(COMPS):
                field[c * PLANES + p, 0:128, :] += total[c, :, 0:128]
                field[c * PLANES + p, 128:256, :] += total[c, :, 128:256]
        for row in range(ROWS // TURNS):
            index = pl.ds(row * CHUNKS + i, PLANES, stride=ROWS)
            lower = low_flat[index, :]
            upper = upp_flat[index, :]
            gain = 1.0 + lower * through
            inverse = 1.0 / (gain + upper)
            w_flat[index, :] = inverse
            lw_flat[index, :] = lower * inverse
            c_flat[index, :] = upper * inverse
            through = gain * inverse
        for step in range(5):
            r = jnp.clip(5 * (i - 1) + step, 0, STEPS - 1)
            edge = pl.ds(pl.multiple_of(r * CHUNKS, CHUNKS), CHUNKS)
            columns = [cols[side, edge, :] for side in range(2)]
            for c in range(COMPS):
                planes = [vel[c * PLANES + p, r] for p in range(PLANES)]
                for p in range(PLANES):
                    q = c * PLANES + p
                    here = planes[p]
                    above = jnp.where(
                        last,
                        pltpu.roll(columns[0], LANES - 1 - q, 1),
                        pltpu.roll(here, LANES - 1, 1),
                    )
                    below = jnp.where(
                        first, pltpu.roll(columns[1], (LANES - q) % LANES, 1), pltpu.roll(here, 1, 1)
                    )
                    stream = planes[(p + 1) % PLANES] + planes[(p + PLANES - 1) % PLANES]
                    rhs[q, r] = (
                        here
                        + diffusion_number * (stream - 2.0 * here)
                        + diffusion_number * (above + below - 2.0 * here)
                    )
        unit = quantize(jnp.minimum(i + 1, TURNS - 1), 1 - buffer)
        return through, unit

    for k in range(1, GROUP):
        block_copy(k, me).wait_recv()
    unit = quantize(0, 0)
    lax.fori_loop(0, TURNS, deposit, (jnp.ones((PLANES, LANES), jnp.float32), unit))

    field_steps = field.reshape(COMPS * PLANES, STEPS, CHUNKS, LANES)
    outs = [pltpu.make_async_copy(field, field_hbm, out_sem.at[0])]
    outs[0].start()

    sub = lax.broadcasted_iota(jnp.int32, (CHUNKS, LANES), 0)

    def down(x, d):
        return jnp.where(sub >= d, pltpu.roll(x, d, 0), 0.0)

    def up(x, d):
        return jnp.where(sub < CHUNKS - d, pltpu.roll(x, CHUNKS - d, 0), 0.0)

    def levels(x, shift):
        out = [x]
        for d in (1, 2):
            out.append(out[-1] * shift(out[-1], d))
        return out

    def scan(x, factors, shift):
        for d, factor in zip((1, 2, 4), factors):
            x = x + factor * shift(x, d)
        return x

    def prefix(r, carry):
        out = []
        for p in range(PLANES):
            value = carry[p] * lw_ref[p, r]
            a_ref[p, r] = value
            out.append(value)
        return tuple(out)

    one = jnp.ones((CHUNKS, LANES), jnp.float32)
    alpha = lax.fori_loop(0, STEPS, prefix, (one,) * PLANES, unroll=4)
    alphas = [levels(x, down) for x in alpha]
    through_low = []
    for p in range(PLANES):
        ends = scan(jnp.where(sub == 0, alpha[p], 0.0), alphas[p], down)
        through_low.append(jnp.where(sub == 0, 1.0, pltpu.roll(ends, 1, 0)))

    def suffix(i, carry):
        r = STEPS - 1 - i
        out = []
        for p in range(PLANES):
            ratio = c_ref[p, r]
            b = carry[p] * ratio
            g = a_ref[p, r] * through_low[p] + ratio * carry[PLANES + p]
            b_ref[p, r] = b
            g_ref[p, r] = g
            out.append((b, g))
        return tuple(x[0] for x in out) + tuple(x[1] for x in out)

    zero = jnp.zeros((CHUNKS, LANES), jnp.float32)
    done = lax.fori_loop(0, STEPS, suffix, (one,) * PLANES + (zero,) * PLANES, unroll=4)
    beta, g_first = done[:PLANES], done[PLANES:]
    betas = [levels(x, up) for x in beta]
    g_carry = []
    for p in range(PLANES):
        g_all = scan(g_first[p], betas[p], up)
        g_carry.append(up(g_all, 1))
        h_all = scan(jnp.where(sub == CHUNKS - 1, beta[p], 0.0), betas[p], up)
        h_carry = jnp.where(sub == CHUNKS - 1, 1.0, pltpu.roll(h_all, CHUNKS - 1, 0))
        hc_ref[p] = h_carry
        cf[wall, 0, p : p + 1, :] = g_all[0:1]
        cf[wall, 1, p : p + 1, :] = h_all[0:1]
        last_g = g_ref[p, STEPS - 1] + b_ref[p, STEPS - 1] * g_carry[p]
        cf[wall, 2, p : p + 1, :] = last_g[CHUNKS - 1 :]
        last_h = b_ref[p, STEPS - 1] * h_carry
        cf[wall, 3, p : p + 1, :] = last_h[CHUNKS - 1 :]

    def to_walls(ref, sems):
        copies = []
        for j in range(1, WALL):
            copy = pltpu.make_async_remote_copy(
                src_ref=ref.at[wall],
                dst_ref=ref.at[wall],
                send_sem=sems[0].at[j],
                recv_sem=sems[1].at[j],
                device_id={"wall": (wall + j) % WALL},
                device_id_type=MESH,
            )
            copy.start()
            copies.append(copy)
        return copies

    def from_walls(ref, sems):
        for j in range(1, WALL):
            pltpu.make_async_remote_copy(
                src_ref=ref.at[wall],
                dst_ref=ref.at[(wall + WALL - j) % WALL],
                send_sem=sems[0].at[j],
                recv_sem=sems[1].at[j],
                device_id={"wall": (wall + j) % WALL},
                device_id_type=MESH,
            ).wait_recv()

    coefficients = to_walls(cf, (cf_send, cf_recv))

    def full_g(r, carry):
        for p in range(PLANES):
            g_ref[p, r] = g_ref[p, r] + b_ref[p, r] * g_carry[p]
        return carry

    lax.fori_loop(0, STEPS, full_g, 0, unroll=4)
    for q, (source, target) in enumerate(((b_ref, b_hbm), (g_ref, g_hbm))):
        outs.append(pltpu.make_async_copy(source, target, out_sem.at[1 + q]))
        outs[-1].start()

    def forward(r, carry):
        out = []
        for p in range(PLANES):
            inverse = w_ref[p, r]
            factor = lw_ref[p, r]
            for c in range(COMPS):
                right = rhs[c * PLANES + p, r] + field_steps[c * PLANES + p, r]
                value = right * inverse + factor * carry[p * COMPS + c]
                ybuf[c * PLANES + p, r] = value
                out.append(value)
        return tuple(out)

    ends = lax.fori_loop(0, STEPS, forward, (zero,) * (PLANES * COMPS), unroll=8)
    carries = []
    for p in range(PLANES):
        for c in range(COMPS):
            carries.append(down(scan(ends[p * COMPS + c], alphas[p], down), 1))

    def backward(i, carry):
        r = STEPS - 1 - i
        out = []
        for p in range(PLANES):
            ratio = c_ref[p, r]
            prefix_product = a_ref[p, r]
            for c in range(COMPS):
                j = p * COMPS + c
                value = ybuf[c * PLANES + p, r] + prefix_product * carries[j] + ratio * carry[j]
                ybuf[c * PLANES + p, r] = value
                out.append(value)
        return tuple(out)

    starts = lax.fori_loop(0, STEPS, backward, (zero,) * (PLANES * COMPS), unroll=8)
    tails = []
    for p in range(PLANES):
        for c in range(COMPS):
            j = p * COMPS + c
            whole = scan(starts[j], betas[p], up)
            tails.append(up(whole, 1))
            bd[wall, 0, c, p : p + 1, :] = whole[0:1]
            bd[wall, 1, c, p : p + 1, :] = ybuf[c * PLANES + p, STEPS - 1][CHUNKS - 1 :]
    boundaries = to_walls(bd, (bd_send, bd_recv))
    outs.append(pltpu.make_async_copy(ybuf, part_hbm, out_sem.at[3]))
    outs[-1].start()
    from_walls(cf, (cf_send, cf_recv))
    betas_in = [jnp.zeros((PLANES, LANES), jnp.float32)]
    divisors, slopes = [], []
    for d in range(WALL):
        g0, h0, g1, h1 = (cf[d, q] for q in range(4))
        divisor = 1.0 / (1.0 - g0 * betas_in[d])
        slope = h0 * divisor
        divisors.append(divisor)
        slopes.append(slope)
        betas_in.append(g1 * betas_in[d] * slope + h1)
    for k in range(1, SPAN):
        block_copy(k, everyone[k]).wait_send()
    from_walls(bd, (bd_send, bd_recv))
    for c in range(COMPS):
        alpha_in = [jnp.zeros((PLANES, LANES), jnp.float32)]
        heads = []
        for d in range(WALL):
            head = (bd[d, 0, c] + cf[d, 0] * alpha_in[d]) * divisors[d]
            heads.append(head)
            alpha_in.append(bd[d, 1, c] + cf[d, 2] * (alpha_in[d] + betas_in[d] * head))
        upper_value = jnp.zeros((PLANES, LANES), jnp.float32)
        x_low = upper_value
        x_high = upper_value
        for d in reversed(range(WALL)):
            x_high = jnp.where(wall == d, upper_value, x_high)
            upper_value = heads[d] + slopes[d] * upper_value
            x_low = jnp.where(wall == d, alpha_in[d] + betas_in[d] * upper_value, x_low)
        xlu[0, c] = x_low
        xlu[1, c] = x_high

    for p in range(PLANES):
        for c in range(COMPS):
            q = c * PLANES + p
            ends_ref[0, q] = tails[p * COMPS + c] + hc_ref[p] * xlu[1, c, p : p + 1, :]
            ends_ref[1, q] = jnp.broadcast_to(xlu[0, c, p : p + 1, :], (CHUNKS, LANES))
    outs.append(pltpu.make_async_copy(ends_ref, ends_hbm, out_sem.at[4]))
    outs[-1].start()
    for copy in edges + coefficients + boundaries:
        copy.wait_send()
    for copy in outs:
        copy.wait()


def finish(
    part_hbm,
    b_hbm,
    g_hbm,
    ends_hbm,
    field_hbm,
    next_hbm,
    dep_hbm,
    part,
    b_ref,
    g_ref,
    ends,
    field,
    dep,
    sems,
    part_sem,
    field_sem,
    out_sem,
    dep_sem,
):
    small = [
        pltpu.make_async_copy(source, target, sems.at[q])
        for q, (source, target) in enumerate(((b_hbm, b_ref), (g_hbm, g_ref), (ends_hbm, ends)))
    ]
    groups = [pl.ds(c * PLANES, PLANES) for c in range(COMPS)]
    parts = [
        pltpu.make_async_copy(part_hbm.at[groups[c]], part.at[groups[c]], part_sem.at[c])
        for c in range(COMPS)
    ]
    fields = []
    for j in range(CHUNKS):
        fields.append(
            pltpu.make_async_copy(
                field_hbm.at[:, :, j, :],
                field.at[:, pl.ds(j * STEPS, STEPS), :],
                field_sem.at[j],
            )
        )
    for copy in small[:2] + parts[:1] + small[2:] + parts[1:] + fields:
        copy.start()
    for copy in small:
        copy.wait()
    outs = []
    for c in range(COMPS):
        parts[c].wait()
        highs = [ends[0, c * PLANES + p] for p in range(PLANES)]
        lows = [ends[1, c * PLANES + p] for p in range(PLANES)]

        def correct(r, carry, c=c, highs=highs, lows=lows):
            for p in range(PLANES):
                q = c * PLANES + p
                part[q, r] = part[q, r] + b_ref[p, r] * highs[p] + g_ref[p, r] * lows[p]
            return carry

        lax.fori_loop(0, STEPS, correct, 0, unroll=8)
        for j in range(CHUNKS):
            copy = pltpu.make_async_copy(
                part.at[groups[c], :, j, :],
                next_hbm.at[groups[c], pl.ds(j * STEPS, STEPS), :],
                out_sem.at[c * CHUNKS + j],
            )
            copy.start()
            outs.append(copy)
    for copy in fields:
        copy.wait()
    for c in range(COMPS):

        def narrow(p, carry, c=c):
            dep[c * PLANES + p] = field[c * PLANES + p].astype(jnp.bfloat16)
            return carry

        lax.fori_loop(0, PLANES, narrow, 0)
        copy = pltpu.make_async_copy(dep.at[groups[c]], dep_hbm.at[groups[c]], dep_sem.at[c])
        copy.start()
        outs.append(copy)
    for copy in outs:
        copy.wait()


def local(velocity, lower_weight, upper_weight, forces, cells, counts):
    f32 = jnp.float32
    flat = (COMPS * PLANES, ROWS, LANES)
    steps = (PLANES, STEPS, CHUNKS, LANES)
    all_steps = (COMPS * PLANES, STEPS, CHUNKS, LANES)
    dma = pltpu.SemaphoreType.DMA
    any_space = pl.BlockSpec(memory_space=pl.ANY)
    ends = (2, COMPS * PLANES, CHUNKS, LANES)
    solved = pl.pallas_call(
        kernel,
        name="substep",
        out_shape=(
            jax.ShapeDtypeStruct(all_steps, f32),
            jax.ShapeDtypeStruct(steps, f32),
            jax.ShapeDtypeStruct(steps, f32),
            jax.ShapeDtypeStruct(ends, f32),
            jax.ShapeDtypeStruct(flat, f32),
        ),
        in_specs=[any_space] * 6,
        out_specs=(any_space,) * 5,
        scratch_shapes=[
            pltpu.VMEM((COMPS, SPAN, PLANES, SLOTS), f32),
            pltpu.VMEM((SPAN, PLANES, SLOTS), jnp.int32),
            pltpu.SMEM((PLANES, SPAN), jnp.int32),
            pltpu.VMEM(all_steps, f32),
            pltpu.VMEM(steps, f32),
            pltpu.VMEM(steps, f32),
            pltpu.VMEM(all_steps, f32),
            pltpu.VMEM(flat, f32),
            pltpu.VMEM(all_steps, f32),
            pltpu.VMEM(steps, f32),
            pltpu.VMEM(steps, f32),
            pltpu.VMEM(steps, f32),
            pltpu.VMEM(steps, f32),
            pltpu.VMEM(steps, f32),
            pltpu.VMEM(steps, f32),
            pltpu.VMEM((PLANES, CHUNKS, LANES), f32),
            pltpu.VMEM(ends, f32),
            pltpu.VMEM((2, SPAN, PLANES, SLOTS), jnp.int32),
            pltpu.VMEM((2, GROUP, 3, COMPS, PLANES, SLOTS), f32),
            pltpu.VMEM((LANES, ROWS), f32),
            pltpu.VMEM((2, ROWS, LANES), f32),
            pltpu.VMEM((2, 16, ROWS), f32),
            pltpu.VMEM((2, 16, ROWS), f32),
            pltpu.VMEM((WALL, 4, PLANES, LANES), f32),
            pltpu.VMEM((WALL, 2, COMPS, PLANES, LANES), f32),
            pltpu.VMEM((2, COMPS, PLANES, LANES), f32),
            dma((SPAN,)),
            dma((SPAN,)),
            dma((2,)),
            dma((2,)),
            dma((WALL,)),
            dma((WALL,)),
            dma((WALL,)),
            dma((WALL,)),
            dma((32,)),
            dma((5,)),
        ],
        compiler_params=pltpu.CompilerParams(
            collective_id=0,
            has_side_effects=True,
        ),
    )(
        velocity.reshape(flat),
        lower_weight,
        upper_weight,
        forces,
        cells,
        jnp.swapaxes(counts, 2, 3),
    )
    velocity_next, deposit = pl.pallas_call(
        finish,
        name="finish",
        out_shape=(jax.ShapeDtypeStruct(flat, f32), jax.ShapeDtypeStruct(flat, jnp.bfloat16)),
        in_specs=[any_space] * 5,
        out_specs=(any_space,) * 2,
        scratch_shapes=[
            pltpu.VMEM(all_steps, f32),
            pltpu.VMEM(steps, f32),
            pltpu.VMEM(steps, f32),
            pltpu.VMEM(ends, f32),
            pltpu.VMEM(flat, f32),
            pltpu.VMEM(flat, jnp.bfloat16),
            dma((3,)),
            dma((COMPS,)),
            dma((CHUNKS,)),
            dma((COMPS * CHUNKS,)),
            dma((COMPS,)),
        ],
    )(*solved[:4], solved[4].reshape(all_steps))
    return velocity_next.reshape(velocity.shape), deposit.reshape(velocity.shape)


def solution(mesh):
    placed = (
        P(None, None, "wall", "span"),
        P(None, "wall", "span"),
        P(None, "wall", "span"),
        P(None, "wall", "span", None, None, None),
        P("wall", "span", None, None, None),
        P("wall", "span", None, None),
    )
    return jax.shard_map(
        local,
        mesh=mesh,
        in_specs=placed,
        out_specs=(P(None, None, "wall", "span"), P(None, None, "wall", "span")),
        check_vma=False,
    )
```

```python
import functools

import jax
import jax.numpy as jnp
from jax import lax
from jax.experimental import pallas as pl
from jax.experimental.pallas import tpu as pltpu
from jax.sharding import PartitionSpec as P

MESH = pl.DeviceIdType.MESH
diffusion_number = 0.2
SPAN = 32
WALL = 4
PLANES = 4
COMPS = 3
ROWS = 256
LANES = 128
SLOTS = 768
CHUNKS = 8
STEPS = ROWS // CHUNKS
GROUP = 4
TURNS = SPAN // GROUP
AHEAD = 4


def kernel(
    vel_hbm,
    low_hbm,
    upp_hbm,
    forces_hbm,
    cells_hbm,
    counts_hbm,
    part_hbm,
    b_hbm,
    g_hbm,
    ends_hbm,
    field_hbm,
    recv,
    cells,
    counts,
    vel,
    low,
    upp,
    rhs,
    field,
    ybuf,
    w_ref,
    lw_ref,
    c_ref,
    a_ref,
    b_ref,
    g_ref,
    hc_ref,
    ends_ref,
    spots,
    quant,
    pack,
    cols,
    hsend,
    hrecv,
    cf,
    bd,
    xlu,
    send_sem,
    recv_sem,
    halo_send,
    halo_recv,
    cf_send,
    cf_recv,
    bd_send,
    bd_recv,
    load_sem,
    out_sem,
):
    wall = lax.axis_index("wall")
    me = lax.axis_index("span")
    px, py, pc = lax.div(me, 8), lax.rem(lax.div(me, 2), 4), lax.rem(me, 2)

    def peers(i, sign):
        if isinstance(i, int):
            odd, high, high_x = i % 2, i // 2, i // 4
            high_y = high % 2
        else:
            odd, high, high_x = lax.rem(i, 2), lax.div(i, 2), lax.div(i, 4)
            high_y = lax.rem(high, 2)
        out = []
        for low in range(2):
            dx = odd * (1 + 2 * low) + (1 - odd) * 2 * high_x
            dy = odd * high + (1 - odd) * (low + 2 * high_y)
            x = lax.rem(px + 4 + sign * dx, 4)
            y = lax.rem(py + 4 + sign * dy, 4)
            for core in range(2):
                out.append(x * 8 + y * 2 + lax.rem(pc + core, 2))
        return out

    everyone = sum((peers(i, 1) for i in range(TURNS)), [])

    low_flat = low.reshape(PLANES * ROWS, LANES)
    upp_flat = upp.reshape(PLANES * ROWS, LANES)
    w_flat = w_ref.reshape(PLANES * ROWS, LANES)
    lw_flat = lw_ref.reshape(PLANES * ROWS, LANES)
    c_flat = c_ref.reshape(PLANES * ROWS, LANES)
    loads = [
        pltpu.make_async_copy(counts_hbm.at[0, 0], counts, load_sem.at[0]),
        pltpu.make_async_copy(cells_hbm.at[0, 0], cells, load_sem.at[1]),
        pltpu.make_async_copy(forces_hbm.at[:, 0, 0, me], recv.at[:, 0], load_sem.at[2]),
    ]
    vel_loads = []
    for j in range(CHUNKS):
        rows = pl.ds(j * STEPS, STEPS)
        vel_loads.append(
            pltpu.make_async_copy(
                vel_hbm.at[:, rows, :], vel.at[:, :, j, :], load_sem.at[8 + j]
            )
        )
        for q, (source, target) in enumerate(((low_hbm, low), (upp_hbm, upp))):
            loads.append(
                pltpu.make_async_copy(
                    source.at[:, rows, :], target.at[:, :, j, :], load_sem.at[16 + 8 * q + j]
                )
            )
    for copy in vel_loads:
        copy.start()
    for copy in loads:
        copy.start()

    barrier = pltpu.get_barrier_semaphore()
    for k in range(1, SPAN):
        pl.semaphore_signal(barrier, inc=1, device_id={"span": everyone[k]}, device_id_type=MESH)
    for j in range(1, WALL):
        pl.semaphore_signal(
            barrier, inc=1, device_id={"wall": (wall + j) % WALL}, device_id_type=MESH
        )
    pl.semaphore_wait(barrier, SPAN - 1 + WALL - 1)

    def block_copy(k, target):
        return pltpu.make_async_remote_copy(
            src_ref=forces_hbm.at[:, 0, 0, target],
            dst_ref=recv.at[:, k],
            send_sem=send_sem.at[k],
            recv_sem=recv_sem.at[k],
            device_id={"span": target},
            device_id_type=MESH,
        )

    for k in range(1, 2 * GROUP):
        block_copy(k, everyone[k]).start()

    for copy in vel_loads:
        copy.wait()
    lane = lax.broadcasted_iota(jnp.int32, (ROWS, LANES), 1)
    edges = []
    for side, column in ((0, 0), (1, LANES - 1)):
        packed = jnp.zeros((ROWS, LANES), jnp.float32)
        for i in range(COMPS * PLANES):
            block = vel[i].reshape(ROWS, LANES)
            packed = jnp.where(lane == i, pltpu.roll(block, (i - column) % LANES, 1), packed)
        hsend[side] = jnp.transpose(packed)[0:16]
        target = (me + SPAN - 1) % SPAN if side == 0 else (me + 1) % SPAN
        copy = pltpu.make_async_remote_copy(
            src_ref=hsend.at[side],
            dst_ref=hrecv.at[side],
            send_sem=halo_send.at[side],
            recv_sem=halo_recv.at[side],
            device_id={"span": target},
            device_id_type=MESH,
        )
        copy.start()
        edges.append(copy)
    for k in range(2 * GROUP, AHEAD * GROUP):
        block_copy(k, everyone[k]).start()

    field[...] = jnp.zeros_like(field)
    cols[...] = jnp.zeros_like(cols)
    pack[...] = jnp.zeros_like(pack)
    for copy in loads:
        copy.wait()

    slot = lax.broadcasted_iota(jnp.int32, (PLANES, SLOTS), 1)
    plane = lax.broadcasted_iota(jnp.int32, (PLANES, SLOTS), 0)

    def locate(s, carry):
        cell = cells[s]
        limit = jnp.where(plane < 1, counts[0, s], counts[1, s])
        limit = jnp.where(plane < 2, limit, jnp.where(plane < 3, counts[2, s], counts[3, s]))
        row = ((cell >> 7) & 31) * CHUNKS + (cell >> 12)
        spots[0, s] = jnp.where(slot < limit, row & 127, -1)
        spots[1, s] = (((row >> 7) << 7) + (cell & 127) - 128)
        return carry

    lax.fori_loop(0, SPAN, locate, 0, unroll=2)

    float8 = jnp.float8_e4m3fn
    one8, zero8 = jnp.ones((), float8), jnp.zeros((), float8)
    io_m = lax.broadcasted_iota(jnp.int32, (LANES, 256), 0).astype(jnp.int8)
    io_n = (lax.broadcasted_iota(jnp.int32, (256, 256), 0) - 128).astype(jnp.int8)
    last = lax.broadcasted_iota(jnp.int32, (CHUNKS, LANES), 1) == LANES - 1
    first = lax.broadcasted_iota(jnp.int32, (CHUNKS, LANES), 1) == 0

    def arrive(i):
        for j in range(GROUP):
            block_copy(GROUP * i + j, me).wait_recv()

    def quantize(i, buffer):
        blocks = [[recv[c, GROUP * i + j] for c in range(COMPS)] for j in range(GROUP)]
        top = None
        for block in sum(blocks, []):
            top = jnp.abs(block) if top is None else jnp.maximum(top, jnp.abs(block))
        top = jnp.maximum(jnp.max(top, axis=(0, 1), keepdims=True), 1e-30)
        scale = 384.0 / top
        for j in range(GROUP):
            for c in range(COMPS):
                rest = blocks[j][c] * scale
                for t in range(3):
                    term = rest.astype(float8).astype(jnp.float32)
                    quant[buffer, j, t, c] = term
                    rest = rest - term
        return top * (1.0 / 384.0)

    def deposit(i, carry):
        through, unit = carry

        @pl.when(i < TURNS - AHEAD)
        def _():
            for j, target in enumerate(peers(i + AHEAD, 1)):
                block_copy(GROUP * (i + AHEAD) + j, target).start()

        @pl.when(i < TURNS - 1)
        def _():
            arrive(i + 1)

        @pl.when(i == 1)
        def _():
            for side in range(2):
                edges[side].wait_recv()
                pack[0:16] = hrecv[side]
                cols[side] = jnp.transpose(pack[...])

        buffer = lax.rem(i, 2)
        sources = peers(i, -1)
        for p in range(PLANES):
            total = None
            for j in range(GROUP):
                m = spots[0, sources[j], p : p + 1, :].astype(jnp.int8)
                n = spots[1, sources[j], p : p + 1, :].astype(jnp.int8)
                values = [
                    [quant[buffer, j, t, c, p : p + 1, :].astype(float8) for c in range(COMPS)]
                    for t in range(3)
                ]
                for start in range(0, SLOTS, 256):
                    part = slice(start, start + 256)
                    hot_m = m[:, part] == io_m
                    hot_n = jnp.where(n[:, part] == io_n, one8, zero8)
                    for t in range(3):
                        weighted = jnp.concatenate(
                            [jnp.where(hot_m, values[t][c][:, part], zero8) for c in range(COMPS)],
                            axis=0,
                        )
                        term = lax.dot_general(
                            weighted,
                            hot_n,
                            (((1,), (1,)), ((), ())),
                            preferred_element_type=jnp.float32,
                        )
                        total = term if total is None else total + term
            total = total.reshape(COMPS, LANES, 256) * unit
            for c in range(COMPS):
                field[c * PLANES + p, 0:128, :] += total[c, :, 0:128]
                field[c * PLANES + p, 128:256, :] += total[c, :, 128:256]
        for row in range(ROWS // TURNS):
            index = pl.ds(row * CHUNKS + i, PLANES, stride=ROWS)
            lower = low_flat[index, :]
            upper = upp_flat[index, :]
            gain = 1.0 + lower * through
            inverse = 1.0 / (gain + upper)
            w_flat[index, :] = inverse
            lw_flat[index, :] = lower * inverse
            c_flat[index, :] = upper * inverse
            through = gain * inverse
        for step in range(5):
            r = jnp.clip(5 * (i - 1) + step, 0, STEPS - 1)
            edge = pl.ds(pl.multiple_of(r * CHUNKS, CHUNKS), CHUNKS)
            columns = [cols[side, edge, :] for side in range(2)]
            for c in range(COMPS):
                planes = [vel[c * PLANES + p, r] for p in range(PLANES)]
                for p in range(PLANES):
                    q = c * PLANES + p
                    here = planes[p]
                    above = jnp.where(
                        last,
                        pltpu.roll(columns[0], LANES - 1 - q, 1),
                        pltpu.roll(here, LANES - 1, 1),
                    )
                    below = jnp.where(
                        first, pltpu.roll(columns[1], (LANES - q) % LANES, 1), pltpu.roll(here, 1, 1)
                    )
                    stream = planes[(p + 1) % PLANES] + planes[(p + PLANES - 1) % PLANES]
                    rhs[q, r] = (
                        here
                        + diffusion_number * (stream - 2.0 * here)
                        + diffusion_number * (above + below - 2.0 * here)
                    )
        unit = quantize(jnp.minimum(i + 1, TURNS - 1), 1 - buffer)
        return through, unit

    for k in range(1, GROUP):
        block_copy(k, me).wait_recv()
    unit = quantize(0, 0)
    lax.fori_loop(0, TURNS, deposit, (jnp.ones((PLANES, LANES), jnp.float32), unit))

    field_steps = field.reshape(COMPS * PLANES, STEPS, CHUNKS, LANES)
    outs = [pltpu.make_async_copy(field, field_hbm, out_sem.at[0])]
    outs[0].start()

    sub = lax.broadcasted_iota(jnp.int32, (CHUNKS, LANES), 0)

    def down(x, d):
        return jnp.where(sub >= d, pltpu.roll(x, d, 0), 0.0)

    def up(x, d):
        return jnp.where(sub < CHUNKS - d, pltpu.roll(x, CHUNKS - d, 0), 0.0)

    def levels(x, shift):
        out = [x]
        for d in (1, 2):
            out.append(out[-1] * shift(out[-1], d))
        return out

    def scan(x, factors, shift):
        for d, factor in zip((1, 2, 4), factors):
            x = x + factor * shift(x, d)
        return x

    def prefix(r, carry):
        out = []
        for p in range(PLANES):
            value = carry[p] * lw_ref[p, r]
            a_ref[p, r] = value
            out.append(value)
        return tuple(out)

    one = jnp.ones((CHUNKS, LANES), jnp.float32)
    alpha = lax.fori_loop(0, STEPS, prefix, (one,) * PLANES, unroll=4)
    alphas = [levels(x, down) for x in alpha]
    through_low = []
    for p in range(PLANES):
        ends = scan(jnp.where(sub == 0, alpha[p], 0.0), alphas[p], down)
        through_low.append(jnp.where(sub == 0, 1.0, pltpu.roll(ends, 1, 0)))

    def suffix(i, carry):
        r = STEPS - 1 - i
        out = []
        for p in range(PLANES):
            ratio = c_ref[p, r]
            b = carry[p] * ratio
            g = a_ref[p, r] * through_low[p] + ratio * carry[PLANES + p]
            b_ref[p, r] = b
            g_ref[p, r] = g
            out.append((b, g))
        return tuple(x[0] for x in out) + tuple(x[1] for x in out)

    zero = jnp.zeros((CHUNKS, LANES), jnp.float32)
    done = lax.fori_loop(0, STEPS, suffix, (one,) * PLANES + (zero,) * PLANES, unroll=4)
    beta, g_first = done[:PLANES], done[PLANES:]
    betas = [levels(x, up) for x in beta]
    g_carry = []
    for p in range(PLANES):
        g_all = scan(g_first[p], betas[p], up)
        g_carry.append(up(g_all, 1))
        h_all = scan(jnp.where(sub == CHUNKS - 1, beta[p], 0.0), betas[p], up)
        h_carry = jnp.where(sub == CHUNKS - 1, 1.0, pltpu.roll(h_all, CHUNKS - 1, 0))
        hc_ref[p] = h_carry
        cf[wall, 0, p : p + 1, :] = g_all[0:1]
        cf[wall, 1, p : p + 1, :] = h_all[0:1]
        last_g = g_ref[p, STEPS - 1] + b_ref[p, STEPS - 1] * g_carry[p]
        cf[wall, 2, p : p + 1, :] = last_g[CHUNKS - 1 :]
        last_h = b_ref[p, STEPS - 1] * h_carry
        cf[wall, 3, p : p + 1, :] = last_h[CHUNKS - 1 :]

    def to_walls(ref, sems):
        copies = []
        for j in range(1, WALL):
            copy = pltpu.make_async_remote_copy(
                src_ref=ref.at[wall],
                dst_ref=ref.at[wall],
                send_sem=sems[0].at[j],
                recv_sem=sems[1].at[j],
                device_id={"wall": (wall + j) % WALL},
                device_id_type=MESH,
            )
            copy.start()
            copies.append(copy)
        return copies

    def from_walls(ref, sems):
        for j in range(1, WALL):
            pltpu.make_async_remote_copy(
                src_ref=ref.at[wall],
                dst_ref=ref.at[(wall + WALL - j) % WALL],
                send_sem=sems[0].at[j],
                recv_sem=sems[1].at[j],
                device_id={"wall": (wall + j) % WALL},
                device_id_type=MESH,
            ).wait_recv()

    coefficients = to_walls(cf, (cf_send, cf_recv))

    def full_g(r, carry):
        for p in range(PLANES):
            g_ref[p, r] = g_ref[p, r] + b_ref[p, r] * g_carry[p]
        return carry

    lax.fori_loop(0, STEPS, full_g, 0, unroll=4)
    for q, (source, target) in enumerate(((b_ref, b_hbm), (g_ref, g_hbm))):
        outs.append(pltpu.make_async_copy(source, target, out_sem.at[1 + q]))
        outs[-1].start()

    def forward(r, carry):
        out = []
        for p in range(PLANES):
            inverse = w_ref[p, r]
            factor = lw_ref[p, r]
            for c in range(COMPS):
                right = rhs[c * PLANES + p, r] + field_steps[c * PLANES + p, r]
                value = right * inverse + factor * carry[p * COMPS + c]
                ybuf[c * PLANES + p, r] = value
                out.append(value)
        return tuple(out)

    ends = lax.fori_loop(0, STEPS, forward, (zero,) * (PLANES * COMPS), unroll=8)
    carries = []
    for p in range(PLANES):
        for c in range(COMPS):
            carries.append(down(scan(ends[p * COMPS + c], alphas[p], down), 1))

    def backward(i, carry):
        r = STEPS - 1 - i
        out = []
        for p in range(PLANES):
            ratio = c_ref[p, r]
            prefix_product = a_ref[p, r]
            for c in range(COMPS):
                j = p * COMPS + c
                value = ybuf[c * PLANES + p, r] + prefix_product * carries[j] + ratio * carry[j]
                ybuf[c * PLANES + p, r] = value
                out.append(value)
        return tuple(out)

    starts = lax.fori_loop(0, STEPS, backward, (zero,) * (PLANES * COMPS), unroll=8)
    tails = []
    for p in range(PLANES):
        for c in range(COMPS):
            j = p * COMPS + c
            whole = scan(starts[j], betas[p], up)
            tails.append(up(whole, 1))
            bd[wall, 0, c, p : p + 1, :] = whole[0:1]
            bd[wall, 1, c, p : p + 1, :] = ybuf[c * PLANES + p, STEPS - 1][CHUNKS - 1 :]
    boundaries = to_walls(bd, (bd_send, bd_recv))
    outs.append(pltpu.make_async_copy(ybuf, part_hbm, out_sem.at[3]))
    outs[-1].start()
    from_walls(cf, (cf_send, cf_recv))
    betas_in = [jnp.zeros((PLANES, LANES), jnp.float32)]
    divisors, slopes = [], []
    for d in range(WALL):
        g0, h0, g1, h1 = (cf[d, q] for q in range(4))
        divisor = 1.0 / (1.0 - g0 * betas_in[d])
        slope = h0 * divisor
        divisors.append(divisor)
        slopes.append(slope)
        betas_in.append(g1 * betas_in[d] * slope + h1)
    for k in range(1, SPAN):
        block_copy(k, everyone[k]).wait_send()
    from_walls(bd, (bd_send, bd_recv))
    for c in range(COMPS):
        alpha_in = [jnp.zeros((PLANES, LANES), jnp.float32)]
        heads = []
        for d in range(WALL):
            head = (bd[d, 0, c] + cf[d, 0] * alpha_in[d]) * divisors[d]
            heads.append(head)
            alpha_in.append(bd[d, 1, c] + cf[d, 2] * (alpha_in[d] + betas_in[d] * head))
        upper_value = jnp.zeros((PLANES, LANES), jnp.float32)
        x_low = upper_value
        x_high = upper_value
        for d in reversed(range(WALL)):
            x_high = jnp.where(wall == d, upper_value, x_high)
            upper_value = heads[d] + slopes[d] * upper_value
            x_low = jnp.where(wall == d, alpha_in[d] + betas_in[d] * upper_value, x_low)
        xlu[0, c] = x_low
        xlu[1, c] = x_high

    for p in range(PLANES):
        for c in range(COMPS):
            q = c * PLANES + p
            ends_ref[0, q] = tails[p * COMPS + c] + hc_ref[p] * xlu[1, c, p : p + 1, :]
            ends_ref[1, q] = jnp.broadcast_to(xlu[0, c, p : p + 1, :], (CHUNKS, LANES))
    outs.append(pltpu.make_async_copy(ends_ref, ends_hbm, out_sem.at[4]))
    outs[-1].start()
    for copy in edges + coefficients + boundaries:
        copy.wait_send()
    for copy in outs:
        copy.wait()


def finish(
    part_hbm,
    b_hbm,
    g_hbm,
    ends_hbm,
    field_hbm,
    next_hbm,
    dep_hbm,
    part,
    b_ref,
    g_ref,
    ends,
    field,
    dep,
    sems,
    part_sem,
    field_sem,
    out_sem,
    dep_sem,
):
    small = [
        pltpu.make_async_copy(source, target, sems.at[q])
        for q, (source, target) in enumerate(((b_hbm, b_ref), (g_hbm, g_ref), (ends_hbm, ends)))
    ]
    groups = [pl.ds(c * PLANES, PLANES) for c in range(COMPS)]
    parts = [
        pltpu.make_async_copy(part_hbm.at[groups[c]], part.at[groups[c]], part_sem.at[c])
        for c in range(COMPS)
    ]
    fields = []
    for j in range(CHUNKS):
        fields.append(
            pltpu.make_async_copy(
                field_hbm.at[:, :, j, :],
                field.at[:, pl.ds(j * STEPS, STEPS), :],
                field_sem.at[j],
            )
        )
    for copy in small[:2] + parts[:1] + small[2:] + parts[1:] + fields:
        copy.start()
    for copy in small:
        copy.wait()
    outs = []
    for c in range(COMPS):
        parts[c].wait()
        highs = [ends[0, c * PLANES + p] for p in range(PLANES)]
        lows = [ends[1, c * PLANES + p] for p in range(PLANES)]

        def correct(r, carry, c=c, highs=highs, lows=lows):
            for p in range(PLANES):
                q = c * PLANES + p
                part[q, r] = part[q, r] + b_ref[p, r] * highs[p] + g_ref[p, r] * lows[p]
            return carry

        lax.fori_loop(0, STEPS, correct, 0, unroll=8)
        for j in range(CHUNKS):
            copy = pltpu.make_async_copy(
                part.at[groups[c], :, j, :],
                next_hbm.at[groups[c], pl.ds(j * STEPS, STEPS), :],
                out_sem.at[c * CHUNKS + j],
            )
            copy.start()
            outs.append(copy)
    for copy in fields:
        copy.wait()
    for c in range(COMPS):

        def narrow(p, carry, c=c):
            dep[c * PLANES + p] = field[c * PLANES + p].astype(jnp.bfloat16)
            return carry

        lax.fori_loop(0, PLANES, narrow, 0)
        copy = pltpu.make_async_copy(dep.at[groups[c]], dep_hbm.at[groups[c]], dep_sem.at[c])
        copy.start()
        outs.append(copy)
    for copy in outs:
        copy.wait()


def local(velocity, lower_weight, upper_weight, forces, cells, counts):
    f32 = jnp.float32
    flat = (COMPS * PLANES, ROWS, LANES)
    steps = (PLANES, STEPS, CHUNKS, LANES)
    all_steps = (COMPS * PLANES, STEPS, CHUNKS, LANES)
    dma = pltpu.SemaphoreType.DMA
    any_space = pl.BlockSpec(memory_space=pl.ANY)
    ends = (2, COMPS * PLANES, CHUNKS, LANES)
    solved = pl.pallas_call(
        kernel,
        name="substep",
        out_shape=(
            jax.ShapeDtypeStruct(all_steps, f32),
            jax.ShapeDtypeStruct(steps, f32),
            jax.ShapeDtypeStruct(steps, f32),
            jax.ShapeDtypeStruct(ends, f32),
            jax.ShapeDtypeStruct(flat, f32),
        ),
        in_specs=[any_space] * 6,
        out_specs=(any_space,) * 5,
        scratch_shapes=[
            pltpu.VMEM((COMPS, SPAN, PLANES, SLOTS), f32),
            pltpu.VMEM((SPAN, PLANES, SLOTS), jnp.int32),
            pltpu.SMEM((PLANES, SPAN), jnp.int32),
            pltpu.VMEM(all_steps, f32),
            pltpu.VMEM(steps, f32),
            pltpu.VMEM(steps, f32),
            pltpu.VMEM(all_steps, f32),
            pltpu.VMEM(flat, f32),
            pltpu.VMEM(all_steps, f32),
            pltpu.VMEM(steps, f32),
            pltpu.VMEM(steps, f32),
            pltpu.VMEM(steps, f32),
            pltpu.VMEM(steps, f32),
            pltpu.VMEM(steps, f32),
            pltpu.VMEM(steps, f32),
            pltpu.VMEM((PLANES, CHUNKS, LANES), f32),
            pltpu.VMEM(ends, f32),
            pltpu.VMEM((2, SPAN, PLANES, SLOTS), jnp.int32),
            pltpu.VMEM((2, GROUP, 3, COMPS, PLANES, SLOTS), f32),
            pltpu.VMEM((LANES, ROWS), f32),
            pltpu.VMEM((2, ROWS, LANES), f32),
            pltpu.VMEM((2, 16, ROWS), f32),
            pltpu.VMEM((2, 16, ROWS), f32),
            pltpu.VMEM((WALL, 4, PLANES, LANES), f32),
            pltpu.VMEM((WALL, 2, COMPS, PLANES, LANES), f32),
            pltpu.VMEM((2, COMPS, PLANES, LANES), f32),
            dma((SPAN,)),
            dma((SPAN,)),
            dma((2,)),
            dma((2,)),
            dma((WALL,)),
            dma((WALL,)),
            dma((WALL,)),
            dma((WALL,)),
            dma((32,)),
            dma((5,)),
        ],
        compiler_params=pltpu.CompilerParams(
            collective_id=0,
            has_side_effects=True,
        ),
    )(
        velocity.reshape(flat),
        lower_weight,
        upper_weight,
        forces,
        cells,
        jnp.swapaxes(counts, 2, 3),
    )
    velocity_next, deposit = pl.pallas_call(
        finish,
        name="finish",
        out_shape=(jax.ShapeDtypeStruct(flat, f32), jax.ShapeDtypeStruct(flat, jnp.bfloat16)),
        in_specs=[any_space] * 5,
        out_specs=(any_space,) * 2,
        scratch_shapes=[
            pltpu.VMEM(all_steps, f32),
            pltpu.VMEM(steps, f32),
            pltpu.VMEM(steps, f32),
            pltpu.VMEM(ends, f32),
            pltpu.VMEM(flat, f32),
            pltpu.VMEM(flat, jnp.bfloat16),
            dma((3,)),
            dma((COMPS,)),
            dma((CHUNKS,)),
            dma((COMPS * CHUNKS,)),
            dma((COMPS,)),
        ],
    )(*solved[:4], solved[4].reshape(all_steps))
    return velocity_next.reshape(velocity.shape), deposit.reshape(velocity.shape)


def solution(mesh):
    placed = (
        P(None, None, "wall", "span"),
        P(None, "wall", "span"),
        P(None, "wall", "span"),
        P(None, "wall", "span", None, None, None),
        P("wall", "span", None, None, None),
        P("wall", "span", None, None),
    )
    return jax.shard_map(
        local,
        mesh=mesh,
        in_specs=placed,
        out_specs=(P(None, None, "wall", "span"), P(None, None, "wall", "span")),
        check_vma=False,
    )
```

```python
import functools

import jax
import jax.numpy as jnp
from jax import lax
from jax.experimental import pallas as pl
from jax.experimental.pallas import tpu as pltpu
from jax.sharding import PartitionSpec as P

MESH = pl.DeviceIdType.MESH
diffusion_number = 0.2
SPAN = 32
WALL = 4
PLANES = 4
COMPS = 3
ROWS = 256
LANES = 128
SLOTS = 768
CHUNKS = 8
STEPS = ROWS // CHUNKS
GROUP = 4
TURNS = SPAN // GROUP
AHEAD = 4


def kernel(
    vel_hbm,
    low_hbm,
    upp_hbm,
    forces_hbm,
    cells_hbm,
    counts_hbm,
    part_hbm,
    b_hbm,
    g_hbm,
    ends_hbm,
    field_hbm,
    recv,
    cells,
    counts,
    vel,
    low,
    upp,
    rhs,
    field,
    ybuf,
    w_ref,
    lw_ref,
    c_ref,
    a_ref,
    b_ref,
    g_ref,
    hc_ref,
    ends_ref,
    spots,
    quant,
    units,
    pack,
    cols,
    hsend,
    hrecv,
    cf,
    bd,
    xlu,
    send_sem,
    recv_sem,
    halo_send,
    halo_recv,
    cf_send,
    cf_recv,
    bd_send,
    bd_recv,
    load_sem,
    out_sem,
):
    wall = lax.axis_index("wall")
    me = lax.axis_index("span")
    px, py, pc = lax.div(me, 8), lax.rem(lax.div(me, 2), 4), lax.rem(me, 2)

    def peers(i, sign):
        if isinstance(i, int):
            odd, high, high_x = i % 2, i // 2, i // 4
            high_y = high % 2
        else:
            odd, high, high_x = lax.rem(i, 2), lax.div(i, 2), lax.div(i, 4)
            high_y = lax.rem(high, 2)
        out = []
        for low in range(2):
            dx = odd * (1 + 2 * low) + (1 - odd) * 2 * high_x
            dy = odd * high + (1 - odd) * (low + 2 * high_y)
            x = lax.rem(px + 4 + sign * dx, 4)
            y = lax.rem(py + 4 + sign * dy, 4)
            for core in range(2):
                out.append(x * 8 + y * 2 + lax.rem(pc + core, 2))
        return out

    everyone = sum((peers(i, 1) for i in range(TURNS)), [])

    low_flat = low.reshape(PLANES * ROWS, LANES)
    upp_flat = upp.reshape(PLANES * ROWS, LANES)
    w_flat = w_ref.reshape(PLANES * ROWS, LANES)
    lw_flat = lw_ref.reshape(PLANES * ROWS, LANES)
    c_flat = c_ref.reshape(PLANES * ROWS, LANES)
    loads = [
        pltpu.make_async_copy(counts_hbm.at[0, 0], counts, load_sem.at[0]),
        pltpu.make_async_copy(cells_hbm.at[0, 0], cells, load_sem.at[1]),
        pltpu.make_async_copy(forces_hbm.at[:, 0, 0, me], recv.at[:, 0], load_sem.at[2]),
    ]
    vel_loads = []
    for j in range(CHUNKS):
        rows = pl.ds(j * STEPS, STEPS)
        vel_loads.append(
            pltpu.make_async_copy(
                vel_hbm.at[:, rows, :], vel.at[:, :, j, :], load_sem.at[8 + j]
            )
        )
        for q, (source, target) in enumerate(((low_hbm, low), (upp_hbm, upp))):
            loads.append(
                pltpu.make_async_copy(
                    source.at[:, rows, :], target.at[:, :, j, :], load_sem.at[16 + 8 * q + j]
                )
            )
    for copy in vel_loads:
        copy.start()
    for copy in loads:
        copy.start()

    barrier = pltpu.get_barrier_semaphore()
    for k in range(1, SPAN):
        pl.semaphore_signal(barrier, inc=1, device_id={"span": everyone[k]}, device_id_type=MESH)
    for j in range(1, WALL):
        pl.semaphore_signal(
            barrier, inc=1, device_id={"wall": (wall + j) % WALL}, device_id_type=MESH
        )
    pl.semaphore_wait(barrier, SPAN - 1 + WALL - 1)

    def block_copy(k, target):
        return pltpu.make_async_remote_copy(
            src_ref=forces_hbm.at[:, 0, 0, target],
            dst_ref=recv.at[:, k],
            send_sem=send_sem.at[k],
            recv_sem=recv_sem.at[k],
            device_id={"span": target},
            device_id_type=MESH,
        )

    for k in range(1, 2 * GROUP):
        block_copy(k, everyone[k]).start()

    for copy in vel_loads:
        copy.wait()
    lane = lax.broadcasted_iota(jnp.int32, (ROWS, LANES), 1)
    edges = []
    for side, column in ((0, 0), (1, LANES - 1)):
        packed = jnp.zeros((ROWS, LANES), jnp.float32)
        for i in range(COMPS * PLANES):
            block = vel[i].reshape(ROWS, LANES)
            packed = jnp.where(lane == i, pltpu.roll(block, (i - column) % LANES, 1), packed)
        hsend[side] = jnp.transpose(packed)[0:16]
        target = (me + SPAN - 1) % SPAN if side == 0 else (me + 1) % SPAN
        copy = pltpu.make_async_remote_copy(
            src_ref=hsend.at[side],
            dst_ref=hrecv.at[side],
            send_sem=halo_send.at[side],
            recv_sem=halo_recv.at[side],
            device_id={"span": target},
            device_id_type=MESH,
        )
        copy.start()
        edges.append(copy)
    for k in range(2 * GROUP, AHEAD * GROUP):
        block_copy(k, everyone[k]).start()

    field[...] = jnp.zeros_like(field)
    cols[...] = jnp.zeros_like(cols)
    pack[...] = jnp.zeros_like(pack)
    for copy in loads:
        copy.wait()

    slot = lax.broadcasted_iota(jnp.int32, (PLANES, SLOTS), 1)
    plane = lax.broadcasted_iota(jnp.int32, (PLANES, SLOTS), 0)

    def locate(s, carry):
        cell = cells[s]
        limit = jnp.where(plane < 1, counts[0, s], counts[1, s])
        limit = jnp.where(plane < 2, limit, jnp.where(plane < 3, counts[2, s], counts[3, s]))
        row = ((cell >> 7) & 31) * CHUNKS + (cell >> 12)
        spots[0, s] = jnp.where(slot < limit, row & 127, -1)
        spots[1, s] = (((row >> 7) << 7) + (cell & 127) - 128)
        return carry

    lax.fori_loop(0, SPAN, locate, 0, unroll=2)

    float8 = jnp.float8_e4m3fn
    one8, zero8 = jnp.ones((), float8), jnp.zeros((), float8)
    io_m = lax.broadcasted_iota(jnp.int32, (LANES, 256), 0).astype(jnp.int8)
    io_n = (lax.broadcasted_iota(jnp.int32, (256, 256), 0) - 128).astype(jnp.int8)
    last = lax.broadcasted_iota(jnp.int32, (CHUNKS, LANES), 1) == LANES - 1
    first = lax.broadcasted_iota(jnp.int32, (CHUNKS, LANES), 1) == 0

    def arrive(i):
        for j in range(GROUP):
            block_copy(GROUP * i + j, me).wait_recv()

    def quantize(i, buffer):
        blocks = [[recv[c, GROUP * i + j] for c in range(COMPS)] for j in range(GROUP)]
        top = None
        for block in sum(blocks, []):
            top = jnp.abs(block) if top is None else jnp.maximum(top, jnp.abs(block))
        top = jnp.maximum(jnp.max(top, axis=(0, 1), keepdims=True), 1e-30)
        scale = 384.0 / top
        for j in range(GROUP):
            for c in range(COMPS):
                rest = blocks[j][c] * scale
                for t in range(3):
                    term = rest.astype(float8).astype(jnp.float32)
                    quant[buffer, j, t, c] = term
                    rest = rest - term
        units[buffer] = jnp.broadcast_to(top * (1.0 / 384.0), (8, LANES))

    def deposit(i, through):
        @pl.when(i < TURNS - AHEAD)
        def _():
            for j, target in enumerate(peers(i + AHEAD, 1)):
                block_copy(GROUP * (i + AHEAD) + j, target).start()

        @pl.when(i * (TURNS - 1 - i) > 0)
        def _():
            arrive(i + 1)

        @pl.when(i == 1)
        def _():
            arrive(1)
            quantize(1, 1)
            for side in range(2):
                edges[side].wait_recv()
                pack[0:16] = hrecv[side]
                cols[side] = jnp.transpose(pack[...])

        buffer = lax.rem(i, 2)
        unit = units[buffer, 0:1, 0:1]
        sources = peers(i, -1)
        for p in range(PLANES):
            total = None
            for j in range(GROUP):
                m = spots[0, sources[j], p : p + 1, :].astype(jnp.int8)
                n = spots[1, sources[j], p : p + 1, :].astype(jnp.int8)
                values = [
                    [quant[buffer, j, t, c, p : p + 1, :].astype(float8) for c in range(COMPS)]
                    for t in range(3)
                ]
                for start in range(0, SLOTS, 256):
                    part = slice(start, start + 256)
                    hot_m = m[:, part] == io_m
                    hot_n = jnp.where(n[:, part] == io_n, one8, zero8)
                    for t in range(3):
                        weighted = jnp.concatenate(
                            [jnp.where(hot_m, values[t][c][:, part], zero8) for c in range(COMPS)],
                            axis=0,
                        )
                        term = lax.dot_general(
                            weighted,
                            hot_n,
                            (((1,), (1,)), ((), ())),
                            preferred_element_type=jnp.float32,
                        )
                        total = term if total is None else total + term
            total = total.reshape(COMPS, LANES, 256) * unit
            for c in range(COMPS):
                field[c * PLANES + p, 0:128, :] += total[c, :, 0:128]
                field[c * PLANES + p, 128:256, :] += total[c, :, 128:256]
        for row in range(ROWS // TURNS):
            index = pl.ds(row * CHUNKS + i, PLANES, stride=ROWS)
            lower = low_flat[index, :]
            upper = upp_flat[index, :]
            gain = 1.0 + lower * through
            inverse = 1.0 / (gain + upper)
            w_flat[index, :] = inverse
            lw_flat[index, :] = lower * inverse
            c_flat[index, :] = upper * inverse
            through = gain * inverse
        for step in range(5):
            r = jnp.clip(5 * (i - 1) + step, 0, STEPS - 1)
            edge = pl.ds(pl.multiple_of(r * CHUNKS, CHUNKS), CHUNKS)
            columns = [cols[side, edge, :] for side in range(2)]
            for c in range(COMPS):
                planes = [vel[c * PLANES + p, r] for p in range(PLANES)]
                for p in range(PLANES):
                    q = c * PLANES + p
                    here = planes[p]
                    above = jnp.where(
                        last,
                        pltpu.roll(columns[0], LANES - 1 - q, 1),
                        pltpu.roll(here, LANES - 1, 1),
                    )
                    below = jnp.where(
                        first, pltpu.roll(columns[1], (LANES - q) % LANES, 1), pltpu.roll(here, 1, 1)
                    )
                    stream = planes[(p + 1) % PLANES] + planes[(p + PLANES - 1) % PLANES]
                    rhs[q, r] = (
                        here
                        + diffusion_number * (stream - 2.0 * here)
                        + diffusion_number * (above + below - 2.0 * here)
                    )
        quantize(jnp.minimum(i + 1, TURNS - 1) * jnp.minimum(i, 1), 1 - buffer)
        return through

    for k in range(1, GROUP):
        block_copy(k, me).wait_recv()
    quantize(0, 0)
    lax.fori_loop(0, TURNS, deposit, jnp.ones((PLANES, LANES), jnp.float32))

    field_steps = field.reshape(COMPS * PLANES, STEPS, CHUNKS, LANES)
    outs = [pltpu.make_async_copy(field, field_hbm, out_sem.at[0])]
    outs[0].start()

    sub = lax.broadcasted_iota(jnp.int32, (CHUNKS, LANES), 0)

    def down(x, d):
        return jnp.where(sub >= d, pltpu.roll(x, d, 0), 0.0)

    def up(x, d):
        return jnp.where(sub < CHUNKS - d, pltpu.roll(x, CHUNKS - d, 0), 0.0)

    def levels(x, shift):
        out = [x]
        for d in (1, 2):
            out.append(out[-1] * shift(out[-1], d))
        return out

    def scan(x, factors, shift):
        for d, factor in zip((1, 2, 4), factors):
            x = x + factor * shift(x, d)
        return x

    def prefix(r, carry):
        out = []
        for p in range(PLANES):
            value = carry[p] * lw_ref[p, r]
            a_ref[p, r] = value
            out.append(value)
        return tuple(out)

    one = jnp.ones((CHUNKS, LANES), jnp.float32)
    alpha = lax.fori_loop(0, STEPS, prefix, (one,) * PLANES, unroll=4)
    alphas = [levels(x, down) for x in alpha]
    through_low = []
    for p in range(PLANES):
        ends = scan(jnp.where(sub == 0, alpha[p], 0.0), alphas[p], down)
        through_low.append(jnp.where(sub == 0, 1.0, pltpu.roll(ends, 1, 0)))

    def suffix(i, carry):
        r = STEPS - 1 - i
        out = []
        for p in range(PLANES):
            ratio = c_ref[p, r]
            b = carry[p] * ratio
            g = a_ref[p, r] * through_low[p] + ratio * carry[PLANES + p]
            b_ref[p, r] = b
            g_ref[p, r] = g
            out.append((b, g))
        return tuple(x[0] for x in out) + tuple(x[1] for x in out)

    zero = jnp.zeros((CHUNKS, LANES), jnp.float32)
    done = lax.fori_loop(0, STEPS, suffix, (one,) * PLANES + (zero,) * PLANES, unroll=4)
    beta, g_first = done[:PLANES], done[PLANES:]
    betas = [levels(x, up) for x in beta]
    g_carry = []
    for p in range(PLANES):
        g_all = scan(g_first[p], betas[p], up)
        g_carry.append(up(g_all, 1))
        h_all = scan(jnp.where(sub == CHUNKS - 1, beta[p], 0.0), betas[p], up)
        h_carry = jnp.where(sub == CHUNKS - 1, 1.0, pltpu.roll(h_all, CHUNKS - 1, 0))
        hc_ref[p] = h_carry
        cf[wall, 0, p : p + 1, :] = g_all[0:1]
        cf[wall, 1, p : p + 1, :] = h_all[0:1]
        last_g = g_ref[p, STEPS - 1] + b_ref[p, STEPS - 1] * g_carry[p]
        cf[wall, 2, p : p + 1, :] = last_g[CHUNKS - 1 :]
        last_h = b_ref[p, STEPS - 1] * h_carry
        cf[wall, 3, p : p + 1, :] = last_h[CHUNKS - 1 :]

    def to_walls(ref, sems):
        copies = []
        for j in range(1, WALL):
            copy = pltpu.make_async_remote_copy(
                src_ref=ref.at[wall],
                dst_ref=ref.at[wall],
                send_sem=sems[0].at[j],
                recv_sem=sems[1].at[j],
                device_id={"wall": (wall + j) % WALL},
                device_id_type=MESH,
            )
            copy.start()
            copies.append(copy)
        return copies

    def from_walls(ref, sems):
        for j in range(1, WALL):
            pltpu.make_async_remote_copy(
                src_ref=ref.at[wall],
                dst_ref=ref.at[(wall + WALL - j) % WALL],
                send_sem=sems[0].at[j],
                recv_sem=sems[1].at[j],
                device_id={"wall": (wall + j) % WALL},
                device_id_type=MESH,
            ).wait_recv()

    coefficients = to_walls(cf, (cf_send, cf_recv))

    def full_g(r, carry):
        for p in range(PLANES):
            g_ref[p, r] = g_ref[p, r] + b_ref[p, r] * g_carry[p]
        return carry

    lax.fori_loop(0, STEPS, full_g, 0, unroll=4)
    for q, (source, target) in enumerate(((b_ref, b_hbm), (g_ref, g_hbm))):
        outs.append(pltpu.make_async_copy(source, target, out_sem.at[1 + q]))
        outs[-1].start()

    def forward(r, carry):
        out = []
        for p in range(PLANES):
            inverse = w_ref[p, r]
            factor = lw_ref[p, r]
            for c in range(COMPS):
                right = rhs[c * PLANES + p, r] + field_steps[c * PLANES + p, r]
                value = right * inverse + factor * carry[p * COMPS + c]
                ybuf[c * PLANES + p, r] = value
                out.append(value)
        return tuple(out)

    ends = lax.fori_loop(0, STEPS, forward, (zero,) * (PLANES * COMPS), unroll=8)
    carries = []
    for p in range(PLANES):
        for c in range(COMPS):
            carries.append(down(scan(ends[p * COMPS + c], alphas[p], down), 1))

    def backward(i, carry):
        r = STEPS - 1 - i
        out = []
        for p in range(PLANES):
            ratio = c_ref[p, r]
            prefix_product = a_ref[p, r]
            for c in range(COMPS):
                j = p * COMPS + c
                value = ybuf[c * PLANES + p, r] + prefix_product * carries[j] + ratio * carry[j]
                ybuf[c * PLANES + p, r] = value
                out.append(value)
        return tuple(out)

    starts = lax.fori_loop(0, STEPS, backward, (zero,) * (PLANES * COMPS), unroll=8)
    tails = []
    for p in range(PLANES):
        for c in range(COMPS):
            j = p * COMPS + c
            whole = scan(starts[j], betas[p], up)
            tails.append(up(whole, 1))
            bd[wall, 0, c, p : p + 1, :] = whole[0:1]
            bd[wall, 1, c, p : p + 1, :] = ybuf[c * PLANES + p, STEPS - 1][CHUNKS - 1 :]
    boundaries = to_walls(bd, (bd_send, bd_recv))
    outs.append(pltpu.make_async_copy(ybuf, part_hbm, out_sem.at[3]))
    outs[-1].start()
    from_walls(cf, (cf_send, cf_recv))
    betas_in = [jnp.zeros((PLANES, LANES), jnp.float32)]
    divisors, slopes = [], []
    for d in range(WALL):
        g0, h0, g1, h1 = (cf[d, q] for q in range(4))
        divisor = 1.0 / (1.0 - g0 * betas_in[d])
        slope = h0 * divisor
        divisors.append(divisor)
        slopes.append(slope)
        betas_in.append(g1 * betas_in[d] * slope + h1)
    for k in range(1, SPAN):
        block_copy(k, everyone[k]).wait_send()
    from_walls(bd, (bd_send, bd_recv))
    for c in range(COMPS):
        alpha_in = [jnp.zeros((PLANES, LANES), jnp.float32)]
        heads = []
        for d in range(WALL):
            head = (bd[d, 0, c] + cf[d, 0] * alpha_in[d]) * divisors[d]
            heads.append(head)
            alpha_in.append(bd[d, 1, c] + cf[d, 2] * (alpha_in[d] + betas_in[d] * head))
        upper_value = jnp.zeros((PLANES, LANES), jnp.float32)
        x_low = upper_value
        x_high = upper_value
        for d in reversed(range(WALL)):
            x_high = jnp.where(wall == d, upper_value, x_high)
            upper_value = heads[d] + slopes[d] * upper_value
            x_low = jnp.where(wall == d, alpha_in[d] + betas_in[d] * upper_value, x_low)
        xlu[0, c] = x_low
        xlu[1, c] = x_high

    for p in range(PLANES):
        for c in range(COMPS):
            q = c * PLANES + p
            ends_ref[0, q] = tails[p * COMPS + c] + hc_ref[p] * xlu[1, c, p : p + 1, :]
            ends_ref[1, q] = jnp.broadcast_to(xlu[0, c, p : p + 1, :], (CHUNKS, LANES))
    outs.append(pltpu.make_async_copy(ends_ref, ends_hbm, out_sem.at[4]))
    outs[-1].start()
    for copy in edges + coefficients + boundaries:
        copy.wait_send()
    for copy in outs:
        copy.wait()


def finish(
    part_hbm,
    b_hbm,
    g_hbm,
    ends_hbm,
    field_hbm,
    next_hbm,
    dep_hbm,
    part,
    b_ref,
    g_ref,
    ends,
    field,
    dep,
    sems,
    part_sem,
    field_sem,
    out_sem,
    dep_sem,
):
    small = [
        pltpu.make_async_copy(source, target, sems.at[q])
        for q, (source, target) in enumerate(((b_hbm, b_ref), (g_hbm, g_ref), (ends_hbm, ends)))
    ]
    groups = [pl.ds(c * PLANES, PLANES) for c in range(COMPS)]
    parts = [
        pltpu.make_async_copy(part_hbm.at[groups[c]], part.at[groups[c]], part_sem.at[c])
        for c in range(COMPS)
    ]
    fields = []
    for j in range(CHUNKS):
        fields.append(
            pltpu.make_async_copy(
                field_hbm.at[:, :, j, :],
                field.at[:, pl.ds(j * STEPS, STEPS), :],
                field_sem.at[j],
            )
        )
    for copy in small[:2] + parts[:1] + small[2:] + parts[1:] + fields:
        copy.start()
    for copy in small:
        copy.wait()
    outs = []
    for c in range(COMPS):
        parts[c].wait()
        highs = [ends[0, c * PLANES + p] for p in range(PLANES)]
        lows = [ends[1, c * PLANES + p] for p in range(PLANES)]

        def correct(r, carry, c=c, highs=highs, lows=lows):
            for p in range(PLANES):
                q = c * PLANES + p
                part[q, r] = part[q, r] + b_ref[p, r] * highs[p] + g_ref[p, r] * lows[p]
            return carry

        lax.fori_loop(0, STEPS, correct, 0, unroll=8)
        for j in range(CHUNKS):
            copy = pltpu.make_async_copy(
                part.at[groups[c], :, j, :],
                next_hbm.at[groups[c], pl.ds(j * STEPS, STEPS), :],
                out_sem.at[c * CHUNKS + j],
            )
            copy.start()
            outs.append(copy)
    for copy in fields:
        copy.wait()
    for c in range(COMPS):

        def narrow(p, carry, c=c):
            dep[c * PLANES + p] = field[c * PLANES + p].astype(jnp.bfloat16)
            return carry

        lax.fori_loop(0, PLANES, narrow, 0)
        copy = pltpu.make_async_copy(dep.at[groups[c]], dep_hbm.at[groups[c]], dep_sem.at[c])
        copy.start()
        outs.append(copy)
    for copy in outs:
        copy.wait()


def local(velocity, lower_weight, upper_weight, forces, cells, counts):
    f32 = jnp.float32
    flat = (COMPS * PLANES, ROWS, LANES)
    steps = (PLANES, STEPS, CHUNKS, LANES)
    all_steps = (COMPS * PLANES, STEPS, CHUNKS, LANES)
    dma = pltpu.SemaphoreType.DMA
    any_space = pl.BlockSpec(memory_space=pl.ANY)
    ends = (2, COMPS * PLANES, CHUNKS, LANES)
    solved = pl.pallas_call(
        kernel,
        name="substep",
        out_shape=(
            jax.ShapeDtypeStruct(all_steps, f32),
            jax.ShapeDtypeStruct(steps, f32),
            jax.ShapeDtypeStruct(steps, f32),
            jax.ShapeDtypeStruct(ends, f32),
            jax.ShapeDtypeStruct(flat, f32),
        ),
        in_specs=[any_space] * 6,
        out_specs=(any_space,) * 5,
        scratch_shapes=[
            pltpu.VMEM((COMPS, SPAN, PLANES, SLOTS), f32),
            pltpu.VMEM((SPAN, PLANES, SLOTS), jnp.int32),
            pltpu.SMEM((PLANES, SPAN), jnp.int32),
            pltpu.VMEM(all_steps, f32),
            pltpu.VMEM(steps, f32),
            pltpu.VMEM(steps, f32),
            pltpu.VMEM(all_steps, f32),
            pltpu.VMEM(flat, f32),
            pltpu.VMEM(all_steps, f32),
            pltpu.VMEM(steps, f32),
            pltpu.VMEM(steps, f32),
            pltpu.VMEM(steps, f32),
            pltpu.VMEM(steps, f32),
            pltpu.VMEM(steps, f32),
            pltpu.VMEM(steps, f32),
            pltpu.VMEM((PLANES, CHUNKS, LANES), f32),
            pltpu.VMEM(ends, f32),
            pltpu.VMEM((2, SPAN, PLANES, SLOTS), jnp.int32),
            pltpu.VMEM((2, GROUP, 3, COMPS, PLANES, SLOTS), f32),
            pltpu.VMEM((2, 8, LANES), f32),
            pltpu.VMEM((LANES, ROWS), f32),
            pltpu.VMEM((2, ROWS, LANES), f32),
            pltpu.VMEM((2, 16, ROWS), f32),
            pltpu.VMEM((2, 16, ROWS), f32),
            pltpu.VMEM((WALL, 4, PLANES, LANES), f32),
            pltpu.VMEM((WALL, 2, COMPS, PLANES, LANES), f32),
            pltpu.VMEM((2, COMPS, PLANES, LANES), f32),
            dma((SPAN,)),
            dma((SPAN,)),
            dma((2,)),
            dma((2,)),
            dma((WALL,)),
            dma((WALL,)),
            dma((WALL,)),
            dma((WALL,)),
            dma((32,)),
            dma((5,)),
        ],
        compiler_params=pltpu.CompilerParams(
            collective_id=0,
            has_side_effects=True,
        ),
    )(
        velocity.reshape(flat),
        lower_weight,
        upper_weight,
        forces,
        cells,
        jnp.swapaxes(counts, 2, 3),
    )
    velocity_next, deposit = pl.pallas_call(
        finish,
        name="finish",
        out_shape=(jax.ShapeDtypeStruct(flat, f32), jax.ShapeDtypeStruct(flat, jnp.bfloat16)),
        in_specs=[any_space] * 5,
        out_specs=(any_space,) * 2,
        scratch_shapes=[
            pltpu.VMEM(all_steps, f32),
            pltpu.VMEM(steps, f32),
            pltpu.VMEM(steps, f32),
            pltpu.VMEM(ends, f32),
            pltpu.VMEM(flat, f32),
            pltpu.VMEM(flat, jnp.bfloat16),
            dma((3,)),
            dma((COMPS,)),
            dma((CHUNKS,)),
            dma((COMPS * CHUNKS,)),
            dma((COMPS,)),
        ],
    )(*solved[:4], solved[4].reshape(all_steps))
    return velocity_next.reshape(velocity.shape), deposit.reshape(velocity.shape)


def solution(mesh):
    placed = (
        P(None, None, "wall", "span"),
        P(None, "wall", "span"),
        P(None, "wall", "span"),
        P(None, "wall", "span", None, None, None),
        P("wall", "span", None, None, None),
        P("wall", "span", None, None),
    )
    return jax.shard_map(
        local,
        mesh=mesh,
        in_specs=placed,
        out_specs=(P(None, None, "wall", "span"), P(None, None, "wall", "span")),
        check_vma=False,
    )
```
